32 devices in a mesh: head: 4 (over y, x), seq: 4 (over z), dp: 2 (over core).
Axes of the slice: x: 2, y: 2, z: 4, core: 2. Of those that a mesh axis runs over, the one named last changes fastest.
Arguments:
- inputs: bfloat16 [2, 2048, 1536], P('dp', 'seq', 'head'), may hold values from -24 to 24
- w_query: bfloat16 [1536, 1536], P(('seq', 'dp'), 'head'), may hold values from -0.15625 to 0.15625
- w_key: bfloat16 [1536, 1536], P(('seq', 'dp'), 'head'), may hold values from -0.15625 to 0.15625
- w_value: bfloat16 [1536, 1536], P(('seq', 'dp'), 'head'), may hold values from -0.15625 to 0.15625
- w_output: bfloat16 [1536, 1536], P(('seq', 'dp'), 'head'), may hold values from -0.21875 to 0.21875
- w_gate: bfloat16 [1536, 4096], P(('seq', 'dp'), 'head'), may hold values from -0.15625 to 0.15625
- w_up: bfloat16 [1536, 4096], P(('seq', 'dp'), 'head'), may hold values from -0.15625 to 0.15625
- w_down: bfloat16 [1536, 4096], P(('seq', 'dp'), 'head'), may hold values from -0.09375 to 0.09375
- gain_attn: float32 [1536], replicated, may hold values from 0.5 to 1.5
- gain_ffn: float32 [1536], replicated, may hold values from 0.5 to 1.5
- group_gain: float32 [128], replicated, may hold values from 0.5 to 1.5
- lambda_q1: float32 [64], replicated, may hold values from -1 to 1
- lambda_k1: float32 [64], replicated, may hold values from -1 to 1
- lambda_q2: float32 [64], replicated, may hold values from -1 to 1
- lambda_k2: float32 [64], replicated, may hold values from -1 to 1
- doc_ids: int32 [2, 2048], P('dp', 'seq'), may hold values from 0 to 3, never falling along the last dimension, each value on 1 to 1024 neighbouring positions
- needles: int32 [2, 2048], P('dp', 'seq'), may hold values 0 or 1
- out_grad: bfloat16 [2, 2048, 1536], P('dp', 'seq', 'head'), may hold values from -6 to 6
Outputs:
- output: bfloat16 [2, 2048, 1536], P('dp', 'seq', 'head')
- input_grad: bfloat16 [2, 2048, 1536], P('dp', 'seq', 'head')
- gain_attn_grad: float32 [1536], P(('head', 'seq', 'dp'))
- gain_ffn_grad: float32 [1536], P(('head', 'seq', 'dp'))
- group_gain_grad: float32 [128], replicated
- lambda_grad: float32 [1], replicated
- w_query_grad: float32 [1536, 1536], P(('seq', 'dp'), 'head')
- w_key_grad: float32 [1536, 1536], P(('seq', 'dp'), 'head')
- w_value_grad: float32 [1536, 1536], P(('seq', 'dp'), 'head')
- w_output_grad: float32 [1536, 1536], P(('seq', 'dp'), 'head')
- w_gate_grad: float32 [1536, 4096], P(('seq', 'dp'), 'head')
- w_up_grad: float32 [1536, 4096], P(('seq', 'dp'), 'head')
- w_down_grad: float32 [1536, 4096], P(('seq', 'dp'), 'head')
The draws below stay inside these ranges and needn't reach their ends.
Inputs may be any that keep to these rules, and one draw needn't show every extreme that they name: `doc_ids`: within each context the document numbers never fall; each of the 4 documents holds 1 to 1024 tokens, and one holds exactly 1024.
All inputs are finite; a program needn't handle non-finite values. No bound on the sum of `needles` on one device may be relied on, other than what follows from the above.
Results may differ from the reference program's by a relative error of at most 0.035.
Values may be sent and summed in bfloat16 or wider, within the bound.
A program may use at most 448 MiB of HBM per device.

```python
import math
import jax
import jax.numpy as jnp
import numpy as np
from jax import lax

D = 1536
HEADS = 12
HALF = 64
VDIM = 128
FF = 4096
DOCS = 4
LENGTH = 2048
CONTEXTS = 2
N_DP = 2


def draw_inputs(key, part):
    key_vals = jax.random.fold_in(key, 11)
    key_cols = jax.random.fold_in(key, 12)
    place = jnp.arange(D, dtype=jnp.float32) / float(max(D - 1, 1))
    rough = jnp.exp(jax.random.uniform(key_cols, (D,), jnp.float32) * jnp.log(1.6))
    entries = jnp.clip(jax.random.normal(key_vals, (CONTEXTS, LENGTH, D), jnp.float32), -5.0, 5.0)
    rise = jnp.exp(place * jnp.log(4.0))
    values = jnp.clip(entries * (rise * rough)[None, None, :], -24.0, 24.0)
    return values.astype(jnp.bfloat16)


def set_ends(values, stream_key, smallest, largest):
    dims = values.shape
    spot = [jax.random.randint(jax.random.fold_in(stream_key, axis), (), 0, dims[axis]) for axis in range(len(dims))]
    values = values.at[tuple(spot)].set(smallest)
    longest = dims.index(max(dims))
    spot[longest] = (spot[longest] + 1) % dims[longest]
    return values.at[tuple(spot)].set(largest)


def levels(rng, shape, cuts, low, high):
    factor_of, own = 1.0, jax.random.fold_in(rng, 6)
    for position, blocks in cuts:
        heights = jnp.exp(jax.random.uniform(jax.random.fold_in(own, position), (blocks,), jnp.float32, low / len(cuts), high / len(cuts)))
        factor_of = factor_of * jnp.repeat(heights, shape[position] // blocks).reshape([-1 if axis == position else 1 for axis in range(len(shape))])
    return factor_of


def profile(amount, total, most, skew):
    weights = [(1 << 20) // math.isqrt(rank ** skew) + 1 for rank in range(2, amount + 1)]
    surplus, holding = total - most - (amount - 1), [1] * (amount - 1)
    while surplus > 0:
        free = [i for i in range(amount - 1) if holding[i] < most]
        pool, budget = sum([weights[i] for i in free]), surplus
        for i in free:
            more = min(most - holding[i], max(1, budget * weights[i] // pool), surplus)
            holding[i] = holding[i] + more
            surplus = surplus - more
    return np.array([most] + holding)


def uneven(own_key, number_of, total, bound, slope):
    if number_of == 2:
        one = jax.random.randint(own_key, (), max(1, total - bound), min(bound, total - 1) + 1)
        return jnp.stack([one, total - one])
    lengths = jnp.asarray(profile(number_of, total, bound, slope), jnp.int32)
    twos = (number_of - 1) // 2
    donor, sink = lengths[1:1 + 2 * twos:2], lengths[2:2 + 2 * twos:2]
    slack = jnp.minimum(donor - 1, bound - sink)
    passed = jax.random.randint(jax.random.fold_in(own_key, 1), (twos,), 0, 1 << 20) % (slack + 1)
    lengths = lengths.at[1:1 + 2 * twos:2].set(donor - passed).at[2:2 + 2 * twos:2].set(sink + passed)
    return lengths[jax.random.permutation(jax.random.fold_in(own_key, 2), number_of)]


def bell_draw(rng, extent, scale, reach, split=(), held_as=jnp.bfloat16):
    level = levels(rng, extent, split, -0.22, 0.18) if split else 1.0
    array = jax.random.normal(rng, extent, jnp.float32) * scale * level
    return jnp.minimum(jnp.maximum(array, -reach), reach).astype(held_as)


def setup_inputs(seed: int = 0) -> dict:
    streams_of = jax.random.split(jax.random.key(seed), 19)
    return {
        "inputs": draw_inputs(jax.random.fold_in(streams_of[18], 71), 0),
        "w_query": bell_draw(streams_of[1], (D, 2 * HEADS * HALF), D ** -0.5, 0.15625, ((0, 8), (1, 4))),
        "w_key": bell_draw(streams_of[2], (D, 2 * HEADS * HALF), D ** -0.5, 0.15625, ((0, 8), (1, 4))),
        "w_value": bell_draw(streams_of[3], (D, HEADS * VDIM), D ** -0.5, 0.15625, ((0, 8), (1, 4))),
        "w_output": bell_draw(streams_of[4], (D, HEADS * VDIM), (D // 2) ** -0.5, 0.21875, ((0, 8), (1, 4))),
        "w_gate": bell_draw(streams_of[5], (D, FF), D ** -0.5, 0.15625, ((0, 8), (1, 4))),
        "w_up": bell_draw(streams_of[6], (D, FF), D ** -0.5, 0.15625, ((0, 8), (1, 4))),
        "w_down": bell_draw(streams_of[7], (D, FF), FF ** -0.5, 0.09375, ((0, 8), (1, 4))),
        "gain_attn": jnp.clip(1.0 + 0.1 * jax.random.normal(streams_of[8], (D,), jnp.float32), 0.5, 1.5),
        "gain_ffn": jnp.clip(1.0 + 0.1 * jax.random.normal(streams_of[9], (D,), jnp.float32), 0.5, 1.5),
        "group_gain": jnp.clip(1.0 + 0.1 * jax.random.normal(streams_of[10], (VDIM,), jnp.float32), 0.5, 1.5),
        "lambda_q1": bell_draw(streams_of[11], (HALF,), 0.2, 1.0, (), jnp.float32),
        "lambda_k1": bell_draw(streams_of[12], (HALF,), 0.2, 1.0, (), jnp.float32),
        "lambda_q2": bell_draw(streams_of[13], (HALF,), 0.2, 1.0, (), jnp.float32),
        "lambda_k2": bell_draw(streams_of[14], (HALF,), 0.2, 1.0, (), jnp.float32),
        "doc_ids": jax.vmap(lambda own: jnp.searchsorted(jnp.cumsum(uneven(own, DOCS, LENGTH, LENGTH // 2, 2)), jnp.arange(LENGTH), side="right"))(jax.random.split(streams_of[15], CONTEXTS)).reshape((CONTEXTS, LENGTH)).astype(jnp.int32),
        "needles": set_ends((jax.random.randint(streams_of[16], (CONTEXTS, LENGTH), 0, 8) < 1).astype(jnp.int32), jax.random.fold_in(streams_of[16], 1), 0, 1),
        "out_grad": bell_draw(streams_of[17], (CONTEXTS, LENGTH, D), 1.0, 6.0, ((0, 2), (1, 4), (2, 4))),
    }


EPS = 1e-05
LAMBDA_INIT = 0.8 - 0.6 * math.exp(-0.3)
NEG_BIG = -1e+30

@jax.custom_vjp
def low(v):
    return lax.optimization_barrier(v.astype(jnp.bfloat16)).astype(jnp.float32)

@jax.custom_vjp
def low_back(v):
    return v

def low_keep(v):
    return (low(v), None)

def low_pass(kept, grad):
    return (grad,)

def back_keep(v):
    return (v, None)

def back_low(kept, grad):
    return (low(grad),)
low.defvjp(low_keep, low_pass)
low_back.defvjp(back_keep, back_low)

def matmul_hi(left, right):
    return jnp.dot(left, right, precision=lax.Precision.HIGHEST, preferred_element_type=jnp.float32)

def normed(rows, gain):
    return rows * lax.rsqrt(lax.optimization_barrier(jnp.mean(rows * rows, axis=-1, keepdims=True)) + EPS) * gain

def attend_context(queries, keys, values, docs):
    block_rows = min(512, LENGTH)
    count = LENGTH // block_rows
    places = jnp.arange(LENGTH, dtype=jnp.int32)
    query_blocks = queries.reshape(count, block_rows, HEADS, 2, HALF)
    place_blocks = places.reshape(count, block_rows)
    doc_blocks = docs.reshape(count, block_rows)

    def one_block(items):
        query_rows, query_places, query_docs = items
        allowed = (query_places[:, None] >= places[None, :]) & (query_docs[:, None] == docs[None, :])
        result = []
        for which in range(2):
            scores = jnp.einsum('qhd,khd->hqk', query_rows[:, :, which], keys[:, :, which], precision=lax.Precision.HIGHEST) * 0.125
            scores = low_back(scores)
            scores = jnp.where(allowed[None], scores, NEG_BIG)
            peak = lax.optimization_barrier(jnp.max(scores, axis=-1, keepdims=True))
            expo = jnp.exp(scores - peak)
            probs = expo / lax.optimization_barrier(jnp.sum(expo, axis=-1, keepdims=True))
            mixed = jnp.einsum('hqk,khd->qhd', low(probs), values, precision=lax.Precision.HIGHEST)
            result.append(low_back(mixed))
        return jnp.stack(result)
    outs = lax.map(jax.checkpoint(one_block), (query_blocks, place_blocks, doc_blocks))
    return jnp.transpose(outs, (1, 0, 2, 3, 4)).reshape(2, LENGTH, HEADS, VDIM)

def forward(inputs, w_query, w_key, w_value, w_output, w_gate, w_up, w_down, gain_attn, gain_ffn, group_gain, lam_array, doc_ids):
    rows = inputs.reshape(-1, D)
    first = low(normed(rows, gain_attn))
    queries = low(low_back(matmul_hi(first, w_query)))
    keys = low(low_back(matmul_hi(first, w_key)))
    values = low(low_back(matmul_hi(first, w_value)))
    lam_value = lam_array[0]
    parts = []
    for context in range(N_DP):
        lo_row = context * LENGTH
        parts.append(attend_context(queries[lo_row:lo_row + LENGTH].reshape(LENGTH, HEADS, 2, HALF), keys[lo_row:lo_row + LENGTH].reshape(LENGTH, HEADS, 2, HALF), values[lo_row:lo_row + LENGTH].reshape(LENGTH, HEADS, VDIM), doc_ids[context]))
    maps = jnp.concatenate(parts, axis=1)
    diff = maps[0] - lam_value * maps[1]
    unit = diff * lax.rsqrt(lax.optimization_barrier(jnp.mean(diff * diff, axis=-1, keepdims=True)) + EPS)
    grouped = low((unit * group_gain * (1.0 - LAMBDA_INIT)).reshape(-1, HEADS * VDIM))
    attn = low_back(matmul_hi(grouped, w_output.T))
    hidden_one = rows + attn
    second = low(normed(low(hidden_one), gain_ffn))
    gate = low_back(matmul_hi(second, w_gate))
    upper = low_back(matmul_hi(second, w_up))
    inner = low(gate * jax.nn.sigmoid(gate) * upper)
    ffn = low_back(matmul_hi(inner, w_down.T))
    return (hidden_one + ffn).reshape(N_DP, LENGTH, D)

def reference(inputs, w_query, w_key, w_value, w_output, w_gate, w_up, w_down, gain_attn, gain_ffn, group_gain, lambda_q1, lambda_k1, lambda_q2, lambda_k2, doc_ids, needles, out_grad):
    lam_value = jnp.exp(jnp.sum(lambda_q1.astype(jnp.float32) * lambda_k1.astype(jnp.float32))) - jnp.exp(jnp.sum(lambda_q2.astype(jnp.float32) * lambda_k2.astype(jnp.float32))) + LAMBDA_INIT
    lam_array = jnp.reshape(lam_value, (1,)).astype(jnp.float32)
    primals = (inputs.astype(jnp.float32), w_query.astype(jnp.float32), w_key.astype(jnp.float32), w_value.astype(jnp.float32), w_output.astype(jnp.float32), w_gate.astype(jnp.float32), w_up.astype(jnp.float32), w_down.astype(jnp.float32), gain_attn.astype(jnp.float32), gain_ffn.astype(jnp.float32), group_gain.astype(jnp.float32), lam_array)

    def run(*params):
        return forward(*params, doc_ids)
    result, pullback = jax.vjp(run, *primals)
    weight = jnp.where(needles == 1, 1.0, 0.1).astype(jnp.float32)
    grads = pullback(out_grad.astype(jnp.float32) * weight[..., None])
    return (result.astype(jnp.bfloat16), grads[0].astype(jnp.bfloat16), grads[8], grads[9], grads[10], grads[11], grads[1], grads[2], grads[3], grads[4], grads[5], grads[6], grads[7])
```

```python
import functools
import math

import jax
import jax.numpy as jnp
from jax import lax
from jax.experimental import pallas as pl
from jax.experimental.pallas import tpu as pltpu
from jax.sharding import PartitionSpec as P

HALF = 64
VDIM = 128
EPS = 1e-05
LAMBDA_INIT = 0.8 - 0.6 * math.exp(-0.3)
KEEP = 1.0 - LAMBDA_INIT
NEG_BIG = -1e30
MESH = pl.DeviceIdType.MESH
VMEM = pltpu.VMEM
F32 = jnp.float32
BF16 = jnp.bfloat16
NN = (((1,), (0,)), ((), ()))
NT = (((1,), (1,)), ((), ()))
TN = (((0,), (0,)), ((), ()))


def mm(a, b, dims):
    return lax.dot_general(a, b, dims, preferred_element_type=F32)


def whole():
    return pl.BlockSpec(memory_space=VMEM)


def peer_of(me, k, n):
    return lax.rem(me + k, n)


def greet(n):
    me = lax.axis_index("head")
    barrier = pltpu.get_barrier_semaphore()
    for k in range(1, n):
        pl.semaphore_signal(
            barrier, 1, device_id={"head": peer_of(me, k, n)}, device_id_type=MESH
        )
    pl.semaphore_wait(barrier, n - 1)
    return me


def push(src, dst, send, recv, peer):
    return pltpu.make_async_remote_copy(
        src_ref=src,
        dst_ref=dst,
        send_sem=send,
        recv_sem=recv,
        device_id={"head": peer},
        device_id_type=MESH,
    )


def rows_of(c, size):
    return pl.ds(pl.multiple_of(c * size, size), size)


class Reduce:
    def __init__(self, n, nc, me, a_ref, w_ref, own_ref, sbuf, rbuf, ssem, rsem):
        self.n, self.nc, self.me = n, nc, me
        self.a_ref, self.w_ref, self.own_ref = a_ref, w_ref, own_ref
        self.sbuf, self.rbuf, self.ssem, self.rsem = sbuf, rbuf, ssem, rsem
        self.size = a_ref.shape[0] // nc
        self.cols = w_ref.shape[0] // n

    def copy(self, k, c):
        rows = rows_of(c, self.size)
        return push(
            self.sbuf.at[k - 1, rows],
            self.rbuf.at[k - 1, rows],
            self.ssem.at[k - 1, c],
            self.rsem.at[k - 1, c],
            peer_of(self.me, k, self.n),
        )

    def send(self):
        n = self.n

        def step(t, _):
            c = t // n
            k = t - c * n + 1
            rows = rows_of(c, self.size)
            peer = peer_of(self.me, k, n)
            part = mm(
                self.a_ref[rows, :],
                self.w_ref[rows_of(peer, self.cols), :],
                NT,
            )

            @pl.when(k < n)
            def _():
                self.sbuf[k - 1, rows] = part.astype(BF16)
                self.copy(k, c).start()

            @pl.when(k == n)
            def _():
                self.own_ref[rows, :] = part

            return 0

        lax.fori_loop(0, self.nc * n, step, 0)

    def take(self, c):
        rows = rows_of(c, self.size)
        total = self.own_ref[rows, :]
        for k in range(1, self.n):
            self.copy(k, c).wait_recv()
        for k in range(1, self.n):
            total = total + self.rbuf[k - 1, rows].astype(F32)
        return total

    def finish(self):
        for c in range(self.nc):
            for k in range(1, self.n):
                self.copy(k, c).wait_send()


class Gather:
    def __init__(self, n, nc, me, buf, ssem, rsem):
        self.n, self.nc, self.me = n, nc, me
        self.buf, self.ssem, self.rsem = buf, ssem, rsem
        self.size = buf.shape[1] // nc

    def copy(self, k, c, source):
        rows = rows_of(c, self.size)
        return push(
            self.buf.at[source, rows],
            self.buf.at[source, rows],
            self.ssem.at[k - 1, c],
            self.rsem.at[k - 1, c],
            peer_of(self.me, k, self.n),
        )

    def send(self, c, value):
        self.buf[self.me, rows_of(c, self.size)] = value
        for k in range(1, self.n):
            self.copy(k, c, self.me).start()

    def take(self, c):
        for k in range(1, self.n):
            self.copy(k, c, peer_of(self.me, self.n - k, self.n)).wait_recv()

    def finish(self):
        for c in range(self.nc):
            for k in range(1, self.n):
                self.copy(k, c, self.me).wait_send()


def norm_rows(n, buf, rows, gain_ref, out_ref, scale_ref):
    cols = buf.shape[2]
    total = None
    for s in range(n):
        piece = buf[s, rows].astype(F32)
        part = jnp.sum(piece * piece, axis=1, keepdims=True)
        total = part if total is None else total + part
    scale = lax.rsqrt(total / (n * cols) + EPS)
    scale_ref[rows, :] = scale
    for s in range(n):
        span = slice(s * cols, (s + 1) * cols)
        piece = buf[s, rows].astype(F32)
        out_ref[rows, span] = (piece * scale * gain_ref[:, span]).astype(BF16)


def spread_rows(n, buf, rows, out_ref):
    cols = buf.shape[2]
    for s in range(n):
        out_ref[rows, s * cols : (s + 1) * cols] = buf[s, rows]


def enter_kernel(n, x_ref, dy_ref, gain_ref, n1_ref, scale_ref, dyr_ref, xall, dall, xs, xr, ds, dr):
    me = greet(n)
    xg = Gather(n, 1, me, xall, xs, xr)
    dg = Gather(n, 1, me, dall, ds, dr)
    xg.send(0, x_ref[...])
    dg.send(0, dy_ref[...])
    tok = x_ref.shape[0]
    size = min(64, tok)
    xg.take(0)

    @pl.loop(0, tok // size)
    def _(i):
        norm_rows(n, xall, rows_of(i, size), gain_ref, n1_ref, scale_ref)

    dg.take(0)

    @pl.loop(0, tok // size)
    def _(i):
        spread_rows(n, dall, rows_of(i, size), dyr_ref)

    xg.finish()
    dg.finish()


def middle_kernel(n, nc, g_ref, w_ref, x_ref, gain_ref, h1_ref, n2_ref, scale_ref, own, sbuf, rbuf, hall, s1, r1, s2, r2):
    me = greet(n)
    red = Reduce(n, nc, me, g_ref, w_ref, own, sbuf, rbuf, s1, r1)
    gat = Gather(n, nc, me, hall, s2, r2)
    red.send()
    for c in range(nc):
        rows = rows_of(c, red.size)
        h1 = red.take(c) + x_ref[rows, :].astype(F32)
        h1_ref[rows, :] = h1
        gat.send(c, h1.astype(BF16))
    size = min(64, red.size)
    for c in range(nc):
        gat.take(c)

        @pl.loop(0, red.size // size)
        def _(i):
            norm_rows(n, hall, pl.ds(pl.multiple_of(c * red.size + i * size, size), size), gain_ref, n2_ref, scale_ref)

    red.finish()
    gat.finish()


class Stats:
    def __init__(self, n, nc, me, buf, ssem, rsem):
        self.n, self.nc, self.me = n, nc, me
        self.buf, self.ssem, self.rsem = buf, ssem, rsem

    def copy(self, k, c, source):
        return push(
            self.buf.at[source, c],
            self.buf.at[source, c],
            self.ssem.at[k - 1, c],
            self.rsem.at[k - 1, c],
            peer_of(self.me, k, self.n),
        )

    def send(self, c, value):
        size, cols = value.shape
        part = value[:, :128]
        for j in range(1, cols // 128):
            part = part + value[:, j * 128 : (j + 1) * 128]
        line = jnp.sum(part.T, axis=0, keepdims=True)
        self.buf[self.me, c] = jnp.broadcast_to(line, (8, size))
        for k in range(1, self.n):
            self.copy(k, c, self.me).start()

    def take(self, c):
        for k in range(1, self.n):
            self.copy(k, c, peer_of(self.me, self.n - k, self.n)).wait_recv()
        total = self.buf[0, c]
        for s in range(1, self.n):
            total = total + self.buf[s, c]
        size = total.shape[1]
        tall = jnp.broadcast_to(total[:1, :], (128, size))
        return tall.T[:, :1]

    def finish(self):
        for c in range(self.nc):
            for k in range(1, self.n):
                self.copy(k, c, self.me).wait_send()


def norm_back(n, nc, me, red, sta, unit_of, gain_ref, base_of, gain_grad_ref, done):
    width = n * red.cols
    for c in range(nc):
        rows = rows_of(c, red.size)
        grad = red.take(c)
        red.own_ref[rows, :] = grad
        unit = unit_of(rows)
        part = jnp.sum(grad * unit, axis=0, keepdims=True)
        if c == 0:
            gain_grad_ref[...] = part
        else:
            gain_grad_ref[...] += part
        sta.send(c, grad * gain_ref[...] * unit)
    for c in range(nc):
        rows = rows_of(c, red.size)
        dots = sta.take(c) / width
        scaled = red.own_ref[rows, :] * gain_ref[...]
        done(c, rows, base_of(rows, scaled - unit_of(rows) * dots))


def back_kernel(n, nc, d_ref, w_ref, h1_ref, scale_ref, gain_ref, dy_ref, dh1_ref, dh1r_ref, gain_grad_ref, own, sbuf, rbuf, stat, dall, s1, r1, s2, r2, s3, r3):
    me = greet(n)
    red = Reduce(n, nc, me, d_ref, w_ref, own, sbuf, rbuf, s1, r1)
    sta = Stats(n, nc, me, stat, s2, r2)
    gat = Gather(n, nc, me, dall, s3, r3)
    red.send()

    def unit_of(rows):
        return h1_ref[rows, :].astype(BF16).astype(F32) * scale_ref[rows, :]

    def base_of(rows, back):
        return dy_ref[rows, :] + scale_ref[rows, :] * back

    def done(c, rows, value):
        dh1_ref[rows, :] = value
        gat.send(c, value.astype(BF16))

    norm_back(n, nc, me, red, sta, unit_of, gain_ref, base_of, gain_grad_ref, done)
    for c in range(nc):
        gat.take(c)
        spread_rows(n, dall, rows_of(c, red.size), dh1r_ref)
    red.finish()
    sta.finish()
    gat.finish()


def leave_kernel(n, nc, d_ref, w_ref, x_ref, scale_ref, gain_ref, dh1_ref, out_ref, gain_grad_ref, own, sbuf, rbuf, stat, s1, r1, s2, r2):
    me = greet(n)
    red = Reduce(n, nc, me, d_ref, w_ref, own, sbuf, rbuf, s1, r1)
    sta = Stats(n, nc, me, stat, s2, r2)
    red.send()

    def unit_of(rows):
        return x_ref[rows, :].astype(F32) * scale_ref[rows, :]

    def base_of(rows, back):
        return dh1_ref[rows, :] + scale_ref[rows, :] * back

    def done(c, rows, value):
        out_ref[rows, :] = value.astype(BF16)

    norm_back(n, nc, me, red, sta, unit_of, gain_ref, base_of, gain_grad_ref, done)
    red.finish()
    sta.finish()


def output_kernel(n, nc, a_ref, w_ref, h1_ref, out_ref, own, sbuf, rbuf, s1, r1):
    me = greet(n)
    red = Reduce(n, nc, me, a_ref, w_ref, own, sbuf, rbuf, s1, r1)
    red.send()
    for c in range(nc):
        rows = rows_of(c, red.size)
        out_ref[rows, :] = (red.take(c) + h1_ref[rows, :]).astype(BF16)
    red.finish()


def dma(*dims):
    return pltpu.SemaphoreType.DMA(dims)


def talk(kernel, ident, outs, scratch, flops, moved, args):
    return pl.pallas_call(
        kernel,
        out_shape=[jax.ShapeDtypeStruct(s, d) for s, d in outs],
        in_specs=[whole()] * len(args),
        out_specs=[whole()] * len(outs),
        scratch_shapes=scratch,
        cost_estimate=pl.CostEstimate(flops=flops, bytes_accessed=moved, transcendentals=0),
        compiler_params=pltpu.CompilerParams(
            collective_id=ident, has_side_effects=True, vmem_limit_bytes=40 * 2**20
        ),
    )(*args)


def forward_kernel(base, nb_ref, lam_ref, q_ref, k_ref, v_ref, start_ref, gain_ref, o1_ref, o2_ref, lse_ref, g_ref, m_s, l_s, acc):
    size = q_ref.shape[0]
    qt = pl.program_id(1)
    q = q_ref[...] * 0.125
    lane = lax.broadcasted_iota(jnp.int32, q.shape, 1)
    zero = jnp.zeros_like(q)
    parts = (jnp.where(lane < HALF, q, zero), jnp.where(lane >= HALF, q, zero))
    key = lax.broadcasted_iota(jnp.int32, (size, size), 0)
    query = lax.broadcasted_iota(jnp.int32, (size, size), 1)
    start = start_ref[...]

    def block(where, first):
        rows = rows_of(where, size)
        k, v = k_ref[rows, :], v_ref[rows, :]
        allowed = key >= start - where * size
        if first:
            allowed = allowed & (key <= query)
        for m in range(2):
            s = jnp.where(allowed, mm(k, parts[m], NT), NEG_BIG)
            top = jnp.max(s, axis=0, keepdims=True)
            if first:
                e = jnp.exp(s - top)
                m_s[m] = top
                l_s[m] = jnp.sum(e, axis=0, keepdims=True)
                acc[m] = mm(v, e.astype(BF16), TN)
            else:
                new = jnp.maximum(m_s[m], top)
                e = jnp.exp(s - new)
                fade = jnp.exp(m_s[m] - new)
                m_s[m] = new
                l_s[m] = l_s[m] * fade + jnp.sum(e, axis=0, keepdims=True)
                acc[m] = acc[m] * fade + mm(v, e.astype(BF16), TN)

    block(base + qt, True)

    def earlier(d, _):
        block(base + qt - d, False)
        return 0

    lax.fori_loop(1, nb_ref[qt], earlier, 0)
    o1 = acc[0] / l_s[0]
    o2 = acc[1] / l_s[1]
    o1_ref[...] = o1
    o2_ref[...] = o2
    lse_ref[0, 0:1, :] = m_s[0] + jnp.log(l_s[0])
    lse_ref[0, 1:2, :] = m_s[1] + jnp.log(l_s[1])
    diff = o1 - lam_ref[0] * o2
    scale = lax.rsqrt(jnp.mean(diff * diff, axis=0, keepdims=True) + EPS)
    g = diff * scale * gain_ref[...] * KEEP
    g_ref[...] = g.T.astype(BF16)


def backward_kernel(base, nb_ref, lam_ref, q_ref, k_ref, v_ref, start_ref, gain_ref, o1_ref, o2_ref, lse_ref, dg_ref, dq_ref, dk_ref, dv_ref, gain_grad_ref, lam_grad_ref, dq_s, dk_s, dv_s):
    size = q_ref.shape[0]
    h, qt = pl.program_id(0), pl.program_id(1)
    lam = lam_ref[0]

    @pl.when((h == 0) & (qt == 0))
    def _():
        gain_grad_ref[...] = jnp.zeros_like(gain_grad_ref)
        lam_grad_ref[...] = jnp.zeros_like(lam_grad_ref)

    @pl.when(qt == 0)
    def _():
        dk_s[...] = jnp.zeros_like(dk_s)
        dv_s[...] = jnp.zeros_like(dv_s)

    o1, o2 = o1_ref[...], o2_ref[...]
    diff = o1 - lam * o2
    scale = lax.rsqrt(jnp.mean(diff * diff, axis=0, keepdims=True) + EPS)
    unit = diff * scale
    dg = dg_ref[...].T
    gain_grad_ref[...] += jnp.sum(dg * unit, axis=1, keepdims=True) * KEEP
    du = dg * gain_ref[...] * KEEP
    do = scale * (du - unit * jnp.mean(du * unit, axis=0, keepdims=True))
    lam_grad_ref[...] -= jnp.sum(do * o2, axis=1, keepdims=True)
    grads = (do.astype(BF16), (-lam * do).astype(BF16))
    deltas = tuple(
        jnp.sum(g.astype(F32) * o, axis=0, keepdims=True) for g, o in zip(grads, (o1, o2))
    )
    q = q_ref[...] * 0.125
    lane = lax.broadcasted_iota(jnp.int32, q.shape, 1)
    zero = jnp.zeros_like(q)
    parts = (jnp.where(lane < HALF, q, zero), jnp.where(lane >= HALF, q, zero))
    key = lax.broadcasted_iota(jnp.int32, (size, size), 0)
    query = lax.broadcasted_iota(jnp.int32, (size, size), 1)
    start = start_ref[...]
    dq_s[...] = jnp.zeros_like(dq_s)

    def block(where, first):
        rows = rows_of(where, size)
        k, v = k_ref[rows, :], v_ref[rows, :]
        halves = (jnp.where(lane < HALF, k, zero), jnp.where(lane >= HALF, k, zero))
        allowed = key >= start - where * size
        if first:
            allowed = allowed & (key <= query)
        dq = dq_s[...]
        dk = dk_s[rows, :]
        dv = dv_s[rows, :]
        for m in range(2):
            s = mm(k, parts[m], NT)
            p = jnp.where(allowed, jnp.exp(s - lse_ref[0, m : m + 1, :]), 0.0)
            dp = mm(v, grads[m], NN)
            ds = (p * (dp - deltas[m])).astype(BF16)
            dq = dq + mm(halves[m], ds, TN)
            dk = dk + mm(ds, parts[m], NN)
            dv = dv + mm(p.astype(BF16), grads[m], NT)
        dq_s[...] = dq
        dk_s[rows, :] = dk
        dv_s[rows, :] = dv

    block(base + qt, True)

    def earlier(d, _):
        block(base + qt - d, False)
        return 0

    lax.fori_loop(1, nb_ref[qt], earlier, 0)
    dq_ref[...] = (dq_s[...] * 0.125).T.astype(BF16)

    @pl.when(qt == pl.num_programs(1) - 1)
    def _():
        dk_ref[...] = dk_s[...].astype(BF16)
        dv_ref[...] = dv_s[...].astype(BF16)


SMEM = pl.BlockSpec(memory_space=pltpu.SMEM)
TILE = 256


def attend(q, kv, start, nb, lam, gain_col):
    tok, width = q.shape
    heads = width // VDIM
    rows = kv.shape[0]
    size = min(TILE, tok)
    base = (rows - tok) // size
    head_block = pl.BlockSpec((VDIM, size), lambda h, t: (h, t))
    return pl.pallas_call(
        functools.partial(forward_kernel, base),
        grid=(heads, tok // size),
        out_shape=[
            jax.ShapeDtypeStruct((width, tok), F32),
            jax.ShapeDtypeStruct((width, tok), F32),
            jax.ShapeDtypeStruct((heads, 2, tok), F32),
            jax.ShapeDtypeStruct((tok, width), BF16),
        ],
        in_specs=[
            SMEM,
            SMEM,
            pl.BlockSpec((size, VDIM), lambda h, t: (t, h)),
            pl.BlockSpec((rows, VDIM), lambda h, t: (0, h)),
            pl.BlockSpec((rows, VDIM), lambda h, t: (0, heads + h)),
            pl.BlockSpec((1, size), lambda h, t: (0, t)),
            pl.BlockSpec((VDIM, 1), lambda h, t: (0, 0)),
        ],
        out_specs=[
            head_block,
            head_block,
            pl.BlockSpec((1, 2, size), lambda h, t: (h, 0, t)),
            pl.BlockSpec((size, VDIM), lambda h, t: (t, h)),
        ],
        scratch_shapes=[
            VMEM((2, 1, size), F32),
            VMEM((2, 1, size), F32),
            VMEM((2, VDIM, size), F32),
        ],
        cost_estimate=pl.CostEstimate(
            flops=4 * tok * rows * heads * VDIM,
            bytes_accessed=8 * tok * width + 4 * rows * width,
            transcendentals=2 * tok * rows * heads,
        ),
        compiler_params=pltpu.CompilerParams(vmem_limit_bytes=32 * 2**20),
    )(nb, lam, q, kv, kv, start, gain_col)


def attend_back(q, kv, start, nb, lam, gain_col, o1, o2, lse, dg):
    tok, width = q.shape
    heads = width // VDIM
    rows = kv.shape[0]
    size = min(TILE, tok)
    base = (rows - tok) // size
    head_block = pl.BlockSpec((VDIM, size), lambda h, t: (h, t))
    return pl.pallas_call(
        functools.partial(backward_kernel, base),
        grid=(heads, tok // size),
        out_shape=[
            jax.ShapeDtypeStruct((tok, width), BF16),
            jax.ShapeDtypeStruct((rows, width), BF16),
            jax.ShapeDtypeStruct((rows, width), BF16),
            jax.ShapeDtypeStruct((VDIM, 1), F32),
            jax.ShapeDtypeStruct((VDIM, 1), F32),
        ],
        in_specs=[
            SMEM,
            SMEM,
            pl.BlockSpec((size, VDIM), lambda h, t: (t, h)),
            pl.BlockSpec((rows, VDIM), lambda h, t: (0, h)),
            pl.BlockSpec((rows, VDIM), lambda h, t: (0, heads + h)),
            pl.BlockSpec((1, size), lambda h, t: (0, t)),
            pl.BlockSpec((VDIM, 1), lambda h, t: (0, 0)),
            head_block,
            head_block,
            pl.BlockSpec((1, 2, size), lambda h, t: (h, 0, t)),
            pl.BlockSpec((size, VDIM), lambda h, t: (t, h)),
        ],
        out_specs=[
            pl.BlockSpec((size, VDIM), lambda h, t: (t, h)),
            pl.BlockSpec((rows, VDIM), lambda h, t: (0, h)),
            pl.BlockSpec((rows, VDIM), lambda h, t: (0, h)),
            pl.BlockSpec((VDIM, 1), lambda h, t: (0, 0)),
            pl.BlockSpec((VDIM, 1), lambda h, t: (0, 0)),
        ],
        scratch_shapes=[
            VMEM((VDIM, size), F32),
            VMEM((rows, VDIM), F32),
            VMEM((rows, VDIM), F32),
        ],
        cost_estimate=pl.CostEstimate(
            flops=10 * tok * rows * heads * VDIM,
            bytes_accessed=16 * tok * width + 8 * rows * width,
            transcendentals=2 * tok * rows * heads,
        ),
        compiler_params=pltpu.CompilerParams(vmem_limit_bytes=40 * 2**20),
    )(nb, lam, q, kv, kv, start, gain_col, o1, o2, lse, dg)


CHUNKS = 2


def on_device(
    n_head,
    n_seq,
    inputs,
    w_query,
    w_key,
    w_value,
    w_output,
    w_gate,
    w_up,
    w_down,
    gain_attn,
    gain_ffn,
    group_gain,
    lambda_q1,
    lambda_k1,
    lambda_q2,
    lambda_k2,
    doc_ids,
    needles,
    out_grad,
):
    x = inputs[0]
    tok, cols = x.shape
    n, nc = n_head, CHUNKS
    full = n * cols
    width = w_query.shape[1]
    hidden = w_gate.shape[1]
    me = lax.axis_index("head")
    halo = n_seq // 2

    w_qkv = lax.all_gather(
        jnp.concatenate([w_query, w_key, w_value], axis=1), ("seq", "dp"), axis=0, tiled=True
    )
    w_rest = lax.all_gather(
        jnp.concatenate([w_output, w_gate, w_up, w_down], axis=1),
        ("seq", "dp"),
        axis=0,
        tiled=True,
    )
    w_out = w_rest[:, :width]
    w_gu = w_rest[:, width : width + 2 * hidden]
    w_dn = w_rest[:, width + 2 * hidden :]

    later = [(i, i + 1) for i in range(n_seq - 1)]
    docs = doc_ids[0] + 1
    window = [docs]
    for _ in range(halo):
        window.append(lax.ppermute(window[-1], "seq", later))
    window = jnp.concatenate(window[::-1])
    start = jnp.sum((window[None, :] < docs[:, None]).astype(jnp.int32), axis=1)
    size = min(TILE, tok)
    base = halo * tok // size
    first = start[::size]
    nb = base + jnp.arange(tok // size, dtype=jnp.int32) - first // size + 1
    start = start[None, :]

    weight = jnp.where(needles[0] == 1, 1.0, 0.1).astype(F32)
    dy = out_grad[0].astype(F32) * weight[:, None]
    gain_one = gain_attn[None, :]
    gain_two = gain_ffn[None, :]
    gain_one_cols = lax.dynamic_slice_in_dim(gain_one, me * cols, cols, 1)
    gain_two_cols = lax.dynamic_slice_in_dim(gain_two, me * cols, cols, 1)
    lam = jnp.exp(jnp.sum(lambda_q1 * lambda_k1)) - jnp.exp(jnp.sum(lambda_q2 * lambda_k2))
    lam = (lam + LAMBDA_INIT)[None]
    gain_col = group_gain[:, None]

    n1, scale_one, dyr = talk(
        functools.partial(enter_kernel, n),
        0,
        [((tok, full), BF16), ((tok, 1), F32), ((tok, full), BF16)],
        [VMEM((n, tok, cols), BF16), VMEM((n, tok, cols), BF16)] + [dma(n - 1, 1)] * 4,
        tok * full * 8,
        40 * 2**20,
        (x, dy.astype(BF16), gain_one),
    )
    qkv = jnp.dot(n1, w_qkv, preferred_element_type=F32).astype(BF16)
    q, kv = qkv[:, :width], qkv[:, width:]
    blocks = [kv]
    for _ in range(halo):
        blocks.append(lax.ppermute(blocks[-1], "seq", later))
    kv = jnp.concatenate(blocks[::-1], axis=0)
    o1, o2, lse, grouped = attend(q, kv, start, nb, lam, gain_col)

    exchange = [VMEM((tok, cols), F32), VMEM((n - 1, tok, cols), BF16), VMEM((n - 1, tok, cols), BF16)]
    h1, n2, scale_two = talk(
        functools.partial(middle_kernel, n, nc),
        1,
        [((tok, cols), F32), ((tok, full), BF16), ((tok, 1), F32)],
        exchange + [VMEM((n, tok, cols), BF16)] + [dma(n - 1, nc)] * 4,
        2 * tok * full * width,
        60 * 2**20,
        (grouped, w_out, x, gain_two),
    )
    gu = jnp.dot(n2, w_gu, preferred_element_type=F32)
    gate, upper = gu[:, :hidden], gu[:, hidden:]
    sigma = jax.nn.sigmoid(gate)
    inner = (gate * sigma * upper).astype(BF16)
    d_inner = jnp.dot(dyr, w_dn, preferred_element_type=F32)
    d_upper = (d_inner * gate * sigma).astype(BF16)
    d_gate = (d_inner * upper * sigma * (1.0 + gate * (1.0 - sigma))).astype(BF16)
    d_gu = jnp.concatenate([d_gate, d_upper], axis=1)

    stat = VMEM((n, nc, 8, tok // nc), F32)
    dh1, dh1r, gain_two_part = talk(
        functools.partial(back_kernel, n, nc),
        2,
        [((tok, cols), F32), ((tok, full), BF16), ((1, cols), F32)],
        exchange + [stat, VMEM((n, tok, cols), BF16)] + [dma(n - 1, nc)] * 6,
        4 * tok * full * hidden,
        60 * 2**20,
        (d_gu, w_gu, h1, scale_two, gain_two_cols, dy),
    )
    d_wgu = lax.dot_general(n2, d_gu, TN, preferred_element_type=F32)
    d_down = lax.dot_general(dyr, inner, TN, preferred_element_type=F32)
    g_ffn = lax.psum_scatter(
        jnp.concatenate([d_wgu.astype(BF16), d_down.astype(BF16)], axis=1),
        ("seq", "dp"),
        scatter_dimension=0,
        tiled=True,
    ).astype(F32)

    dg = jnp.dot(dh1r, w_out, preferred_element_type=F32)
    dq, dk, dv, group_part, lam_part = attend_back(
        q, kv, start, nb, lam, gain_col, o1, o2, lse, dg
    )
    before = [(i + 1, i) for i in range(n_seq - 1)]
    d_kv = jnp.concatenate([dk, dv], axis=1)
    come = None
    for b in range(halo):
        mine = d_kv[b * tok : (b + 1) * tok]
        if come is not None:
            mine = (mine.astype(F32) + come.astype(F32)).astype(BF16)
        come = lax.ppermute(mine, "seq", before)
    own = d_kv[halo * tok :]
    if come is not None:
        own = (own.astype(F32) + come.astype(F32)).astype(BF16)
    d_qkv = jnp.concatenate([dq, own], axis=1)

    input_grad, gain_one_part = talk(
        functools.partial(leave_kernel, n, nc),
        3,
        [((tok, cols), BF16), ((1, cols), F32)],
        exchange + [stat] + [dma(n - 1, nc)] * 4,
        2 * tok * full * 3 * width,
        40 * 2**20,
        (d_qkv, w_qkv, x, scale_one, gain_one_cols, dh1),
    )
    (output,) = talk(
        functools.partial(output_kernel, n, nc),
        4,
        [((tok, cols), BF16)],
        exchange + [dma(n - 1, nc)] * 2,
        2 * tok * full * hidden,
        40 * 2**20,
        (inner, w_dn, h1),
    )
    d_wqkv = lax.dot_general(n1, d_qkv, TN, preferred_element_type=F32)
    d_wout = lax.dot_general(dh1r, grouped, TN, preferred_element_type=F32)
    g_attn = lax.psum_scatter(
        jnp.concatenate([d_wqkv.astype(BF16), d_wout.astype(BF16)], axis=1),
        ("seq", "dp"),
        scatter_dimension=0,
        tiled=True,
    ).astype(F32)
    gain_attn_grad, gain_ffn_grad = (
        lax.psum_scatter(
            part[0].astype(BF16), ("seq", "dp"), scatter_dimension=0, tiled=True
        ).astype(F32)
        for part in (gain_one_part, gain_two_part)
    )
    lam_total, group_gain_grad = lax.psum(
        (jnp.sum(lam_part), group_part[:, 0]), ("head", "seq", "dp")
    )
    return (
        output[None],
        input_grad[None],
        gain_attn_grad,
        gain_ffn_grad,
        group_gain_grad,
        jnp.reshape(lam_total, (1,)),
        g_attn[:, :width],
        g_attn[:, width : 2 * width],
        g_attn[:, 2 * width : 3 * width],
        g_attn[:, 3 * width :],
        g_ffn[:, :hidden],
        g_ffn[:, hidden : 2 * hidden],
        g_ffn[:, 2 * hidden :],
    )


def solution(mesh):
    act = P("dp", "seq", "head")
    mat = P(("seq", "dp"), "head")
    vec = P(("head", "seq", "dp"))
    return jax.shard_map(
        functools.partial(on_device, mesh.shape["head"], mesh.shape["seq"]),
        mesh=mesh,
        in_specs=(act,) + (mat,) * 7 + (P(),) * 7 + (P("dp", "seq"),) * 2 + (act,),
        out_specs=(act, act, vec, vec, P(), P()) + (mat,) * 7,
        check_vma=False,
    )
```

```python
import functools
import math

import jax
import jax.numpy as jnp
from jax import lax
from jax.experimental import pallas as pl
from jax.experimental.pallas import tpu as pltpu
from jax.sharding import PartitionSpec as P

HALF = 64
VDIM = 128
EPS = 1e-05
LAMBDA_INIT = 0.8 - 0.6 * math.exp(-0.3)
KEEP = 1.0 - LAMBDA_INIT
NEG_BIG = -1e30
MESH = pl.DeviceIdType.MESH
VMEM = pltpu.VMEM
F32 = jnp.float32
BF16 = jnp.bfloat16
NN = (((1,), (0,)), ((), ()))
NT = (((1,), (1,)), ((), ()))
TN = (((0,), (0,)), ((), ()))


def mm(a, b, dims):
    return lax.dot_general(a, b, dims, preferred_element_type=F32)


def whole():
    return pl.BlockSpec(memory_space=VMEM)


def peer_of(me, k, n):
    return lax.rem(me + k, n)


def greet(*peers):
    barrier = pltpu.get_barrier_semaphore()
    for peer in peers:
        pl.semaphore_signal(barrier, 1, device_id=peer, device_id_type=MESH)
    pl.semaphore_wait(barrier, len(peers))


def along(axis, size, steps):
    spot = lax.axis_index(axis)
    return [{axis: lax.rem(spot + k, size)} for k in steps]


def group(n):
    return along("head", n, range(1, n))


def push(src, dst, send, recv, **peer):
    return pltpu.make_async_remote_copy(
        src_ref=src,
        dst_ref=dst,
        send_sem=send,
        recv_sem=recv,
        device_id=peer,
        device_id_type=MESH,
    )


def rows_of(c, size):
    return pl.ds(pl.multiple_of(c * size, size), size)


def fetch(w_hbm, off, w_ref, sem):
    copy = pltpu.make_async_copy(w_hbm.at[:, off : off + w_ref.shape[1]], w_ref, sem)
    copy.start()
    return copy


class Reduce:
    def __init__(self, n, size, me, own_ref, sbuf, rbuf, ssem, rsem):
        self.n, self.size, self.me = n, size, me
        self.own_ref, self.sbuf, self.rbuf, self.ssem, self.rsem = own_ref, sbuf, rbuf, ssem, rsem
        self.cols = own_ref.shape[1]

    def copy(self, k, c):
        rows = rows_of(c, self.size)
        return push(
            self.sbuf.at[k - 1, rows],
            self.rbuf.at[k - 1, rows],
            self.ssem.at[k - 1, c],
            self.rsem.at[k - 1, c],
            head=peer_of(self.me, k, self.n),
        )

    def send(self, first, last, pairs):
        n = self.n

        def step(t, _):
            turn = t // n
            c = first + turn
            k = t - turn * n + 1
            rows = rows_of(c, self.size)
            peer = peer_of(self.me, k, n)
            part = None
            for a_ref, behind, w_ref, off in pairs:
                span = slice(off, off + a_ref.shape[1])
                term = mm(
                    a_ref[rows_of(c - behind, self.size), :],
                    w_ref[rows_of(peer, self.cols), span],
                    NT,
                )
                part = term if part is None else part + term

            @pl.when(k < n)
            def _():
                self.sbuf[k - 1, rows] = part.astype(BF16)
                self.copy(k, c).start()

            @pl.when(k == n)
            def _():
                self.own_ref[rows, :] = part

            return 0

        lax.fori_loop(0, (last - first) * n, step, 0)

    def take(self, c):
        rows = rows_of(c, self.size)
        total = self.own_ref[rows, :]
        for k in range(1, self.n):
            self.copy(k, c).wait_recv()
        for k in range(1, self.n):
            total = total + self.rbuf[k - 1, rows].astype(F32)
        return total

    def finish(self, first, last):
        for c in range(first, last):
            for k in range(1, self.n):
                self.copy(k, c).wait_send()


class Gather:
    def __init__(self, n, nc, me, buf, ssem, rsem):
        self.n, self.nc, self.me = n, nc, me
        self.buf, self.ssem, self.rsem = buf, ssem, rsem
        self.size = buf.shape[1] // nc

    def copy(self, k, c, source):
        rows = rows_of(c, self.size)
        return push(
            self.buf.at[source, rows],
            self.buf.at[source, rows],
            self.ssem.at[k - 1, c],
            self.rsem.at[k - 1, c],
            head=peer_of(self.me, k, self.n),
        )

    def send(self, c, value=None):
        if value is not None:
            self.buf[self.me, rows_of(c, self.size)] = value
        for k in range(1, self.n):
            self.copy(k, c, self.me).start()

    def take(self, c):
        for k in range(1, self.n):
            self.copy(k, c, peer_of(self.me, self.n - k, self.n)).wait_recv()

    def finish(self, only=None):
        for c in range(self.nc) if only is None else (only,):
            for k in range(1, self.n):
                self.copy(k, c, self.me).wait_send()


def norm_rows(n, buf, rows, gain_ref, out_ref, scale_ref=None, scale_rows=None):
    cols = buf.shape[2]
    total = None
    for s in range(n):
        piece = buf[s, rows].astype(F32)
        part = jnp.sum(piece * piece, axis=1, keepdims=True)
        total = part if total is None else total + part
    scale = lax.rsqrt(total / (n * cols) + EPS)
    if scale_ref is not None:
        scale_ref[rows if scale_rows is None else scale_rows, :] = scale
    for s in range(n):
        span = slice(s * cols, (s + 1) * cols)
        piece = buf[s, rows].astype(F32)
        out_ref[rows, span] = (piece * scale * gain_ref[:, span]).astype(BF16)


def spread_rows(n, buf, rows, out_ref):
    cols = buf.shape[2]
    for s in range(n):
        out_ref[rows, s * cols : (s + 1) * cols] = buf[s, rows]


def enter_kernel(n, n_seq, halo, x_ref, dy_ref, gain_ref, docs_ref, n1_ref, scale_ref, dyr_ref, window_ref, n1t_hbm, xall, dall, docs, n1t_ref, ts, xs, xr, ds, dr, hs, hr, ks, kr):
    tok = x_ref.shape[0]
    spot = lax.axis_index("seq")
    me = lax.axis_index("head")
    more = spot + 1 < n_seq
    for k in range(1, halo + 1):
        @pl.when(spot < k)
        def _():
            docs[halo - k] = jnp.zeros_like(docs_ref)

    docs[halo] = docs_ref[...]
    xall[me, halo * tok :] = x_ref[...]
    greet(*group(n), *along("seq", n_seq, range(1, n_seq)))
    xg = Gather(n, halo + 1, me, xall, xs, xr)
    dg = Gather(n, 1, me, dall, ds, dr)

    def word(k):
        return push(
            docs.at[halo], docs.at[halo - k], ks.at[k - 1], kr.at[k - 1], seq=lax.rem(spot + k, n_seq)
        )

    def hop(j):
        here = pl.ds((halo - j + 1) * tok, tok)
        there = pl.ds((halo - j) * tok, tok)
        return push(
            xall.at[me, here], xall.at[me, there], hs.at[j - 1], hr.at[j - 1], seq=lax.rem(spot + 1, n_seq)
        )

    if halo:
        @pl.when(more)
        def _():
            hop(1).start()

    xg.send(halo)
    for k in range(1, halo + 1):
        @pl.when(spot + k < n_seq)
        def _():
            word(k).start()

    for j in range(1, halo + 1):
        @pl.when(spot >= j)
        def _():
            hop(j).wait_recv()

        if j < halo:
            @pl.when((spot >= j) & more)
            def _():
                hop(j + 1).start()

        @pl.when(spot >= j)
        def _():
            xg.send(halo - j)

    dg.send(0, dy_ref[...])
    for k in range(1, halo + 1):
        @pl.when(spot >= k)
        def _():
            word(k).wait_recv()

    for k in range(halo + 1):
        window_ref[:, k * tok : (k + 1) * tok] = docs[k]
    size = min(64, tok)
    per = tok // size
    xg.take(halo)

    @pl.loop(0, per)
    def _(i):
        norm_rows(n, xall, rows_of(halo * per + i, size), gain_ref, n1_ref, scale_ref, rows_of(i, size))

    for j in range(1, halo + 1):
        @pl.when(spot >= j)
        def _():
            xg.take(halo - j)

            @pl.loop(0, per)
            def _(i):
                norm_rows(n, xall, rows_of((halo - j) * per + i, size), gain_ref, n1_ref)

        @pl.when(spot < j)
        def _():
            n1_ref[(halo - j) * tok : (halo - j + 1) * tok, :] = jnp.zeros((tok, n1_ref.shape[1]), BF16)

    dg.take(0)

    @pl.loop(0, per)
    def _(i):
        spread_rows(n, dall, rows_of(i, size), dyr_ref)

    for k in range(halo + 1):
        rows = slice(k * tok, (k + 1) * tok)
        n1t_ref[:, rows] = n1_ref[rows, :].T
    leave = pltpu.make_async_copy(n1t_ref, n1t_hbm, ts)
    leave.start()
    xg.finish(halo)
    for j in range(1, halo + 1):
        @pl.when(spot >= j)
        def _():
            xg.finish(halo - j)

        @pl.when((spot >= j - 1) & more)
        def _():
            hop(j).wait_send()

        @pl.when(spot + j < n_seq)
        def _():
            word(j).wait_send()

    dg.finish()
    leave.wait()


def projection_kernel(halo, n1t_ref, dq_ref, dk_ref, dv_ref, dh1r_ref, g_ref, dw_hbm, dh1t, held, sems):
    full, width = n1t_ref.shape[0], dq_ref.shape[1]
    tok = dq_ref.shape[0]
    size = min(256, full)

    def leave(i):
        return pltpu.make_async_copy(held.at[i], dw_hbm.at[:, i * width : (i + 1) * width], sems.at[i])

    def fill(i, left, right):
        @pl.loop(0, full // size)
        def _(t):
            rows = rows_of(t, size)
            held[i, rows] = mm(left[rows, :], right[...], NN).astype(BF16)

        leave(i).start()

    fill(0, n1t_ref.at[:, halo * tok :], dq_ref)
    fill(1, n1t_ref, dk_ref)
    fill(2, n1t_ref, dv_ref)
    dh1t[...] = dh1r_ref[...].T
    fill(3, dh1t, g_ref)
    for i in range(4):
        leave(i).wait()


def projection_grads(halo, n1t, dq, dk, dv, dh1r, g):
    full, (tok, width) = n1t.shape[0], dq.shape
    args = (n1t, dq, dk, dv, dh1r, g)
    return pl.pallas_call(
        functools.partial(projection_kernel, halo),
        out_shape=pltpu.HBM((full, 4 * width), BF16),
        in_specs=[whole()] * len(args),
        out_specs=pl.BlockSpec(memory_space=pltpu.HBM),
        scratch_shapes=[VMEM((full, tok), BF16), VMEM((4, full, width), BF16), dma(4)],
        cost_estimate=pl.CostEstimate(
            flops=4 * full * width * (n1t.shape[1] + tok),
            bytes_accessed=2 * full * (n1t.shape[1] + 4 * width),
            transcendentals=0,
        ),
        compiler_params=pltpu.CompilerParams(vmem_limit_bytes=40 * 2**20),
    )(*args)


def ffn_kernel(n2_ref, dy_ref, wg_ref, wu_ref, wd_ref, hid_ref, dgate_ref, dup_ref, dw_hbm, n2t, dyt, held, sems):
    j, steps = pl.program_id(0), pl.num_programs(0)

    @pl.when(j == 0)
    def _():
        n2t[...] = n2_ref[...].T
        dyt[...] = dy_ref[...].T

    size = wg_ref.shape[1]
    slot = lax.rem(j, 2)

    def leave(i, step, slot):
        start = pl.multiple_of((i * steps + step) * size, size)
        return pltpu.make_async_copy(held.at[slot, i], dw_hbm.at[:, pl.ds(start, size)], sems.at[slot, i])

    gate = mm(n2_ref[...], wg_ref[...], NN)
    upper = mm(n2_ref[...], wu_ref[...], NN)
    sigma = lax.logistic(gate)
    act = gate * sigma
    hid_ref[...] = (act * upper).astype(BF16)
    d_hid = mm(dy_ref[...], wd_ref[...], NN)
    dup_ref[...] = (d_hid * act).astype(BF16)
    dgate_ref[...] = (d_hid * upper * sigma * (1.0 + gate * (1.0 - sigma))).astype(BF16)

    @pl.when(j >= 2)
    def _():
        for i in range(3):
            leave(i, j - 2, slot).wait()

    for i, (left, right) in enumerate(((n2t, dgate_ref), (n2t, dup_ref), (dyt, hid_ref))):
        held[slot, i] = mm(left[...], right[...], NN).astype(BF16)
        leave(i, j, slot).start()

    @pl.when(j == steps - 1)
    def _():
        for i in range(3):
            leave(i, j, slot).wait()

        @pl.when(j >= 1)
        def _():
            for i in range(3):
                leave(i, j - 1, 1 - slot).wait()


def ffn(n2, dyr, w, tile):
    tok, full = n2.shape
    hidden = w.shape[1] // 3
    steps = hidden // tile
    act = pl.BlockSpec((tok, full), lambda j: (0, 0))
    part = pl.BlockSpec((tok, tile), lambda j: (0, j))
    return pl.pallas_call(
        ffn_kernel,
        grid=(steps,),
        out_shape=[jax.ShapeDtypeStruct((tok, hidden), BF16)] * 3
        + [pltpu.HBM((full, 3 * hidden), BF16)],
        in_specs=[act, act]
        + [pl.BlockSpec((full, tile), functools.partial(lambda i, j: (0, i * steps + j), i)) for i in range(3)],
        out_specs=[part] * 3 + [pl.BlockSpec(memory_space=pltpu.HBM)],
        scratch_shapes=[
            VMEM((full, tok), BF16),
            VMEM((full, tok), BF16),
            VMEM((2, 3, full, tile), BF16),
            dma(2, 3),
        ],
        cost_estimate=pl.CostEstimate(
            flops=12 * tok * full * hidden,
            bytes_accessed=12 * full * hidden,
            transcendentals=tok * hidden,
        ),
        compiler_params=pltpu.CompilerParams(vmem_limit_bytes=40 * 2**20),
    )(n2, dyr, *(far_away(w),) * 3)


def middle_kernel(n, nc, off, g_ref, w_hbm, x_ref, gain_ref, h1_ref, n2_ref, scale_ref, own, sbuf, rbuf, w_ref, hall, ws, s1, r1, s2, r2):
    load = fetch(w_hbm, off, w_ref, ws)
    greet(*group(n))
    me = lax.axis_index("head")
    red = Reduce(n, own.shape[0] // nc, me, own, sbuf, rbuf, s1, r1)
    gat = Gather(n, nc, me, hall, s2, r2)
    load.wait()
    red.send(0, nc, [(g_ref, 0, w_ref, 0)])
    for c in range(nc):
        rows = rows_of(c, red.size)
        h1 = red.take(c) + x_ref[rows, :].astype(F32)
        h1_ref[rows, :] = h1
        gat.send(c, h1.astype(BF16))
    size = min(64, red.size)
    for c in range(nc):
        gat.take(c)

        @pl.loop(0, red.size // size)
        def _(i):
            norm_rows(n, hall, pl.ds(pl.multiple_of(c * red.size + i * size, size), size), gain_ref, n2_ref, scale_ref)

    red.finish(0, nc)
    gat.finish()


class Stats:
    def __init__(self, n, nc, me, buf, ssem, rsem):
        self.n, self.nc, self.me = n, nc, me
        self.buf, self.ssem, self.rsem = buf, ssem, rsem

    def copy(self, k, c, source):
        return push(
            self.buf.at[source, c],
            self.buf.at[source, c],
            self.ssem.at[k - 1, c],
            self.rsem.at[k - 1, c],
            head=peer_of(self.me, k, self.n),
        )

    def send(self, c, value):
        size, cols = value.shape
        part = value[:, :128]
        for j in range(1, cols // 128):
            part = part + value[:, j * 128 : (j + 1) * 128]
        line = jnp.sum(part.T, axis=0, keepdims=True)
        self.buf[self.me, c] = jnp.broadcast_to(line, (8, size))
        for k in range(1, self.n):
            self.copy(k, c, self.me).start()

    def take(self, c):
        for k in range(1, self.n):
            self.copy(k, c, peer_of(self.me, self.n - k, self.n)).wait_recv()
        total = self.buf[0, c]
        for s in range(1, self.n):
            total = total + self.buf[s, c]
        size = total.shape[1]
        tall = jnp.broadcast_to(total[:1, :], (128, size))
        return tall.T[:, :1]

    def finish(self):
        for c in range(self.nc):
            for k in range(1, self.n):
                self.copy(k, c, self.me).wait_send()


def norm_back(nc, size, width, grad_of, keep, sta, unit_of, gain_ref, base_of, gain_grad_ref, done):
    for c in range(nc):
        rows = rows_of(c, size)
        grad = grad_of(c)
        keep[rows, :] = grad
        unit = unit_of(rows)
        part = jnp.sum(grad * unit, axis=0, keepdims=True)
        if c == 0:
            gain_grad_ref[...] = part
        else:
            gain_grad_ref[...] += part
        sta.send(c, grad * gain_ref[...] * unit)
    for c in range(nc):
        rows = rows_of(c, size)
        dots = sta.take(c) / width
        scaled = keep[rows, :] * gain_ref[...]
        done(c, rows, base_of(rows, scaled - unit_of(rows) * dots))


def back_kernel(n, nc, off, dgate_ref, dup_ref, w_hbm, h1_ref, scale_ref, gain_ref, dy_ref, dh1_ref, dh1r_ref, gain_grad_ref, own, sbuf, rbuf, w_ref, stat, dall, ws, s1, r1, s2, r2, s3, r3):
    load = fetch(w_hbm, off, w_ref, ws)
    greet(*group(n))
    me = lax.axis_index("head")
    pairs = [(dgate_ref, 0, w_ref, 0), (dup_ref, 0, w_ref, dgate_ref.shape[1])]
    size = own.shape[0] // nc
    red = Reduce(n, size, me, own, sbuf, rbuf, s1, r1)
    sta = Stats(n, nc, me, stat, s2, r2)
    load.wait()
    gat = Gather(n, nc, me, dall, s3, r3)
    red.send(0, nc, pairs)

    def unit_of(rows):
        return h1_ref[rows, :].astype(BF16).astype(F32) * scale_ref[rows, :]

    def base_of(rows, back):
        return dy_ref[rows, :] + scale_ref[rows, :] * back

    def done(c, rows, value):
        dh1_ref[rows, :] = value
        gat.send(c, value.astype(BF16))

    norm_back(nc, size, n * red.cols, red.take, own, sta, unit_of, gain_ref, base_of, gain_grad_ref, done)
    for c in range(nc):
        gat.take(c)
        spread_rows(n, dall, rows_of(c, red.size), dh1r_ref)
    red.finish(0, nc)
    sta.finish()
    gat.finish()


def output_kernel(n, nc, off, a_ref, w_hbm, h1_ref, out_ref, own, sbuf, rbuf, w_ref, ws, s1, r1):
    load = fetch(w_hbm, off, w_ref, ws)
    greet(*group(n))
    me = lax.axis_index("head")
    red = Reduce(n, own.shape[0] // nc, me, own, sbuf, rbuf, s1, r1)
    load.wait()
    red.send(0, nc, [(a_ref, 0, w_ref, 0)])
    for c in range(nc):
        rows = rows_of(c, red.size)
        out_ref[rows, :] = (red.take(c) + h1_ref[rows, :]).astype(BF16)
    red.finish(0, nc)


def leave_kernel(n, n_seq, n_dp, halo, nc, dq_ref, dk_ref, dv_ref, w_hbm, x_ref, scale_ref, gain_ref, dh1_ref, gain_two_ref, group_ref, out_ref, sums_ref, own, sbuf, rbuf, w_ref, stat, gain_s, words, sums, zsend, zrecv, keep, ws, s1, r1, s2, r2, s3, r3, s4, r4, s5, r5):
    load = fetch(w_hbm, 0, w_ref, ws)
    spot, core = lax.axis_index("seq"), lax.axis_index("dp")
    others = [(i, j) for i in range(n_seq) for j in range(n_dp) if i or j]

    def of(i, j):
        return {"seq": lax.rem(spot + i, n_seq), "dp": lax.rem(core + j, n_dp)}

    def sends(j):
        return spot >= halo - j + 1

    def comes(j):
        return (spot + 1 < n_seq) & (spot + 1 >= halo - j + 1)

    for j in range(1, halo + 1):
        @pl.when(jnp.logical_not(comes(j)))
        def _():
            zrecv[j - 1] = jnp.zeros(zrecv.shape[1:], BF16)

    me = lax.axis_index("head")
    words[me] = group_ref[...]
    greet(*group(n), *(of(i, j) for i, j in others))
    tok, width = dq_ref.shape
    size = tok // nc
    red = Reduce(n, size, me, own, sbuf, rbuf, s1, r1)
    sta = Stats(n, nc, me, stat, s2, r2)

    def word(k, source):
        return push(
            words.at[source], words.at[source], s3.at[k - 1], r3.at[k - 1], head=peer_of(me, k, n)
        )

    def hop(j, c):
        rows = pl.ds(c * size, size)
        return push(
            zsend.at[j - 1, rows], zrecv.at[j - 1, rows], s5.at[j - 1, c], r5.at[j - 1, c], seq=lax.rem(spot + n_seq - 1, n_seq)
        )

    for k in range(1, n):
        word(k, me).start()
    load.wait()
    pairs = [(dk_ref, 0, w_ref, width), (dv_ref, 0, w_ref, 2 * width)]
    for b in range(halo):
        @pl.when(sends(b + 1))
        def _():
            red.send(b * nc, (b + 1) * nc, pairs)

    red.send(halo * nc, (halo + 1) * nc, [(dq_ref, halo * nc, w_ref, 0)] + pairs)

    def total(b, c):
        value = red.take(b * nc + c)
        if b == 0:
            return value

        @pl.when(comes(b))
        def _():
            hop(b, c).wait_recv()

        return value + zrecv[b - 1, pl.ds(c * size, size)].astype(F32)

    for j in range(1, halo + 1):
        for c in range(nc):
            @pl.when(sends(j))
            def _():
                zsend[j - 1, pl.ds(c * size, size)] = total(j - 1, c).astype(BF16)
                hop(j, c).start()

            if j > 1:
                @pl.when(jnp.logical_not(sends(j)) & comes(j - 1))
                def _():
                    hop(j - 1, c).wait_recv()

    def unit_of(rows):
        return x_ref[rows, :].astype(F32) * scale_ref[rows, :]

    def base_of(rows, back):
        return dh1_ref[rows, :] + scale_ref[rows, :] * back

    def done(c, rows, value):
        out_ref[rows, :] = value.astype(BF16)

    norm_back(nc, size, n * red.cols, functools.partial(total, halo), keep, sta, unit_of, gain_ref, base_of, gain_s, done)
    for k in range(1, n):
        word(k, peer_of(me, n - k, n)).wait_recv()
    total = words[0]
    for k in range(1, n):
        total = total + words[k]
    place = spot * n_dp + core
    mine = sums.at[place]
    cols = gain_s.shape[1]
    mine[...] = jnp.zeros((8, cols), F32)
    mine[0:1, :] = gain_s[...]
    mine[1:2, :] = gain_two_ref[...]
    mine[2:4, : total.shape[1]] = total[0:2]

    def share(t):
        i, j = others[t]
        return push(mine, mine, s4.at[t], r4.at[t], **of(i, j))

    def await_from(t):
        i, j = others[t]
        back = lax.rem(spot + n_seq - i, n_seq) * n_dp + lax.rem(core + n_dp - j, n_dp)
        theirs = sums.at[back]
        return push(theirs, theirs, s4.at[t], r4.at[t], **of(i, j))

    for t in range(len(others)):
        share(t).start()
    for t in range(len(others)):
        await_from(t).wait_recv()
    total = sums[0]
    for t in range(1, n_seq * n_dp):
        total = total + sums[t]
    sums_ref[...] = total
    for b in range(halo):
        @pl.when(sends(b + 1))
        def _():
            red.finish(b * nc, (b + 1) * nc)
            for c in range(nc):
                hop(b + 1, c).wait_send()

    red.finish(halo * nc, (halo + 1) * nc)
    sta.finish()
    for k in range(1, n):
        word(k, me).wait_send()
    for t in range(len(others)):
        share(t).wait_send()


def far_away(x):
    return pltpu.with_memory_space_constraint(x, pltpu.HBM)


def dma(*dims):
    return pltpu.SemaphoreType.DMA(dims)


def talk(kernel, ident, outs, scratch, flops, room, args, far=(), far_outs=()):
    return pl.pallas_call(
        kernel,
        out_shape=[
            pltpu.HBM(s, d) if i in far_outs else jax.ShapeDtypeStruct(s, d)
            for i, (s, d) in enumerate(outs)
        ],
        in_specs=[
            pl.BlockSpec(memory_space=pltpu.HBM) if i in far else whole() for i in range(len(args))
        ],
        out_specs=[
            pl.BlockSpec(memory_space=pltpu.HBM) if i in far_outs else whole()
            for i in range(len(outs))
        ],
        scratch_shapes=scratch,
        cost_estimate=pl.CostEstimate(flops=flops, bytes_accessed=40 * 2**20, transcendentals=0),
        compiler_params=pltpu.CompilerParams(
            collective_id=ident, has_side_effects=True, vmem_limit_bytes=room * 2**20
        ),
    )(*(far_away(a) if i in far else a for i, a in enumerate(args)))


def forward_kernel(base, nb_ref, lam_ref, q_ref, k_ref, v_ref, start_ref, gain_ref, o1_ref, o2_ref, lse_ref, g_ref, m_s, l_s, acc):
    size = q_ref.shape[0]
    qt = pl.program_id(1)
    q = q_ref[...] * 0.125
    lane = lax.broadcasted_iota(jnp.int32, q.shape, 1)
    zero = jnp.zeros_like(q)
    parts = (jnp.where(lane < HALF, q, zero), jnp.where(lane >= HALF, q, zero))
    key = lax.broadcasted_iota(jnp.int32, (size, size), 0)
    query = lax.broadcasted_iota(jnp.int32, (size, size), 1)
    start = start_ref[...]

    def block(where, first):
        rows = rows_of(where, size)
        k, v = k_ref[rows, :], v_ref[rows, :]
        allowed = key >= start - where * size
        if first:
            allowed = allowed & (key <= query)
        for m in range(2):
            s = jnp.where(allowed, mm(k, parts[m], NT), NEG_BIG)
            top = jnp.max(s, axis=0, keepdims=True)
            if first:
                e = jnp.exp(s - top)
                m_s[m] = top
                l_s[m] = jnp.sum(e, axis=0, keepdims=True)
                acc[m] = mm(v, e.astype(BF16), TN)
            else:
                new = jnp.maximum(m_s[m], top)
                e = jnp.exp(s - new)
                fade = jnp.exp(m_s[m] - new)
                m_s[m] = new
                l_s[m] = l_s[m] * fade + jnp.sum(e, axis=0, keepdims=True)
                acc[m] = acc[m] * fade + mm(v, e.astype(BF16), TN)

    block(base + qt, True)

    def earlier(d, _):
        block(base + qt - d, False)
        return 0

    lax.fori_loop(1, nb_ref[qt], earlier, 0)
    o1 = acc[0] / l_s[0]
    o2 = acc[1] / l_s[1]
    o1_ref[...] = o1
    o2_ref[...] = o2
    lse_ref[0, 0:1, :] = m_s[0] + jnp.log(l_s[0])
    lse_ref[0, 1:2, :] = m_s[1] + jnp.log(l_s[1])
    diff = o1 - lam_ref[0] * o2
    scale = lax.rsqrt(jnp.mean(diff * diff, axis=0, keepdims=True) + EPS)
    g = diff * scale * gain_ref[...] * KEEP
    g_ref[...] = g.T.astype(BF16)


def backward_kernel(base, nb_ref, lam_ref, q_ref, k_ref, v_ref, start_ref, gain_ref, o1_ref, o2_ref, lse_ref, dg_ref, dq_ref, dk_ref, dv_ref, gain_grad_ref, lam_grad_ref, dq_s, dk_s, dv_s):
    size = q_ref.shape[0]
    h, qt = pl.program_id(0), pl.program_id(1)
    lam = lam_ref[0]

    @pl.when((h == 0) & (qt == 0))
    def _():
        gain_grad_ref[...] = jnp.zeros_like(gain_grad_ref)
        lam_grad_ref[...] = jnp.zeros_like(lam_grad_ref)

    @pl.when(qt == 0)
    def _():
        dk_s[...] = jnp.zeros_like(dk_s)
        dv_s[...] = jnp.zeros_like(dv_s)

    o1, o2 = o1_ref[...], o2_ref[...]
    diff = o1 - lam * o2
    scale = lax.rsqrt(jnp.mean(diff * diff, axis=0, keepdims=True) + EPS)
    unit = diff * scale
    dg = dg_ref[...].T
    gain_grad_ref[...] += jnp.sum(dg * unit, axis=1, keepdims=True) * KEEP
    du = dg * gain_ref[...] * KEEP
    do = scale * (du - unit * jnp.mean(du * unit, axis=0, keepdims=True))
    lam_grad_ref[...] -= jnp.sum(do * o2, axis=1, keepdims=True)
    grads = (do.astype(BF16), (-lam * do).astype(BF16))
    deltas = tuple(
        jnp.sum(g.astype(F32) * o, axis=0, keepdims=True) for g, o in zip(grads, (o1, o2))
    )
    q = q_ref[...] * 0.125
    lane = lax.broadcasted_iota(jnp.int32, q.shape, 1)
    zero = jnp.zeros_like(q)
    parts = (jnp.where(lane < HALF, q, zero), jnp.where(lane >= HALF, q, zero))
    key = lax.broadcasted_iota(jnp.int32, (size, size), 0)
    query = lax.broadcasted_iota(jnp.int32, (size, size), 1)
    start = start_ref[...]
    dq_s[...] = jnp.zeros_like(dq_s)

    def block(where, first):
        rows = rows_of(where, size)
        k, v = k_ref[rows, :], v_ref[rows, :]
        halves = (jnp.where(lane < HALF, k, zero), jnp.where(lane >= HALF, k, zero))
        allowed = key >= start - where * size
        if first:
            allowed = allowed & (key <= query)
        dq = dq_s[...]
        dk = dk_s[rows, :]
        dv = dv_s[rows, :]
        for m in range(2):
            s = mm(k, parts[m], NT)
            p = jnp.where(allowed, jnp.exp(s - lse_ref[0, m : m + 1, :]), 0.0)
            dp = mm(v, grads[m], NN)
            ds = (p * (dp - deltas[m])).astype(BF16)
            dq = dq + mm(halves[m], ds, TN)
            dk = dk + mm(ds, parts[m], NN)
            dv = dv + mm(p.astype(BF16), grads[m], NT)
        dq_s[...] = dq
        dk_s[rows, :] = dk
        dv_s[rows, :] = dv

    block(base + qt, True)

    def earlier(d, _):
        block(base + qt - d, False)
        return 0

    lax.fori_loop(1, nb_ref[qt], earlier, 0)
    dq_ref[...] = (dq_s[...] * 0.125).T.astype(BF16)

    @pl.when(qt == pl.num_programs(1) - 1)
    def _():
        dk_ref[...] = dk_s[...].astype(BF16)
        dv_ref[...] = dv_s[...].astype(BF16)


SMEM = pl.BlockSpec(memory_space=pltpu.SMEM)
TILE = 256


def attend(q, kv, start, nb, lam, gain_col):
    tok, width = q.shape
    heads = width // VDIM
    rows = kv.shape[0]
    size = min(TILE, tok)
    base = (rows - tok) // size
    head_block = pl.BlockSpec((VDIM, size), lambda h, t: (h, t))
    return pl.pallas_call(
        functools.partial(forward_kernel, base),
        grid=(heads, tok // size),
        out_shape=[
            jax.ShapeDtypeStruct((width, tok), F32),
            jax.ShapeDtypeStruct((width, tok), F32),
            jax.ShapeDtypeStruct((heads, 2, tok), F32),
            jax.ShapeDtypeStruct((tok, width), BF16),
        ],
        in_specs=[
            SMEM,
            SMEM,
            pl.BlockSpec((size, VDIM), lambda h, t: (t, h)),
            pl.BlockSpec((rows, VDIM), lambda h, t: (0, h)),
            pl.BlockSpec((rows, VDIM), lambda h, t: (0, heads + h)),
            pl.BlockSpec((1, size), lambda h, t: (0, t)),
            pl.BlockSpec((VDIM, 1), lambda h, t: (0, 0)),
        ],
        out_specs=[
            head_block,
            head_block,
            pl.BlockSpec((1, 2, size), lambda h, t: (h, 0, t)),
            pl.BlockSpec((size, VDIM), lambda h, t: (t, h)),
        ],
        scratch_shapes=[
            VMEM((2, 1, size), F32),
            VMEM((2, 1, size), F32),
            VMEM((2, VDIM, size), F32),
        ],
        cost_estimate=pl.CostEstimate(
            flops=4 * tok * rows * heads * VDIM,
            bytes_accessed=8 * tok * width + 4 * rows * width,
            transcendentals=2 * tok * rows * heads,
        ),
        compiler_params=pltpu.CompilerParams(vmem_limit_bytes=32 * 2**20),
    )(nb, lam, q, kv, kv, start, gain_col)


def attend_back(q, kv, start, nb, lam, gain_col, o1, o2, lse, dg):
    tok, width = q.shape
    heads = width // VDIM
    rows = kv.shape[0]
    size = min(TILE, tok)
    base = (rows - tok) // size
    head_block = pl.BlockSpec((VDIM, size), lambda h, t: (h, t))
    return pl.pallas_call(
        functools.partial(backward_kernel, base),
        grid=(heads, tok // size),
        out_shape=[
            jax.ShapeDtypeStruct((tok, width), BF16),
            jax.ShapeDtypeStruct((rows, width), BF16),
            jax.ShapeDtypeStruct((rows, width), BF16),
            jax.ShapeDtypeStruct((VDIM, 1), F32),
            jax.ShapeDtypeStruct((VDIM, 1), F32),
        ],
        in_specs=[
            SMEM,
            SMEM,
            pl.BlockSpec((size, VDIM), lambda h, t: (t, h)),
            pl.BlockSpec((rows, VDIM), lambda h, t: (0, h)),
            pl.BlockSpec((rows, VDIM), lambda h, t: (0, heads + h)),
            pl.BlockSpec((1, size), lambda h, t: (0, t)),
            pl.BlockSpec((VDIM, 1), lambda h, t: (0, 0)),
            head_block,
            head_block,
            pl.BlockSpec((1, 2, size), lambda h, t: (h, 0, t)),
            pl.BlockSpec((size, VDIM), lambda h, t: (t, h)),
        ],
        out_specs=[
            pl.BlockSpec((size, VDIM), lambda h, t: (t, h)),
            pl.BlockSpec((rows, VDIM), lambda h, t: (0, h)),
            pl.BlockSpec((rows, VDIM), lambda h, t: (0, h)),
            pl.BlockSpec((VDIM, 1), lambda h, t: (0, 0)),
            pl.BlockSpec((VDIM, 1), lambda h, t: (0, 0)),
        ],
        scratch_shapes=[
            VMEM((VDIM, size), F32),
            VMEM((rows, VDIM), F32),
            VMEM((rows, VDIM), F32),
        ],
        cost_estimate=pl.CostEstimate(
            flops=10 * tok * rows * heads * VDIM,
            bytes_accessed=16 * tok * width + 8 * rows * width,
            transcendentals=2 * tok * rows * heads,
        ),
        compiler_params=pltpu.CompilerParams(vmem_limit_bytes=40 * 2**20),
    )(nb, lam, q, kv, kv, start, gain_col, o1, o2, lse, dg)


CHUNKS = 2


def on_device(
    n_head,
    n_seq,
    n_dp,
    inputs,
    w_query,
    w_key,
    w_value,
    w_output,
    w_gate,
    w_up,
    w_down,
    gain_attn,
    gain_ffn,
    group_gain,
    lambda_q1,
    lambda_k1,
    lambda_q2,
    lambda_k2,
    doc_ids,
    needles,
    out_grad,
):
    x = inputs[0]
    tok, cols = x.shape
    n, nc = n_head, CHUNKS
    full = n * cols
    width = w_query.shape[1]
    hidden = w_gate.shape[1]
    me = lax.axis_index("head")
    halo = n_seq // 2

    w_attn = lax.all_gather(
        jnp.concatenate([w_query, w_key, w_value, w_output], axis=1),
        ("seq", "dp"),
        axis=0,
        tiled=True,
    )
    w_ffn = lax.all_gather(
        jnp.concatenate([w_gate, w_up, w_down], axis=1), ("seq", "dp"), axis=0, tiled=True
    )

    weight = jnp.where(needles[0] == 1, 1.0, 0.1).astype(F32)
    dy = out_grad[0].astype(F32) * weight[:, None]
    gain_one = gain_attn[None, :]
    gain_two = gain_ffn[None, :]
    gain_one_cols = lax.dynamic_slice_in_dim(gain_one, me * cols, cols, 1)
    gain_two_cols = lax.dynamic_slice_in_dim(gain_two, me * cols, cols, 1)
    lam = jnp.exp(jnp.sum(lambda_q1 * lambda_k1)) - jnp.exp(jnp.sum(lambda_q2 * lambda_k2))
    lam = (lam + LAMBDA_INIT)[None]
    gain_col = group_gain[:, None]

    docs = jnp.broadcast_to(doc_ids + 1, (8, tok))
    n1, scale_one, dyr, window, n1t = talk(
        functools.partial(enter_kernel, n, n_seq, halo),
        0,
        [
            (((halo + 1) * tok, full), BF16),
            ((tok, 1), F32),
            ((tok, full), BF16),
            ((8, (halo + 1) * tok), jnp.int32),
            ((full, (halo + 1) * tok), BF16),
        ],
        [
            VMEM((n, (halo + 1) * tok, cols), BF16),
            VMEM((n, tok, cols), BF16),
            VMEM((halo + 1, 8, tok), jnp.int32),
            VMEM((full, (halo + 1) * tok), BF16),
            pltpu.SemaphoreType.DMA,
        ]
        + [dma(n - 1, halo + 1)] * 2
        + [dma(n - 1, 1)] * 2
        + [dma(max(halo, 1))] * 4,
        tok * full * 8,
        28 + 8 * halo,
        (x, dy.astype(BF16), gain_one, docs),
        far_outs=(4,),
    )
    start = jnp.sum((window[0][None, :] < docs[0][:, None]).astype(jnp.int32), axis=1)
    size = min(TILE, tok)
    base = halo * tok // size
    first = start[::size]
    nb = base + jnp.arange(tok // size, dtype=jnp.int32) - first // size + 1
    start = start[None, :]

    q = jnp.dot(n1[halo * tok :], w_attn[:, :width], preferred_element_type=F32).astype(BF16)
    kv = jnp.dot(n1, w_attn[:, width : 3 * width], preferred_element_type=F32).astype(BF16)
    o1, o2, lse, grouped = attend(q, kv, start, nb, lam, gain_col)

    exchange = [VMEM((tok, cols), F32), VMEM((n - 1, tok, cols), BF16), VMEM((n - 1, tok, cols), BF16)]
    h1, n2, scale_two = talk(
        functools.partial(middle_kernel, n, nc, 3 * width),
        1,
        [((tok, cols), F32), ((tok, full), BF16), ((tok, 1), F32)],
        exchange
        + [VMEM((full, width), BF16), VMEM((n, tok, cols), BF16), pltpu.SemaphoreType.DMA]
        + [dma(n - 1, nc)] * 4,
        2 * tok * full * width,
        24,
        (grouped, w_attn, x, gain_two),
        far=(1,),
    )
    tile = min(TILE, hidden)
    inner, d_gate, d_up, d_wffn = ffn(n2, dyr, w_ffn, tile)
    g_ffn = lax.psum_scatter(d_wffn, ("seq", "dp"), scatter_dimension=0, tiled=True)

    stat = VMEM((n, nc, 8, tok // nc), F32)
    dh1, dh1r, gain_two_part = talk(
        functools.partial(back_kernel, n, nc, 0),
        2,
        [((tok, cols), F32), ((tok, full), BF16), ((1, cols), F32)],
        exchange
        + [VMEM((full, 2 * hidden), BF16), stat, VMEM((n, tok, cols), BF16), pltpu.SemaphoreType.DMA]
        + [dma(n - 1, nc)] * 6,
        4 * tok * full * hidden,
        28,
        (d_gate, d_up, w_ffn, h1, scale_two, gain_two_cols, dy),
        far=(2,),
    )
    dg = jnp.dot(dh1r, w_attn[:, 3 * width :], preferred_element_type=F32)
    dq, dk, dv, group_part, lam_part = attend_back(
        q, kv, start, nb, lam, gain_col, o1, o2, lse, dg
    )
    d_wattn = projection_grads(halo, n1t, dq, dk, dv, dh1r, grouped)
    inner, d_wattn = lax.optimization_barrier((inner, d_wattn))
    (output,) = talk(
        functools.partial(output_kernel, n, nc, 2 * hidden),
        4,
        [((tok, cols), BF16)],
        exchange + [VMEM((full, hidden), BF16), pltpu.SemaphoreType.DMA] + [dma(n - 1, nc)] * 2,
        2 * tok * full * hidden,
        20,
        (inner, w_ffn, h1),
        far=(1,),
    )
    d_wattn, g_ffn, output = lax.optimization_barrier((d_wattn, g_ffn, output))
    g_ffn = g_ffn.astype(F32)
    g_attn = lax.psum_scatter(d_wattn, ("seq", "dp"), scatter_dimension=0, tiled=True).astype(F32)
    group_words = jnp.concatenate(
        [
            group_part.T,
            jnp.broadcast_to(jnp.sum(lam_part), (1, VDIM)),
            jnp.zeros((6, VDIM), F32),
        ]
    )
    others = n_seq * n_dp - 1
    span = (halo + 1) * tok
    input_grad, sums = talk(
        functools.partial(leave_kernel, n, n_seq, n_dp, halo, nc),
        3,
        [((tok, cols), BF16), ((8, cols), F32)],
        [
            VMEM((span, cols), F32),
            VMEM((n - 1, span, cols), BF16),
            VMEM((n - 1, span, cols), BF16),
            VMEM((full, 3 * width), BF16),
            stat,
            VMEM((1, cols), F32),
            VMEM((n, 8, VDIM), F32),
            VMEM((others + 1, 8, cols), F32),
            VMEM((max(halo, 1), tok, cols), BF16),
            VMEM((max(halo, 1), tok, cols), BF16),
            VMEM((tok, cols), F32),
            pltpu.SemaphoreType.DMA,
        ]
        + [dma(n - 1, (halo + 1) * nc)] * 2
        + [dma(n - 1, nc)] * 2
        + [dma(n - 1)] * 2
        + [dma(max(others, 1))] * 2
        + [dma(max(halo, 1), nc)] * 2,
        6 * tok * full * width * (halo + 1),
        26 + 5 * halo,
        (dq, dk, dv, w_attn, x, scale_one, gain_one_cols, dh1, gain_two_part, group_words),
        far=(3,),
    )
    share = cols // (n_seq * n_dp)
    place = lax.axis_index("seq") * n_dp + lax.axis_index("dp")
    gains = lax.dynamic_slice_in_dim(sums[:2], place * share, share, 1)
    return (
        output[None],
        input_grad[None],
        gains[0],
        gains[1],
        sums[2, :VDIM],
        sums[3, :1],
        g_attn[:, :width],
        g_attn[:, width : 2 * width],
        g_attn[:, 2 * width : 3 * width],
        g_attn[:, 3 * width :],
        g_ffn[:, :hidden],
        g_ffn[:, hidden : 2 * hidden],
        g_ffn[:, 2 * hidden :],
    )


def solution(mesh):
    act = P("dp", "seq", "head")
    mat = P(("seq", "dp"), "head")
    vec = P(("head", "seq", "dp"))
    return jax.shard_map(
        functools.partial(on_device, mesh.shape["head"], mesh.shape["seq"], mesh.shape["dp"]),
        mesh=mesh,
        in_specs=(act,) + (mat,) * 7 + (P(),) * 7 + (P("dp", "seq"),) * 2 + (act,),
        out_specs=(act, act, vec, vec, P(), P()) + (mat,) * 7,
        check_vma=False,
    )
```

```python
import functools
import math

import jax
import jax.numpy as jnp
from jax import lax
from jax.experimental import pallas as pl
from jax.experimental.pallas import tpu as pltpu
from jax.sharding import PartitionSpec as P

HALF = 64
VDIM = 128
EPS = 1e-05
LAMBDA_INIT = 0.8 - 0.6 * math.exp(-0.3)
KEEP = 1.0 - LAMBDA_INIT
NEG_BIG = -1e30
MESH = pl.DeviceIdType.MESH
VMEM = pltpu.VMEM
F32 = jnp.float32
BF16 = jnp.bfloat16
NN = (((1,), (0,)), ((), ()))
NT = (((1,), (1,)), ((), ()))
TN = (((0,), (0,)), ((), ()))


def mm(a, b, dims):
    return lax.dot_general(a, b, dims, preferred_element_type=F32)


def whole():
    return pl.BlockSpec(memory_space=VMEM)


def peer_of(me, k, n):
    return lax.rem(me + k, n)


def greet(*peers):
    barrier = pltpu.get_barrier_semaphore()
    for peer in peers:
        pl.semaphore_signal(barrier, 1, device_id=peer, device_id_type=MESH)
    pl.semaphore_wait(barrier, len(peers))


def along(axis, size, steps):
    spot = lax.axis_index(axis)
    return [{axis: lax.rem(spot + k, size)} for k in steps]


def group(n):
    return along("head", n, range(1, n))


def push(src, dst, send, recv, **peer):
    return pltpu.make_async_remote_copy(
        src_ref=src,
        dst_ref=dst,
        send_sem=send,
        recv_sem=recv,
        device_id=peer,
        device_id_type=MESH,
    )


def rows_of(c, size):
    return pl.ds(pl.multiple_of(c * size, size), size)


def fetch(w_hbm, off, w_ref, sem):
    copy = pltpu.make_async_copy(w_hbm.at[:, off : off + w_ref.shape[1]], w_ref, sem)
    copy.start()
    return copy


class Reduce:
    def __init__(self, n, size, me, own_ref, sbuf, rbuf, ssem, rsem):
        self.n, self.size, self.me = n, size, me
        self.own_ref, self.sbuf, self.rbuf, self.ssem, self.rsem = own_ref, sbuf, rbuf, ssem, rsem
        self.cols = own_ref.shape[1]

    def copy(self, k, c):
        rows = rows_of(c, self.size)
        return push(
            self.sbuf.at[k - 1, rows],
            self.rbuf.at[k - 1, rows],
            self.ssem.at[k - 1, c],
            self.rsem.at[k - 1, c],
            head=peer_of(self.me, k, self.n),
        )

    def send(self, first, last, pairs):
        n = self.n

        def step(t, _):
            turn = t // n
            c = first + turn
            k = t - turn * n + 1
            rows = rows_of(c, self.size)
            peer = peer_of(self.me, k, n)
            part = None
            for a_ref, behind, w_ref, off in pairs:
                span = slice(off, off + a_ref.shape[1])
                term = mm(
                    a_ref[rows_of(c - behind, self.size), :],
                    w_ref[rows_of(peer, self.cols), span],
                    NT,
                )
                part = term if part is None else part + term

            @pl.when(k < n)
            def _():
                self.sbuf[k - 1, rows] = part.astype(BF16)
                self.copy(k, c).start()

            @pl.when(k == n)
            def _():
                self.own_ref[rows, :] = part

            return 0

        lax.fori_loop(0, (last - first) * n, step, 0)

    def take(self, c):
        rows = rows_of(c, self.size)
        total = self.own_ref[rows, :]
        for k in range(1, self.n):
            self.copy(k, c).wait_recv()
        for k in range(1, self.n):
            total = total + self.rbuf[k - 1, rows].astype(F32)
        return total

    def finish(self, first, last):
        for c in range(first, last):
            for k in range(1, self.n):
                self.copy(k, c).wait_send()


class Gather:
    def __init__(self, n, nc, me, buf, ssem, rsem):
        self.n, self.nc, self.me = n, nc, me
        self.buf, self.ssem, self.rsem = buf, ssem, rsem
        self.size = buf.shape[1] // nc

    def copy(self, k, c, source):
        rows = rows_of(c, self.size)
        return push(
            self.buf.at[source, rows],
            self.buf.at[source, rows],
            self.ssem.at[k - 1, c],
            self.rsem.at[k - 1, c],
            head=peer_of(self.me, k, self.n),
        )

    def send(self, c, value=None):
        if value is not None:
            self.buf[self.me, rows_of(c, self.size)] = value
        for k in range(1, self.n):
            self.copy(k, c, self.me).start()

    def take(self, c):
        for k in range(1, self.n):
            self.copy(k, c, peer_of(self.me, self.n - k, self.n)).wait_recv()

    def finish(self, only=None):
        for c in range(self.nc) if only is None else (only,):
            for k in range(1, self.n):
                self.copy(k, c, self.me).wait_send()


def norm_rows(n, buf, rows, gain_ref, out_ref, scale_ref=None, scale_rows=None):
    cols = buf.shape[2]
    total = None
    for s in range(n):
        piece = buf[s, rows].astype(F32)
        part = jnp.sum(piece * piece, axis=1, keepdims=True)
        total = part if total is None else total + part
    scale = lax.rsqrt(total / (n * cols) + EPS)
    if scale_ref is not None:
        scale_ref[rows if scale_rows is None else scale_rows, :] = scale
    for s in range(n):
        span = slice(s * cols, (s + 1) * cols)
        piece = buf[s, rows].astype(F32)
        out_ref[rows, span] = (piece * scale * gain_ref[:, span]).astype(BF16)


def spread_rows(n, buf, rows, out_ref):
    cols = buf.shape[2]
    for s in range(n):
        out_ref[rows, s * cols : (s + 1) * cols] = buf[s, rows]


def enter_kernel(n, n_seq, halo, x_ref, dy_ref, gain_ref, docs_ref, n1_ref, scale_ref, dyr_ref, window_ref, n1t_hbm, xall, dall, docs, n1t_ref, ts, xs, xr, ds, dr, hs, hr, ks, kr):
    tok = x_ref.shape[0]
    spot = lax.axis_index("seq")
    me = lax.axis_index("head")
    more = spot + 1 < n_seq
    for k in range(1, halo + 1):
        @pl.when(spot < k)
        def _():
            docs[halo - k] = jnp.zeros_like(docs_ref)

    docs[halo] = docs_ref[...]
    xall[me, halo * tok :] = x_ref[...]
    greet(*group(n), *along("seq", n_seq, range(1, n_seq)))
    xg = Gather(n, halo + 1, me, xall, xs, xr)
    dg = Gather(n, 1, me, dall, ds, dr)

    def word(k):
        return push(
            docs.at[halo], docs.at[halo - k], ks.at[k - 1], kr.at[k - 1], seq=lax.rem(spot + k, n_seq)
        )

    def hop(j):
        here = pl.ds((halo - j + 1) * tok, tok)
        there = pl.ds((halo - j) * tok, tok)
        return push(
            xall.at[me, here], xall.at[me, there], hs.at[j - 1], hr.at[j - 1], seq=lax.rem(spot + 1, n_seq)
        )

    if halo:
        @pl.when(more)
        def _():
            hop(1).start()

    xg.send(halo)
    for k in range(1, halo + 1):
        @pl.when(spot + k < n_seq)
        def _():
            word(k).start()

    for j in range(1, halo + 1):
        @pl.when(spot >= j)
        def _():
            hop(j).wait_recv()

        if j < halo:
            @pl.when((spot >= j) & more)
            def _():
                hop(j + 1).start()

        @pl.when(spot >= j)
        def _():
            xg.send(halo - j)

    dg.send(0, dy_ref[...])
    for k in range(1, halo + 1):
        @pl.when(spot >= k)
        def _():
            word(k).wait_recv()

    for k in range(halo + 1):
        window_ref[:, k * tok : (k + 1) * tok] = docs[k]
    size = min(64, tok)
    per = tok // size
    xg.take(halo)

    @pl.loop(0, per)
    def _(i):
        norm_rows(n, xall, rows_of(halo * per + i, size), gain_ref, n1_ref, scale_ref, rows_of(i, size))

    for j in range(1, halo + 1):
        @pl.when(spot >= j)
        def _():
            xg.take(halo - j)

            @pl.loop(0, per)
            def _(i):
                norm_rows(n, xall, rows_of((halo - j) * per + i, size), gain_ref, n1_ref)

        @pl.when(spot < j)
        def _():
            n1_ref[(halo - j) * tok : (halo - j + 1) * tok, :] = jnp.zeros((tok, n1_ref.shape[1]), BF16)

    dg.take(0)

    @pl.loop(0, per)
    def _(i):
        spread_rows(n, dall, rows_of(i, size), dyr_ref)

    for k in range(halo + 1):
        rows = slice(k * tok, (k + 1) * tok)
        n1t_ref[:, rows] = n1_ref[rows, :].T
    leave = pltpu.make_async_copy(n1t_ref, n1t_hbm, ts)
    leave.start()
    xg.finish(halo)
    for j in range(1, halo + 1):
        @pl.when(spot >= j)
        def _():
            xg.finish(halo - j)

        @pl.when((spot >= j - 1) & more)
        def _():
            hop(j).wait_send()

        @pl.when(spot + j < n_seq)
        def _():
            word(j).wait_send()

    dg.finish()
    leave.wait()


def projection_kernel(halo, n1t_ref, dq_ref, dk_ref, dv_ref, dh1r_ref, g_ref, dw_hbm, dh1t, held, sems):
    full, width = n1t_ref.shape[0], dq_ref.shape[1]
    tok = dq_ref.shape[0]
    size = min(256, full)

    def leave(i):
        return pltpu.make_async_copy(held.at[i], dw_hbm.at[:, i * width : (i + 1) * width], sems.at[i])

    def fill(i, left, right):
        @pl.loop(0, full // size)
        def _(t):
            rows = rows_of(t, size)
            held[i, rows] = mm(left[rows, :], right[...], NN).astype(BF16)

        leave(i).start()

    fill(0, n1t_ref.at[:, halo * tok :], dq_ref)
    fill(1, n1t_ref, dk_ref)
    fill(2, n1t_ref, dv_ref)
    dh1t[...] = dh1r_ref[...].T
    fill(3, dh1t, g_ref)
    for i in range(4):
        leave(i).wait()


def projection_grads(halo, n1t, dq, dk, dv, dh1r, g):
    full, (tok, width) = n1t.shape[0], dq.shape
    args = (n1t, dq, dk, dv, dh1r, g)
    return pl.pallas_call(
        functools.partial(projection_kernel, halo),
        out_shape=pltpu.HBM((full, 4 * width), BF16),
        in_specs=[whole()] * len(args),
        out_specs=pl.BlockSpec(memory_space=pltpu.HBM),
        scratch_shapes=[VMEM((full, tok), BF16), VMEM((4, full, width), BF16), dma(4)],
        cost_estimate=pl.CostEstimate(
            flops=4 * full * width * (n1t.shape[1] + tok),
            bytes_accessed=2 * full * (n1t.shape[1] + 4 * width),
            transcendentals=0,
        ),
        compiler_params=pltpu.CompilerParams(vmem_limit_bytes=40 * 2**20),
    )(*args)


def ffn_kernel(n2_ref, dy_ref, wg_ref, wu_ref, wd_ref, hid_ref, dgate_ref, dup_ref, dw_hbm, n2t, dyt, held, sems):
    j, steps = pl.program_id(0), pl.num_programs(0)

    @pl.when(j == 0)
    def _():
        n2t[...] = n2_ref[...].T
        dyt[...] = dy_ref[...].T

    size = wg_ref.shape[1]
    slot = lax.rem(j, 2)

    def leave(i, step, slot):
        start = pl.multiple_of((i * steps + step) * size, size)
        return pltpu.make_async_copy(held.at[slot, i], dw_hbm.at[:, pl.ds(start, size)], sems.at[slot, i])

    gate = mm(n2_ref[...], wg_ref[...], NN)
    upper = mm(n2_ref[...], wu_ref[...], NN)
    sigma = lax.logistic(gate)
    act = gate * sigma
    hid_ref[...] = (act * upper).astype(BF16)
    d_hid = mm(dy_ref[...], wd_ref[...], NN)
    dup_ref[...] = (d_hid * act).astype(BF16)
    dgate_ref[...] = (d_hid * upper * sigma * (1.0 + gate * (1.0 - sigma))).astype(BF16)

    @pl.when(j >= 2)
    def _():
        for i in range(3):
            leave(i, j - 2, slot).wait()

    for i, (left, right) in enumerate(((n2t, dgate_ref), (n2t, dup_ref), (dyt, hid_ref))):
        held[slot, i] = mm(left[...], right[...], NN).astype(BF16)
        leave(i, j, slot).start()

    @pl.when(j == steps - 1)
    def _():
        for i in range(3):
            leave(i, j, slot).wait()

        @pl.when(j >= 1)
        def _():
            for i in range(3):
                leave(i, j - 1, 1 - slot).wait()


def ffn(n2, dyr, w, tile):
    tok, full = n2.shape
    hidden = w.shape[1] // 3
    steps = hidden // tile
    act = pl.BlockSpec((tok, full), lambda j: (0, 0))
    part = pl.BlockSpec((tok, tile), lambda j: (0, j))
    return pl.pallas_call(
        ffn_kernel,
        grid=(steps,),
        out_shape=[jax.ShapeDtypeStruct((tok, hidden), BF16)] * 3
        + [pltpu.HBM((full, 3 * hidden), BF16)],
        in_specs=[act, act]
        + [pl.BlockSpec((full, tile), functools.partial(lambda i, j: (0, i * steps + j), i)) for i in range(3)],
        out_specs=[part] * 3 + [pl.BlockSpec(memory_space=pltpu.HBM)],
        scratch_shapes=[
            VMEM((full, tok), BF16),
            VMEM((full, tok), BF16),
            VMEM((2, 3, full, tile), BF16),
            dma(2, 3),
        ],
        cost_estimate=pl.CostEstimate(
            flops=12 * tok * full * hidden,
            bytes_accessed=12 * full * hidden,
            transcendentals=tok * hidden,
        ),
        compiler_params=pltpu.CompilerParams(vmem_limit_bytes=40 * 2**20),
    )(n2, dyr, *(far_away(w),) * 3)


def middle_kernel(n, nc, off, g_ref, w_hbm, x_ref, gain_ref, h1_ref, n2_ref, scale_ref, own, sbuf, rbuf, w_ref, hall, ws, s1, r1, s2, r2):
    load = fetch(w_hbm, off, w_ref, ws)
    greet(*group(n))
    me = lax.axis_index("head")
    red = Reduce(n, own.shape[0] // nc, me, own, sbuf, rbuf, s1, r1)
    gat = Gather(n, nc, me, hall, s2, r2)
    load.wait()
    red.send(0, nc, [(g_ref, 0, w_ref, 0)])
    for c in range(nc):
        rows = rows_of(c, red.size)
        h1 = red.take(c) + x_ref[rows, :].astype(F32)
        h1_ref[rows, :] = h1
        gat.send(c, h1.astype(BF16))
    size = min(64, red.size)
    for c in range(nc):
        gat.take(c)

        @pl.loop(0, red.size // size)
        def _(i):
            norm_rows(n, hall, pl.ds(pl.multiple_of(c * red.size + i * size, size), size), gain_ref, n2_ref, scale_ref)

    red.finish(0, nc)
    gat.finish()


class Stats:
    def __init__(self, n, nc, me, buf, ssem, rsem):
        self.n, self.nc, self.me = n, nc, me
        self.buf, self.ssem, self.rsem = buf, ssem, rsem

    def copy(self, k, c, source):
        return push(
            self.buf.at[source, c],
            self.buf.at[source, c],
            self.ssem.at[k - 1, c],
            self.rsem.at[k - 1, c],
            head=peer_of(self.me, k, self.n),
        )

    def send(self, c, value):
        size, cols = value.shape
        part = value[:, :128]
        for j in range(1, cols // 128):
            part = part + value[:, j * 128 : (j + 1) * 128]
        line = jnp.sum(part.T, axis=0, keepdims=True)
        self.buf[self.me, c] = jnp.broadcast_to(line, (8, size))
        for k in range(1, self.n):
            self.copy(k, c, self.me).start()

    def take(self, c):
        for k in range(1, self.n):
            self.copy(k, c, peer_of(self.me, self.n - k, self.n)).wait_recv()
        total = self.buf[0, c]
        for s in range(1, self.n):
            total = total + self.buf[s, c]
        size = total.shape[1]
        tall = jnp.broadcast_to(total[:1, :], (128, size))
        return tall.T[:, :1]

    def finish(self):
        for c in range(self.nc):
            for k in range(1, self.n):
                self.copy(k, c, self.me).wait_send()


def norm_back(nc, size, width, grad_of, keep, sta, unit_of, gain_ref, base_of, gain_grad_ref, done):
    for c in range(nc):
        rows = rows_of(c, size)
        grad = grad_of(c)
        keep[rows, :] = grad
        unit = unit_of(rows)
        part = jnp.sum(grad * unit, axis=0, keepdims=True)
        if c == 0:
            gain_grad_ref[...] = part
        else:
            gain_grad_ref[...] += part
        sta.send(c, grad * gain_ref[...] * unit)
    for c in range(nc):
        rows = rows_of(c, size)
        dots = sta.take(c) / width
        scaled = keep[rows, :] * gain_ref[...]
        done(c, rows, base_of(rows, scaled - unit_of(rows) * dots))


def back_kernel(n, nc, off, dgate_ref, dup_ref, w_hbm, h1_ref, scale_ref, gain_ref, dy_ref, dh1_ref, dh1r_ref, gain_grad_ref, own, sbuf, rbuf, w_ref, stat, dall, ws, s1, r1, s2, r2, s3, r3):
    load = fetch(w_hbm, off, w_ref, ws)
    greet(*group(n))
    me = lax.axis_index("head")
    pairs = [(dgate_ref, 0, w_ref, 0), (dup_ref, 0, w_ref, dgate_ref.shape[1])]
    size = own.shape[0] // nc
    red = Reduce(n, size, me, own, sbuf, rbuf, s1, r1)
    sta = Stats(n, nc, me, stat, s2, r2)
    load.wait()
    gat = Gather(n, nc, me, dall, s3, r3)
    red.send(0, nc, pairs)

    def unit_of(rows):
        return h1_ref[rows, :].astype(BF16).astype(F32) * scale_ref[rows, :]

    def base_of(rows, back):
        return dy_ref[rows, :] + scale_ref[rows, :] * back

    def done(c, rows, value):
        dh1_ref[rows, :] = value
        gat.send(c, value.astype(BF16))

    norm_back(nc, size, n * red.cols, red.take, own, sta, unit_of, gain_ref, base_of, gain_grad_ref, done)
    for c in range(nc):
        gat.take(c)
        spread_rows(n, dall, rows_of(c, red.size), dh1r_ref)
    red.finish(0, nc)
    sta.finish()
    gat.finish()


def output_kernel(n, nc, off, a_ref, w_hbm, h1_ref, out_ref, own, sbuf, rbuf, w_ref, ws, s1, r1):
    load = fetch(w_hbm, off, w_ref, ws)
    greet(*group(n))
    me = lax.axis_index("head")
    red = Reduce(n, own.shape[0] // nc, me, own, sbuf, rbuf, s1, r1)
    load.wait()
    red.send(0, nc, [(a_ref, 0, w_ref, 0)])
    for c in range(nc):
        rows = rows_of(c, red.size)
        out_ref[rows, :] = (red.take(c) + h1_ref[rows, :]).astype(BF16)
    red.finish(0, nc)


def leave_kernel(n, n_seq, n_dp, halo, nc, dq_ref, dk_ref, dv_ref, w_hbm, x_ref, scale_ref, gain_ref, dh1_ref, gain_two_ref, group_ref, out_ref, sums_ref, own, sbuf, rbuf, w_ref, stat, gain_s, words, sums, zsend, zrecv, keep, ws, s1, r1, s2, r2, s3, r3, s4, r4, s5, r5):
    load = fetch(w_hbm, 0, w_ref, ws)
    spot, core = lax.axis_index("seq"), lax.axis_index("dp")
    others = [(i, j) for i in range(n_seq) for j in range(n_dp) if i or j]

    def of(i, j):
        return {"seq": lax.rem(spot + i, n_seq), "dp": lax.rem(core + j, n_dp)}

    def sends(j):
        return spot >= halo - j + 1

    def comes(j):
        return (spot + 1 < n_seq) & (spot + 1 >= halo - j + 1)

    for j in range(1, halo + 1):
        @pl.when(jnp.logical_not(comes(j)))
        def _():
            zrecv[j - 1] = jnp.zeros(zrecv.shape[1:], BF16)

    me = lax.axis_index("head")
    words[me] = group_ref[...]
    greet(*group(n), *(of(i, j) for i, j in others))
    tok, width = dq_ref.shape
    size = tok // nc
    red = Reduce(n, size, me, own, sbuf, rbuf, s1, r1)
    sta = Stats(n, nc, me, stat, s2, r2)

    def word(k, source):
        return push(
            words.at[source], words.at[source], s3.at[k - 1], r3.at[k - 1], head=peer_of(me, k, n)
        )

    def hop(j, c):
        rows = pl.ds(c * size, size)
        return push(
            zsend.at[j - 1, rows], zrecv.at[j - 1, rows], s5.at[j - 1, c], r5.at[j - 1, c], seq=lax.rem(spot + n_seq - 1, n_seq)
        )

    for k in range(1, n):
        word(k, me).start()
    load.wait()
    pairs = [(dk_ref, 0, w_ref, width), (dv_ref, 0, w_ref, 2 * width)]
    for b in range(halo):
        @pl.when(sends(b + 1))
        def _():
            red.send(b * nc, (b + 1) * nc, pairs)

    red.send(halo * nc, (halo + 1) * nc, [(dq_ref, halo * nc, w_ref, 0)] + pairs)

    def total(b, c):
        value = red.take(b * nc + c)
        if b == 0:
            return value

        @pl.when(comes(b))
        def _():
            hop(b, c).wait_recv()

        return value + zrecv[b - 1, pl.ds(c * size, size)].astype(F32)

    for j in range(1, halo + 1):
        for c in range(nc):
            @pl.when(sends(j))
            def _():
                zsend[j - 1, pl.ds(c * size, size)] = total(j - 1, c).astype(BF16)
                hop(j, c).start()

            if j > 1:
                @pl.when(jnp.logical_not(sends(j)) & comes(j - 1))
                def _():
                    hop(j - 1, c).wait_recv()

    def unit_of(rows):
        return x_ref[rows, :].astype(F32) * scale_ref[rows, :]

    def base_of(rows, back):
        return dh1_ref[rows, :] + scale_ref[rows, :] * back

    def done(c, rows, value):
        out_ref[rows, :] = value.astype(BF16)

    norm_back(nc, size, n * red.cols, functools.partial(total, halo), keep, sta, unit_of, gain_ref, base_of, gain_s, done)
    for k in range(1, n):
        word(k, peer_of(me, n - k, n)).wait_recv()
    total = words[0]
    for k in range(1, n):
        total = total + words[k]
    place = spot * n_dp + core
    mine = sums.at[place]
    cols = gain_s.shape[1]
    mine[...] = jnp.zeros((8, cols), F32)
    mine[0:1, :] = gain_s[...]
    mine[1:2, :] = gain_two_ref[...]
    mine[2:4, : total.shape[1]] = total[0:2]

    def share(t):
        i, j = others[t]
        return push(mine, mine, s4.at[t], r4.at[t], **of(i, j))

    def await_from(t):
        i, j = others[t]
        back = lax.rem(spot + n_seq - i, n_seq) * n_dp + lax.rem(core + n_dp - j, n_dp)
        theirs = sums.at[back]
        return push(theirs, theirs, s4.at[t], r4.at[t], **of(i, j))

    for t in range(len(others)):
        share(t).start()
    for t in range(len(others)):
        await_from(t).wait_recv()
    total = sums[0]
    for t in range(1, n_seq * n_dp):
        total = total + sums[t]
    sums_ref[...] = total
    for b in range(halo):
        @pl.when(sends(b + 1))
        def _():
            red.finish(b * nc, (b + 1) * nc)
            for c in range(nc):
                hop(b + 1, c).wait_send()

    red.finish(halo * nc, (halo + 1) * nc)
    sta.finish()
    for k in range(1, n):
        word(k, me).wait_send()
    for t in range(len(others)):
        share(t).wait_send()


def finish_kernel(n, n_seq, n_dp, halo, nc, off, n1t_hbm, w_hbm, wd_hbm, dq_ref, dk_ref, dv_ref, dh1r_ref, g_ref, hid_ref, h1_ref, x_ref, scale_ref, gain_ref, dh1_ref, gain_two_ref, group_ref, out_ref, output_ref, sums_ref, gq_ref, gk_ref, gv_ref, go_ref, own, sbuf, rbuf, osum, osend, orecv, n1t_ref, w_ref, wd_ref, dh1t, mine, given, taken, sent, came, stat, gain_s, words, sums, zsend, zrecv, keep, load_sem, s1, r1, s2, r2, s3, r3, s4, r4, s5, r5, s6, r6, s7, r7, s8, rl, rr):
    loads = [
        fetch(n1t_hbm, 0, n1t_ref, load_sem.at[0]),
        fetch(w_hbm, 0, w_ref, load_sem.at[1]),
        fetch(wd_hbm, off, wd_ref, load_sem.at[2]),
    ]
    spot, core = lax.axis_index("seq"), lax.axis_index("dp")
    me = lax.axis_index("head")
    tok, width = dq_ref.shape
    size = tok // nc
    share = mine.shape[1]
    others = [(i, j) for i in range(n_seq) for j in range(n_dp) if i or j]

    def of(i, j):
        return {"seq": lax.rem(spot + i, n_seq), "dp": lax.rem(core + j, n_dp)}

    def sends(j):
        return spot >= halo - j + 1

    def comes(j):
        return (spot + 1 < n_seq) & (spot + 1 >= halo - j + 1)

    for j in range(1, halo + 1):
        @pl.when(jnp.logical_not(comes(j)))
        def _():
            zrecv[j - 1] = jnp.zeros(zrecv.shape[1:], BF16)

    words[me] = group_ref[...]
    dh1t[...] = dh1r_ref[...].T
    greet(*group(n), *(of(i, j) for i, j in others))
    red = Reduce(n, size, me, own, sbuf, rbuf, s1, r1)
    last = Reduce(n, size, me, osum, osend, orecv, s6, r6)
    sta = Stats(n, nc, me, stat, s2, r2)

    def word(k, source):
        return push(
            words.at[source], words.at[source], s3.at[k - 1], r3.at[k - 1], head=peer_of(me, k, n)
        )

    def hop(j, c):
        rows = pl.ds(c * size, size)
        return push(
            zsend.at[j - 1, rows], zrecv.at[j - 1, rows], s5.at[j - 1, c], r5.at[j - 1, c], seq=lax.rem(spot + n_seq - 1, n_seq)
        )

    for k in range(1, n):
        word(k, me).start()
    loads[0].wait()

    def block_grads(i, c, ref):
        rows = rows_of(i * n_dp + c, share)
        ref[:, :width] = mm(n1t_ref[rows, halo * tok :], dq_ref[...], NN).astype(ref.dtype)
        ref[:, width : 2 * width] = mm(n1t_ref[rows, :], dk_ref[...], NN).astype(ref.dtype)
        ref[:, 2 * width : 3 * width] = mm(n1t_ref[rows, :], dv_ref[...], NN).astype(ref.dtype)
        ref[:, 3 * width :] = mm(dh1t[rows, :], g_ref[...], NN).astype(ref.dtype)

    def give(k, i):
        return push(
            given.at[k - 1, i], taken.at[k - 1, i], s7.at[k - 1, i], r7.at[k - 1, i], dp=lax.rem(core + k, n_dp)
        )

    for k in range(1, n_dp):

        @pl.loop(0, n_seq)
        def _(i):
            block_grads(i, lax.rem(core + k, n_dp), given.at[k - 1, i])
            give(k, i).start()

    loads[1].wait()
    pairs = [(dk_ref, 0, w_ref, width), (dv_ref, 0, w_ref, 2 * width)]
    for b in range(halo):
        @pl.when(sends(b + 1))
        def _():
            red.send(b * nc, (b + 1) * nc, pairs)

    @pl.loop(0, n_seq)
    def _(i):
        block_grads(i, core, mine.at[i])

    red.send(halo * nc, (halo + 1) * nc, [(dq_ref, halo * nc, w_ref, 0)] + pairs)
    for k in range(1, n_dp):
        for i in range(n_seq):
            give(k, i).wait_recv()

        @pl.loop(0, n_seq)
        def _(i):
            mine[i] = mine[i] + taken[k - 1, i].astype(F32)

    def right(d):
        return push(sent.at[d], came.at[d], s8.at[d], rl.at[d], seq=lax.rem(spot + 1, n_seq))

    def left(d):
        slot = jnp.where(spot - 1 == d, n_seq, d)
        return push(sent.at[d], came.at[slot], s8.at[d], rr.at[d], seq=lax.rem(spot + n_seq - 1, n_seq))

    def arrived(d, slot, sem):
        return push(sent.at[d], came.at[slot], s8.at[d], sem.at[d], seq=lax.rem(spot + 1, n_seq))

    def start_line(i):
        d = n_seq - 1 - i
        if d > 0:
            @pl.when(spot == 0)
            def _():
                if i:
                    right(d + 1).wait_send()
                sent[d] = mine[d].astype(BF16)
                right(d).start()

            @pl.when(spot == n_seq - 1)
            def _():
                if i:
                    left(i - 1).wait_send()
                sent[i] = mine[i].astype(BF16)
                left(i).start()

    def pass_line(i):
        d = n_seq - 1 - i
        if d > 0:
            @pl.when((spot > 0) & (d > spot))
            def _():
                arrived(d, d, rl).wait_recv()
                sent[d] = (mine[d] + came[d].astype(F32)).astype(BF16)
                right(d).start()

            @pl.when((spot < n_seq - 1) & (i < spot))
            def _():
                arrived(i, i, rr).wait_recv()
                sent[i] = (mine[i] + came[i].astype(F32)).astype(BF16)
                left(i).start()

    def total(b, c):
        value = red.take(b * nc + c)
        if b == 0:
            return value

        @pl.when(comes(b))
        def _():
            hop(b, c).wait_recv()

        return value + zrecv[b - 1, pl.ds(c * size, size)].astype(F32)

    def send_hop(j):
        for c in range(nc):
            @pl.when(sends(j))
            def _():
                zsend[j - 1, pl.ds(c * size, size)] = total(j - 1, c).astype(BF16)
                hop(j, c).start()

            if j > 1:
                @pl.when(jnp.logical_not(sends(j)) & comes(j - 1))
                def _():
                    hop(j - 1, c).wait_recv()

    start_line(0)
    loads[2].wait()
    last.send(0, nc, [(hid_ref, 0, wd_ref, 0)])
    for t in range(max(n_seq - 1, halo)):
        if t and t < n_seq - 1:
            start_line(t)
        if t < halo:
            send_hop(t + 1)
        if t < n_seq - 1:
            pass_line(t)

    def unit_of(rows):
        return x_ref[rows, :].astype(F32) * scale_ref[rows, :]

    def base_of(rows, back):
        return dh1_ref[rows, :] + scale_ref[rows, :] * back

    def done(c, rows, value):
        out_ref[rows, :] = value.astype(BF16)

    norm_back(nc, size, n * red.cols, functools.partial(total, halo), keep, sta, unit_of, gain_ref, base_of, gain_s, done)
    for k in range(1, n):
        word(k, peer_of(me, n - k, n)).wait_recv()
    group_sum = words[0]
    for k in range(1, n):
        group_sum = group_sum + words[k]
    place = spot * n_dp + core
    slip = sums.at[place]
    cols = gain_s.shape[1]
    slip[...] = jnp.zeros((8, cols), F32)
    slip[0:1, :] = gain_s[...]
    slip[1:2, :] = gain_two_ref[...]
    slip[2:4, : group_sum.shape[1]] = group_sum[0:2]

    def hand(t):
        i, j = others[t]
        return push(slip, slip, s4.at[t], r4.at[t], **of(i, j))

    def handed(t):
        i, j = others[t]
        back = lax.rem(spot + n_seq - i, n_seq) * n_dp + lax.rem(core + n_dp - j, n_dp)
        theirs = sums.at[back]
        return push(theirs, theirs, s4.at[t], r4.at[t], **of(i, j))

    for t in range(len(others)):
        hand(t).start()
    for c in range(nc):
        rows = rows_of(c, size)
        output_ref[rows, :] = (last.take(c) + h1_ref[rows, :]).astype(BF16)

    @pl.when(spot > 0)
    def _():
        arrived(spot, spot, rl).wait_recv()
        mine[spot] = mine[spot] + came[spot].astype(F32)

    @pl.when(spot < n_seq - 1)
    def _():
        arrived(spot, n_seq, rr).wait_recv()
        mine[spot] = mine[spot] + came[n_seq].astype(F32)

    for i, ref in enumerate((gq_ref, gk_ref, gv_ref, go_ref)):
        ref[...] = mine[spot, :, i * width : (i + 1) * width]
    for t in range(len(others)):
        handed(t).wait_recv()
    full_sum = sums[0]
    for t in range(1, n_seq * n_dp):
        full_sum = full_sum + sums[t]
    sums_ref[...] = full_sum
    for b in range(halo):
        @pl.when(sends(b + 1))
        def _():
            red.finish(b * nc, (b + 1) * nc)
            for c in range(nc):
                hop(b + 1, c).wait_send()

    red.finish(halo * nc, (halo + 1) * nc)
    last.finish(0, nc)
    sta.finish()
    for k in range(1, n):
        word(k, me).wait_send()
    for t in range(len(others)):
        hand(t).wait_send()
    for k in range(1, n_dp):
        for i in range(n_seq):
            give(k, i).wait_send()
    for d in range(n_seq):
        @pl.when((spot < d) & ((spot > 0) | (d == 1)))
        def _():
            right(d).wait_send()

        @pl.when((spot > d) & ((spot < n_seq - 1) | (d == n_seq - 2)))
        def _():
            left(d).wait_send()


def far_away(x):
    return pltpu.with_memory_space_constraint(x, pltpu.HBM)


def dma(*dims):
    return pltpu.SemaphoreType.DMA(dims)


def talk(kernel, ident, outs, scratch, flops, room, args, far=(), far_outs=()):
    return pl.pallas_call(
        kernel,
        out_shape=[
            pltpu.HBM(s, d) if i in far_outs else jax.ShapeDtypeStruct(s, d)
            for i, (s, d) in enumerate(outs)
        ],
        in_specs=[
            pl.BlockSpec(memory_space=pltpu.HBM) if i in far else whole() for i in range(len(args))
        ],
        out_specs=[
            pl.BlockSpec(memory_space=pltpu.HBM) if i in far_outs else whole()
            for i in range(len(outs))
        ],
        scratch_shapes=scratch,
        cost_estimate=pl.CostEstimate(flops=flops, bytes_accessed=40 * 2**20, transcendentals=0),
        compiler_params=pltpu.CompilerParams(
            collective_id=ident, has_side_effects=True, vmem_limit_bytes=room * 2**20
        ),
    )(*(far_away(a) if i in far else a for i, a in enumerate(args)))


def forward_kernel(base, nb_ref, lam_ref, q_ref, k_ref, v_ref, start_ref, gain_ref, o1_ref, o2_ref, lse_ref, g_ref, held, m_s, l_s, acc):
    size = q_ref.shape[0]
    qt = pl.program_id(1)
    q = q_ref[...] * 0.125
    lane = lax.broadcasted_iota(jnp.int32, q.shape, 1)
    zero = jnp.zeros_like(q)
    parts = (jnp.where(lane < HALF, q, zero), jnp.where(lane >= HALF, q, zero))
    key = lax.broadcasted_iota(jnp.int32, (size, size), 0)
    query = lax.broadcasted_iota(jnp.int32, (size, size), 1)
    start = start_ref[...]

    count = nb_ref[qt]

    def scores(d, first):
        where = base + qt - d
        k = k_ref[rows_of(where, size), :]
        allowed = key >= start - where * size
        if first:
            allowed = allowed & (key <= query)
        for m in range(2):
            s = jnp.where(allowed, mm(k, parts[m], NT), NEG_BIG)
            held[d, m] = s
            top = jnp.max(s, axis=0, keepdims=True)
            m_s[m] = top if first else jnp.maximum(m_s[m], top)

    def weights(d, _):
        for m in range(2):
            e = jnp.exp(held[d, m] - m_s[m])
            held[d, m] = e
            l_s[m] += jnp.sum(e, axis=0, keepdims=True)
        return 0

    def mix(d, first):
        v = v_ref[rows_of(base + qt - d, size), :]
        for m in range(2):
            term = mm(v, (held[d, m] * l_s[m]).astype(BF16), TN)
            if first:
                acc[m] = term
            else:
                acc[m] += term

    def each(step):
        def body(d, _):
            step(d, False)
            return 0

        step(0, True)
        lax.fori_loop(1, count, body, 0)

    each(scores)
    l_s[...] = jnp.zeros_like(l_s)
    lax.fori_loop(0, count, weights, 0)
    for m in range(2):
        lse_ref[0, m : m + 1, :] = m_s[m] + jnp.log(l_s[m])
        l_s[m] = 1.0 / l_s[m]
    each(mix)
    o1, o2 = acc[0], acc[1]
    o1_ref[...] = o1
    o2_ref[...] = o2
    diff = o1 - lam_ref[0] * o2
    scale = lax.rsqrt(jnp.mean(diff * diff, axis=0, keepdims=True) + EPS)
    g = diff * scale * gain_ref[...] * KEEP
    g_ref[...] = g.T.astype(BF16)


def backward_kernel(base, nb_ref, lam_ref, q_ref, k_ref, v_ref, start_ref, gain_ref, o1_ref, o2_ref, lse_ref, dg_ref, dq_ref, dk_ref, dv_ref, gain_grad_ref, lam_grad_ref, dq_s, dk_s, dv_s):
    size = q_ref.shape[0]
    h, qt = pl.program_id(0), pl.program_id(1)
    lam = lam_ref[0]

    @pl.when((h == 0) & (qt == 0))
    def _():
        gain_grad_ref[...] = jnp.zeros_like(gain_grad_ref)
        lam_grad_ref[...] = jnp.zeros_like(lam_grad_ref)

    @pl.when(qt == 0)
    def _():
        dk_s[...] = jnp.zeros_like(dk_s)
        dv_s[...] = jnp.zeros_like(dv_s)

    o1, o2 = o1_ref[...], o2_ref[...]
    diff = o1 - lam * o2
    scale = lax.rsqrt(jnp.mean(diff * diff, axis=0, keepdims=True) + EPS)
    unit = diff * scale
    dg = dg_ref[...].T
    gain_grad_ref[...] += jnp.sum(dg * unit, axis=1, keepdims=True) * KEEP
    du = dg * gain_ref[...] * KEEP
    do = scale * (du - unit * jnp.mean(du * unit, axis=0, keepdims=True))
    lam_grad_ref[...] -= jnp.sum(do * o2, axis=1, keepdims=True)
    grads = (do.astype(BF16), (-lam * do).astype(BF16))
    deltas = tuple(
        jnp.sum(g.astype(F32) * o, axis=0, keepdims=True) for g, o in zip(grads, (o1, o2))
    )
    q = q_ref[...] * 0.125
    lane = lax.broadcasted_iota(jnp.int32, q.shape, 1)
    zero = jnp.zeros_like(q)
    parts = (jnp.where(lane < HALF, q, zero), jnp.where(lane >= HALF, q, zero))
    key = lax.broadcasted_iota(jnp.int32, (size, size), 0)
    query = lax.broadcasted_iota(jnp.int32, (size, size), 1)
    start = start_ref[...]
    dq_s[...] = jnp.zeros_like(dq_s)

    def block(where, first):
        rows = rows_of(where, size)
        k, v = k_ref[rows, :], v_ref[rows, :]
        halves = (jnp.where(lane < HALF, k, zero), jnp.where(lane >= HALF, k, zero))
        allowed = key >= start - where * size
        if first:
            allowed = allowed & (key <= query)
        dq = dq_s[...]
        dk = dk_s[rows, :]
        dv = dv_s[rows, :]
        for m in range(2):
            s = mm(k, parts[m], NT)
            p = jnp.where(allowed, jnp.exp(s - lse_ref[0, m : m + 1, :]), 0.0)
            dp = mm(v, grads[m], NN)
            ds = (p * (dp - deltas[m])).astype(BF16)
            dq = dq + mm(halves[m], ds, TN)
            dk = dk + mm(ds, parts[m], NN)
            dv = dv + mm(p.astype(BF16), grads[m], NT)
        dq_s[...] = dq
        dk_s[rows, :] = dk
        dv_s[rows, :] = dv

    block(base + qt, True)

    def earlier(d, _):
        block(base + qt - d, False)
        return 0

    lax.fori_loop(1, nb_ref[qt], earlier, 0)
    dq_ref[...] = (dq_s[...] * 0.125).T.astype(BF16)

    @pl.when(qt == pl.num_programs(1) - 1)
    def _():
        dk_ref[...] = dk_s[...].astype(BF16)
        dv_ref[...] = dv_s[...].astype(BF16)


SMEM = pl.BlockSpec(memory_space=pltpu.SMEM)
TILE = 256


def attend(q, kv, start, nb, lam, gain_col):
    tok, width = q.shape
    heads = width // VDIM
    rows = kv.shape[0]
    size = min(TILE, tok)
    base = (rows - tok) // size
    head_block = pl.BlockSpec((VDIM, size), lambda h, t: (h, t))
    return pl.pallas_call(
        functools.partial(forward_kernel, base),
        grid=(heads, tok // size),
        out_shape=[
            jax.ShapeDtypeStruct((width, tok), F32),
            jax.ShapeDtypeStruct((width, tok), F32),
            jax.ShapeDtypeStruct((heads, 2, tok), F32),
            jax.ShapeDtypeStruct((tok, width), BF16),
        ],
        in_specs=[
            SMEM,
            SMEM,
            pl.BlockSpec((size, VDIM), lambda h, t: (t, h)),
            pl.BlockSpec((rows, VDIM), lambda h, t: (0, h)),
            pl.BlockSpec((rows, VDIM), lambda h, t: (0, heads + h)),
            pl.BlockSpec((1, size), lambda h, t: (0, t)),
            pl.BlockSpec((VDIM, 1), lambda h, t: (0, 0)),
        ],
        out_specs=[
            head_block,
            head_block,
            pl.BlockSpec((1, 2, size), lambda h, t: (h, 0, t)),
            pl.BlockSpec((size, VDIM), lambda h, t: (t, h)),
        ],
        scratch_shapes=[
            VMEM((rows // size, 2, size, size), F32),
            VMEM((2, 1, size), F32),
            VMEM((2, 1, size), F32),
            VMEM((2, VDIM, size), F32),
        ],
        cost_estimate=pl.CostEstimate(
            flops=4 * tok * rows * heads * VDIM,
            bytes_accessed=8 * tok * width + 4 * rows * width,
            transcendentals=2 * tok * rows * heads,
        ),
        compiler_params=pltpu.CompilerParams(vmem_limit_bytes=32 * 2**20),
    )(nb, lam, q, kv, kv, start, gain_col)


def attend_back(q, kv, start, nb, lam, gain_col, o1, o2, lse, dg):
    tok, width = q.shape
    heads = width // VDIM
    rows = kv.shape[0]
    size = min(TILE, tok)
    base = (rows - tok) // size
    head_block = pl.BlockSpec((VDIM, size), lambda h, t: (h, t))
    return pl.pallas_call(
        functools.partial(backward_kernel, base),
        grid=(heads, tok // size),
        out_shape=[
            jax.ShapeDtypeStruct((tok, width), BF16),
            jax.ShapeDtypeStruct((rows, width), BF16),
            jax.ShapeDtypeStruct((rows, width), BF16),
            jax.ShapeDtypeStruct((VDIM, 1), F32),
            jax.ShapeDtypeStruct((VDIM, 1), F32),
        ],
        in_specs=[
            SMEM,
            SMEM,
            pl.BlockSpec((size, VDIM), lambda h, t: (t, h)),
            pl.BlockSpec((rows, VDIM), lambda h, t: (0, h)),
            pl.BlockSpec((rows, VDIM), lambda h, t: (0, heads + h)),
            pl.BlockSpec((1, size), lambda h, t: (0, t)),
            pl.BlockSpec((VDIM, 1), lambda h, t: (0, 0)),
            head_block,
            head_block,
            pl.BlockSpec((1, 2, size), lambda h, t: (h, 0, t)),
            pl.BlockSpec((size, VDIM), lambda h, t: (t, h)),
        ],
        out_specs=[
            pl.BlockSpec((size, VDIM), lambda h, t: (t, h)),
            pl.BlockSpec((rows, VDIM), lambda h, t: (0, h)),
            pl.BlockSpec((rows, VDIM), lambda h, t: (0, h)),
            pl.BlockSpec((VDIM, 1), lambda h, t: (0, 0)),
            pl.BlockSpec((VDIM, 1), lambda h, t: (0, 0)),
        ],
        scratch_shapes=[
            VMEM((VDIM, size), F32),
            VMEM((rows, VDIM), F32),
            VMEM((rows, VDIM), F32),
        ],
        cost_estimate=pl.CostEstimate(
            flops=10 * tok * rows * heads * VDIM,
            bytes_accessed=16 * tok * width + 8 * rows * width,
            transcendentals=2 * tok * rows * heads,
        ),
        compiler_params=pltpu.CompilerParams(vmem_limit_bytes=40 * 2**20),
    )(nb, lam, q, kv, kv, start, gain_col, o1, o2, lse, dg)


CHUNKS = 2


def on_device(
    n_head,
    n_seq,
    n_dp,
    inputs,
    w_query,
    w_key,
    w_value,
    w_output,
    w_gate,
    w_up,
    w_down,
    gain_attn,
    gain_ffn,
    group_gain,
    lambda_q1,
    lambda_k1,
    lambda_q2,
    lambda_k2,
    doc_ids,
    needles,
    out_grad,
):
    x = inputs[0]
    tok, cols = x.shape
    n, nc = n_head, CHUNKS
    full = n * cols
    width = w_query.shape[1]
    hidden = w_gate.shape[1]
    me = lax.axis_index("head")
    halo = n_seq // 2

    w_attn = lax.all_gather(
        jnp.concatenate([w_query, w_key, w_value, w_output], axis=1),
        ("seq", "dp"),
        axis=0,
        tiled=True,
    )
    w_ffn = lax.all_gather(
        jnp.concatenate([w_gate, w_up, w_down], axis=1), ("seq", "dp"), axis=0, tiled=True
    )

    weight = jnp.where(needles[0] == 1, 1.0, 0.1).astype(F32)
    dy = out_grad[0].astype(F32) * weight[:, None]
    gain_one = gain_attn[None, :]
    gain_two = gain_ffn[None, :]
    gain_one_cols = lax.dynamic_slice_in_dim(gain_one, me * cols, cols, 1)
    gain_two_cols = lax.dynamic_slice_in_dim(gain_two, me * cols, cols, 1)
    lam = jnp.exp(jnp.sum(lambda_q1 * lambda_k1)) - jnp.exp(jnp.sum(lambda_q2 * lambda_k2))
    lam = (lam + LAMBDA_INIT)[None]
    gain_col = group_gain[:, None]

    docs = jnp.broadcast_to(doc_ids + 1, (8, tok))
    n1, scale_one, dyr, window, n1t = talk(
        functools.partial(enter_kernel, n, n_seq, halo),
        0,
        [
            (((halo + 1) * tok, full), BF16),
            ((tok, 1), F32),
            ((tok, full), BF16),
            ((8, (halo + 1) * tok), jnp.int32),
            ((full, (halo + 1) * tok), BF16),
        ],
        [
            VMEM((n, (halo + 1) * tok, cols), BF16),
            VMEM((n, tok, cols), BF16),
            VMEM((halo + 1, 8, tok), jnp.int32),
            VMEM((full, (halo + 1) * tok), BF16),
            pltpu.SemaphoreType.DMA,
        ]
        + [dma(n - 1, halo + 1)] * 2
        + [dma(n - 1, 1)] * 2
        + [dma(max(halo, 1))] * 4,
        tok * full * 8,
        28 + 8 * halo,
        (x, dy.astype(BF16), gain_one, docs),
        far_outs=(4,),
    )
    start = jnp.sum((window[0][None, :] < docs[0][:, None]).astype(jnp.int32), axis=1)
    size = min(TILE, tok)
    base = halo * tok // size
    first = start[::size]
    nb = base + jnp.arange(tok // size, dtype=jnp.int32) - first // size + 1
    start = start[None, :]

    q = jnp.dot(n1[halo * tok :], w_attn[:, :width], preferred_element_type=F32).astype(BF16)
    kv = jnp.dot(n1, w_attn[:, width : 3 * width], preferred_element_type=F32).astype(BF16)
    o1, o2, lse, grouped = attend(q, kv, start, nb, lam, gain_col)

    exchange = [VMEM((tok, cols), F32), VMEM((n - 1, tok, cols), BF16), VMEM((n - 1, tok, cols), BF16)]
    h1, n2, scale_two = talk(
        functools.partial(middle_kernel, n, nc, 3 * width),
        1,
        [((tok, cols), F32), ((tok, full), BF16), ((tok, 1), F32)],
        exchange
        + [VMEM((full, width), BF16), VMEM((n, tok, cols), BF16), pltpu.SemaphoreType.DMA]
        + [dma(n - 1, nc)] * 4,
        2 * tok * full * width,
        24,
        (grouped, w_attn, x, gain_two),
        far=(1,),
    )
    tile = min(TILE, hidden)
    inner, d_gate, d_up, d_wffn = ffn(n2, dyr, w_ffn, tile)
    g_ffn = lax.psum_scatter(d_wffn, ("seq", "dp"), scatter_dimension=0, tiled=True)

    stat = VMEM((n, nc, 8, tok // nc), F32)
    dh1, dh1r, gain_two_part = talk(
        functools.partial(back_kernel, n, nc, 0),
        2,
        [((tok, cols), F32), ((tok, full), BF16), ((1, cols), F32)],
        exchange
        + [VMEM((full, 2 * hidden), BF16), stat, VMEM((n, tok, cols), BF16), pltpu.SemaphoreType.DMA]
        + [dma(n - 1, nc)] * 6,
        4 * tok * full * hidden,
        28,
        (d_gate, d_up, w_ffn, h1, scale_two, gain_two_cols, dy),
        far=(2,),
    )
    dg = jnp.dot(dh1r, w_attn[:, 3 * width :], preferred_element_type=F32)
    dq, dk, dv, group_part, lam_part = attend_back(
        q, kv, start, nb, lam, gain_col, o1, o2, lse, dg
    )
    group_words = jnp.concatenate(
        [
            group_part.T,
            jnp.broadcast_to(jnp.sum(lam_part), (1, VDIM)),
            jnp.zeros((6, VDIM), F32),
        ]
    )
    others = n_seq * n_dp - 1
    span = (halo + 1) * tok
    if halo <= 2:
        rows = w_query.shape[0]
        line = (n_seq, rows, 4 * width)
        input_grad, output, sums, g_query, g_key, g_value, g_output = talk(
            functools.partial(finish_kernel, n, n_seq, n_dp, halo, nc, 2 * hidden),
            3,
            [((tok, cols), BF16), ((tok, cols), BF16), ((8, cols), F32)] + [((rows, width), F32)] * 4,
            [
                VMEM((span, cols), F32),
                VMEM((n - 1, span, cols), BF16),
                VMEM((n - 1, span, cols), BF16),
            ]
            + exchange
            + [
                VMEM((full, span), BF16),
                VMEM((full, 3 * width), BF16),
                VMEM((full, hidden), BF16),
                VMEM((full, tok), BF16),
                VMEM(line, F32),
                VMEM((max(n_dp - 1, 1),) + line, BF16),
                VMEM((max(n_dp - 1, 1),) + line, BF16),
                VMEM(line, BF16),
                VMEM((n_seq + 1, rows, 4 * width), BF16),
                stat,
                VMEM((1, cols), F32),
                VMEM((n, 8, VDIM), F32),
                VMEM((others + 1, 8, cols), F32),
                VMEM((max(halo, 1), tok, cols), BF16),
                VMEM((max(halo, 1), tok, cols), BF16),
                VMEM((tok, cols), F32),
                dma(3),
            ]
            + [dma(n - 1, (halo + 1) * nc)] * 2
            + [dma(n - 1, nc)] * 2
            + [dma(n - 1)] * 2
            + [dma(max(others, 1))] * 2
            + [dma(max(halo, 1), nc)] * 2
            + [dma(n - 1, nc)] * 2
            + [dma(max(n_dp - 1, 1), n_seq)] * 2
            + [dma(n_seq)] * 3,
            6 * tok * full * width * (halo + 1) + 2 * tok * full * hidden,
            60,
            (n1t, w_attn, w_ffn, dq, dk, dv, dh1r, grouped, inner, h1, x, scale_one, gain_one_cols, dh1, gain_two_part, group_words),
            far=(0, 1, 2),
        )
    else:
        d_wattn = projection_grads(halo, n1t, dq, dk, dv, dh1r, grouped)
        inner, d_wattn = lax.optimization_barrier((inner, d_wattn))
        (output,) = talk(
            functools.partial(output_kernel, n, nc, 2 * hidden),
            4,
            [((tok, cols), BF16)],
            exchange + [VMEM((full, hidden), BF16), pltpu.SemaphoreType.DMA] + [dma(n - 1, nc)] * 2,
            2 * tok * full * hidden,
            20,
            (inner, w_ffn, h1),
            far=(1,),
        )
        d_wattn, g_ffn, output = lax.optimization_barrier((d_wattn, g_ffn, output))
        g_attn = lax.psum_scatter(d_wattn, ("seq", "dp"), scatter_dimension=0, tiled=True).astype(F32)
        input_grad, sums = talk(
            functools.partial(leave_kernel, n, n_seq, n_dp, halo, nc),
            3,
            [((tok, cols), BF16), ((8, cols), F32)],
            [
                VMEM((span, cols), F32),
                VMEM((n - 1, span, cols), BF16),
                VMEM((n - 1, span, cols), BF16),
                VMEM((full, 3 * width), BF16),
                stat,
                VMEM((1, cols), F32),
                VMEM((n, 8, VDIM), F32),
                VMEM((others + 1, 8, cols), F32),
                VMEM((max(halo, 1), tok, cols), BF16),
                VMEM((max(halo, 1), tok, cols), BF16),
                VMEM((tok, cols), F32),
                pltpu.SemaphoreType.DMA,
            ]
            + [dma(n - 1, (halo + 1) * nc)] * 2
            + [dma(n - 1, nc)] * 2
            + [dma(n - 1)] * 2
            + [dma(max(others, 1))] * 2
            + [dma(max(halo, 1), nc)] * 2,
            6 * tok * full * width * (halo + 1),
            26 + 5 * halo,
            (dq, dk, dv, w_attn, x, scale_one, gain_one_cols, dh1, gain_two_part, group_words),
            far=(3,),
        )
        g_query, g_key, g_value, g_output = (
            g_attn[:, i * width : (i + 1) * width] for i in range(4)
        )
    g_ffn = g_ffn.astype(F32)
    share = cols // (n_seq * n_dp)
    place = lax.axis_index("seq") * n_dp + lax.axis_index("dp")
    gains = lax.dynamic_slice_in_dim(sums[:2], place * share, share, 1)
    return (
        output[None],
        input_grad[None],
        gains[0],
        gains[1],
        sums[2, :VDIM],
        sums[3, :1],
        g_query,
        g_key,
        g_value,
        g_output,
        g_ffn[:, :hidden],
        g_ffn[:, hidden : 2 * hidden],
        g_ffn[:, 2 * hidden :],
    )


def solution(mesh):
    act = P("dp", "seq", "head")
    mat = P(("seq", "dp"), "head")
    vec = P(("head", "seq", "dp"))
    return jax.shard_map(
        functools.partial(on_device, mesh.shape["head"], mesh.shape["seq"], mesh.shape["dp"]),
        mesh=mesh,
        in_specs=(act,) + (mat,) * 7 + (P(),) * 7 + (P("dp", "seq"),) * 2 + (act,),
        out_specs=(act, act, vec, vec, P(), P()) + (mat,) * 7,
        check_vma=False,
    )
```

```python
import functools
import math

import jax
import jax.numpy as jnp
from jax import lax
from jax.experimental import pallas as pl
from jax.experimental.pallas import tpu as pltpu
from jax.sharding import PartitionSpec as P

HALF = 64
VDIM = 128
EPS = 1e-05
LAMBDA_INIT = 0.8 - 0.6 * math.exp(-0.3)
KEEP = 1.0 - LAMBDA_INIT
NEG_BIG = -1e30
MESH = pl.DeviceIdType.MESH
VMEM = pltpu.VMEM
F32 = jnp.float32
BF16 = jnp.bfloat16
NN = (((1,), (0,)), ((), ()))
NT = (((1,), (1,)), ((), ()))
TN = (((0,), (0,)), ((), ()))


def mm(a, b, dims):
    return lax.dot_general(a, b, dims, preferred_element_type=F32)


def whole():
    return pl.BlockSpec(memory_space=VMEM)


def peer_of(me, k, n):
    return lax.rem(me + k, n)


def greet(*peers):
    barrier = pltpu.get_barrier_semaphore()
    for peer in peers:
        pl.semaphore_signal(barrier, 1, device_id=peer, device_id_type=MESH)
    pl.semaphore_wait(barrier, len(peers))


def along(axis, size, steps):
    spot = lax.axis_index(axis)
    return [{axis: lax.rem(spot + k, size)} for k in steps]


def group(n):
    return along("head", n, range(1, n))


def push(src, dst, send, recv, **peer):
    return pltpu.make_async_remote_copy(
        src_ref=src,
        dst_ref=dst,
        send_sem=send,
        recv_sem=recv,
        device_id=peer,
        device_id_type=MESH,
    )


def rows_of(c, size):
    return pl.ds(pl.multiple_of(c * size, size), size)


def fetch(w_hbm, off, w_ref, sem):
    copy = pltpu.make_async_copy(w_hbm.at[:, off : off + w_ref.shape[1]], w_ref, sem)
    copy.start()
    return copy


class Reduce:
    def __init__(self, n, size, me, own_ref, sbuf, rbuf, ssem, rsem):
        self.n, self.size, self.me = n, size, me
        self.own_ref, self.sbuf, self.rbuf, self.ssem, self.rsem = own_ref, sbuf, rbuf, ssem, rsem
        self.cols = own_ref.shape[1]

    def copy(self, k, c):
        rows = rows_of(c, self.size)
        return push(
            self.sbuf.at[k - 1, rows],
            self.rbuf.at[k - 1, rows],
            self.ssem.at[k - 1, c],
            self.rsem.at[k - 1, c],
            head=peer_of(self.me, k, self.n),
        )

    def send(self, first, last, pairs):
        n = self.n

        def step(t, _):
            turn = t // n
            c = first + turn
            k = t - turn * n + 1
            rows = rows_of(c, self.size)
            peer = peer_of(self.me, k, n)
            part = None
            for a_ref, behind, w_ref, off in pairs:
                span = slice(off, off + a_ref.shape[1])
                term = mm(
                    a_ref[rows_of(c - behind, self.size), :],
                    w_ref[rows_of(peer, self.cols), span],
                    NT,
                )
                part = term if part is None else part + term

            @pl.when(k < n)
            def _():
                self.sbuf[k - 1, rows] = part.astype(BF16)
                self.copy(k, c).start()

            @pl.when(k == n)
            def _():
                self.own_ref[rows, :] = part

            return 0

        lax.fori_loop(0, (last - first) * n, step, 0)

    def relay(self, first, last):
        pass

    def take(self, c):
        rows = rows_of(c, self.size)
        total = self.own_ref[rows, :]
        for k in range(1, self.n):
            self.copy(k, c).wait_recv()
        for k in range(1, self.n):
            total = total + self.rbuf[k - 1, rows].astype(F32)
        return total

    def finish(self, first, last):
        for c in range(first, last):
            for k in range(1, self.n):
                self.copy(k, c).wait_send()


class Gather:
    def __init__(self, n, nc, me, buf, ssem, rsem):
        self.n, self.nc, self.me = n, nc, me
        self.buf, self.ssem, self.rsem = buf, ssem, rsem
        self.size = buf.shape[1] // nc

    def copy(self, k, c, source):
        rows = rows_of(c, self.size)
        return push(
            self.buf.at[source, rows],
            self.buf.at[source, rows],
            self.ssem.at[k - 1, c],
            self.rsem.at[k - 1, c],
            head=peer_of(self.me, k, self.n),
        )

    def send(self, c, value=None):
        if value is not None:
            self.buf[self.me, rows_of(c, self.size)] = value
        for k in range(1, self.n):
            self.copy(k, c, self.me).start()

    def relay(self, c):
        pass

    def take(self, c):
        for k in range(1, self.n):
            self.copy(k, c, peer_of(self.me, self.n - k, self.n)).wait_recv()

    def finish(self, only=None):
        for c in range(self.nc) if only is None else (only,):
            for k in range(1, self.n):
                self.copy(k, c, self.me).wait_send()


def square(me):
    return me + 1 - 2 * lax.rem(me, 2), lax.rem(me + 2, 4), 3 - me


class SquareReduce(Reduce):
    def copy(self, k, c, odd):
        rows = rows_of(c, self.size)
        near, far, _ = square(self.me)
        return push(
            self.sbuf.at[k - 1, rows],
            self.rbuf.at[k - 1, rows],
            self.ssem.at[k - 1, c],
            self.rsem.at[k - 1, c],
            head=far if (k == 2) != odd else near,
        )

    def send(self, first, last, pairs):
        size = self.size
        near, far, across = square(self.me)

        def step(turn, _):
            t = turn // 4
            k = turn - 4 * t
            two = rows_of(t, 2 * size)
            even, odd = rows_of(2 * t, size), rows_of(2 * t + 1, size)
            owner = jnp.where(k == 0, across, jnp.where(k == 1, near, jnp.where(k == 2, far, self.me)))
            part = None
            for a_ref, behind, w_ref, off in pairs:
                span = slice(off, off + a_ref.shape[1])
                term = mm(
                    a_ref[rows_of(t - behind // 2, 2 * size), :],
                    w_ref[rows_of(owner, self.cols), span],
                    NT,
                )
                part = term if part is None else part + term
            self.own_ref[two, :] = part

            @pl.when(k == 0)
            def _():
                self.sbuf[2, two] = part.astype(BF16)
                self.copy(3, 2 * t, False).start()
                self.copy(3, 2 * t + 1, True).start()

            @pl.when(k == 1)
            def _():
                self.sbuf[0, even] = part[:size].astype(BF16)
                self.sbuf[1, odd] = part[size:].astype(BF16)
                self.copy(1, 2 * t, False).start()

            @pl.when(k == 2)
            def _():
                self.sbuf[1, even] = part[:size].astype(BF16)
                self.sbuf[0, odd] = part[size:].astype(BF16)
                self.copy(1, 2 * t + 1, True).start()

            return 0

        lax.fori_loop(2 * first, 2 * last, step, 0)

    def relay(self, first, last):
        for c in range(first, last):
            rows = rows_of(c, self.size)
            odd = c % 2 == 1
            self.copy(3, c, odd).wait_recv()
            both = self.sbuf[1, rows].astype(F32) + self.rbuf[2, rows].astype(F32)
            self.sbuf[1, rows] = both.astype(BF16)
            self.copy(2, c, odd).start()

    def take(self, c):
        rows = rows_of(c, self.size)
        for k in (1, 2):
            self.copy(k, c, c % 2 == 1).wait_recv()
        return self.own_ref[rows, :] + self.rbuf[0, rows].astype(F32) + self.rbuf[1, rows].astype(F32)

    def finish(self, first, last):
        for c in range(first, last):
            for k in range(1, self.n):
                self.copy(k, c, c % 2 == 1).wait_send()


class SquareGather(Gather):
    def own(self, k, c):
        near, far, _ = square(self.me)
        rows = rows_of(c, self.size)
        return push(
            self.buf.at[self.me, rows],
            self.buf.at[self.me, rows],
            self.ssem.at[k - 1, c],
            self.rsem.at[k - 1, c],
            head=(near, far)[k - 1],
        )

    def came(self, k, c):
        source = square(self.me)[k - 1]
        rows = rows_of(c, self.size)
        return push(
            self.buf.at[source, rows],
            self.buf.at[source, rows],
            self.ssem.at[k - 1, c],
            self.rsem.at[k - 1, c],
            head=square(self.me)[0],
        )

    def passed(self, c):
        near, far, _ = square(self.me)
        source, to = (near, far) if c % 2 else (far, near)
        rows = rows_of(c, self.size)
        return push(
            self.buf.at[source, rows],
            self.buf.at[source, rows],
            self.ssem.at[2, c],
            self.rsem.at[2, c],
            head=to,
        )

    def send(self, c, value=None):
        if value is not None:
            self.buf[self.me, rows_of(c, self.size)] = value
        for k in (1, 2):
            self.own(k, c).start()

    def relay(self, c):
        self.came(1 if c % 2 else 2, c).wait_recv()
        self.passed(c).start()

    def take(self, c):
        self.came(2 if c % 2 else 1, c).wait_recv()
        self.came(3, c).wait_recv()

    def finish(self, only=None):
        for c in range(self.nc) if only is None else (only,):
            for k in (1, 2):
                self.own(k, c).wait_send()
            self.passed(c).wait_send()


def reducer(n, *args):
    return (SquareReduce if n == 4 else Reduce)(n, *args)


def gatherer(n, *args):
    return (SquareGather if n == 4 else Gather)(n, *args)


def norm_rows(n, buf, rows, gain_ref, out_ref, scale_ref=None, scale_rows=None):
    cols = buf.shape[2]
    total = None
    for s in range(n):
        piece = buf[s, rows].astype(F32)
        part = jnp.sum(piece * piece, axis=1, keepdims=True)
        total = part if total is None else total + part
    scale = lax.rsqrt(total / (n * cols) + EPS)
    if scale_ref is not None:
        scale_ref[rows if scale_rows is None else scale_rows, :] = scale
    for s in range(n):
        span = slice(s * cols, (s + 1) * cols)
        piece = buf[s, rows].astype(F32)
        out_ref[rows, span] = (piece * scale * gain_ref[:, span]).astype(BF16)


def spread_rows(n, buf, rows, out_ref):
    cols = buf.shape[2]
    for s in range(n):
        out_ref[rows, s * cols : (s + 1) * cols] = buf[s, rows]


def enter_kernel(n, n_seq, halo, x_ref, dy_ref, gain_ref, docs_ref, n1_ref, scale_ref, dyr_ref, window_ref, n1t_hbm, xall, dall, docs, n1t_ref, ts, xs, xr, ds, dr, hs, hr, ks, kr):
    tok = x_ref.shape[0]
    spot = lax.axis_index("seq")
    me = lax.axis_index("head")
    more = spot + 1 < n_seq
    for k in range(1, halo + 1):
        @pl.when(spot < k)
        def _():
            docs[halo - k] = jnp.zeros_like(docs_ref)

    docs[halo] = docs_ref[...]
    xall[me, halo * tok :] = x_ref[...]
    greet(*group(n), *along("seq", n_seq, range(1, n_seq)))
    xg = gatherer(n, 2 * (halo + 1), me, xall, xs, xr)
    dg = gatherer(n, 2, me, dall, ds, dr)

    def word(k):
        return push(
            docs.at[halo], docs.at[halo - k], ks.at[k - 1], kr.at[k - 1], seq=lax.rem(spot + k, n_seq)
        )

    def hop(j):
        here = pl.ds((halo - j + 1) * tok, tok)
        there = pl.ds((halo - j) * tok, tok)
        return push(
            xall.at[me, here], xall.at[me, there], hs.at[j - 1], hr.at[j - 1], seq=lax.rem(spot + 1, n_seq)
        )

    size = min(64, tok)
    per = tok // size

    def block_send(b):
        for c in (2 * b, 2 * b + 1):
            xg.send(c)

    def block_take(b):
        for c in (2 * b, 2 * b + 1):
            xg.relay(c)
        for c in (2 * b, 2 * b + 1):
            xg.take(c)
        own = b == halo

        @pl.loop(0, per)
        def _(i):
            rows = rows_of(b * per + i, size)
            if own:
                norm_rows(n, xall, rows, gain_ref, n1_ref, scale_ref, rows_of(i, size))
            else:
                norm_rows(n, xall, rows, gain_ref, n1_ref)

        rows = slice(b * tok, (b + 1) * tok)
        n1t_ref[:, rows] = n1_ref[rows, :].T

    if halo:
        @pl.when(more)
        def _():
            hop(1).start()

    block_send(halo)
    for k in range(1, halo + 1):
        @pl.when(spot + k < n_seq)
        def _():
            word(k).start()

    for j in range(1, halo + 1):
        @pl.when(spot >= j)
        def _():
            hop(j).wait_recv()

        if j < halo:
            @pl.when((spot >= j) & more)
            def _():
                hop(j + 1).start()

        @pl.when(spot >= j)
        def _():
            block_send(halo - j)

        if j == 1:
            block_take(halo)
        else:
            @pl.when(spot >= j - 1)
            def _():
                block_take(halo - j + 1)

    if not halo:
        block_take(halo)
    dg.send(0, dy_ref[: tok // 2, :])
    dg.send(1, dy_ref[tok // 2 :, :])
    if halo:
        @pl.when(spot >= halo)
        def _():
            block_take(0)

    for j in range(1, halo + 1):
        @pl.when(spot < j)
        def _():
            rows = slice((halo - j) * tok, (halo - j + 1) * tok)
            n1_ref[rows, :] = jnp.zeros((tok, n1_ref.shape[1]), BF16)
            n1t_ref[:, rows] = jnp.zeros((n1_ref.shape[1], tok), BF16)

    leave = pltpu.make_async_copy(n1t_ref, n1t_hbm, ts)
    leave.start()
    for k in range(1, halo + 1):
        @pl.when(spot >= k)
        def _():
            word(k).wait_recv()

    for k in range(halo + 1):
        window_ref[:, k * tok : (k + 1) * tok] = docs[k]
    for c in range(2):
        dg.relay(c)
    for c in range(2):
        dg.take(c)

    @pl.loop(0, per)
    def _(i):
        spread_rows(n, dall, rows_of(i, size), dyr_ref)

    for b in range(halo + 1):
        @pl.when(spot >= halo - b)
        def _():
            xg.finish(2 * b)
            xg.finish(2 * b + 1)

    for j in range(1, halo + 1):
        @pl.when((spot >= j - 1) & more)
        def _():
            hop(j).wait_send()

        @pl.when(spot + j < n_seq)
        def _():
            word(j).wait_send()

    dg.finish()
    leave.wait()


def projection_kernel(halo, n1t_ref, dq_ref, dk_ref, dv_ref, dh1r_ref, g_ref, dw_hbm, dh1t, held, sems):
    full, width = n1t_ref.shape[0], dq_ref.shape[1]
    tok = dq_ref.shape[0]
    size = min(256, full)

    def leave(i):
        return pltpu.make_async_copy(held.at[i], dw_hbm.at[:, i * width : (i + 1) * width], sems.at[i])

    def fill(i, left, right):
        @pl.loop(0, full // size)
        def _(t):
            rows = rows_of(t, size)
            held[i, rows] = mm(left[rows, :], right[...], NN).astype(BF16)

        leave(i).start()

    fill(0, n1t_ref.at[:, halo * tok :], dq_ref)
    fill(1, n1t_ref, dk_ref)
    fill(2, n1t_ref, dv_ref)
    dh1t[...] = dh1r_ref[...].T
    fill(3, dh1t, g_ref)
    for i in range(4):
        leave(i).wait()


def projection_grads(halo, n1t, dq, dk, dv, dh1r, g):
    full, (tok, width) = n1t.shape[0], dq.shape
    args = (n1t, dq, dk, dv, dh1r, g)
    return pl.pallas_call(
        functools.partial(projection_kernel, halo),
        out_shape=pltpu.HBM((full, 4 * width), BF16),
        in_specs=[whole()] * len(args),
        out_specs=pl.BlockSpec(memory_space=pltpu.HBM),
        scratch_shapes=[VMEM((full, tok), BF16), VMEM((4, full, width), BF16), dma(4)],
        cost_estimate=pl.CostEstimate(
            flops=4 * full * width * (n1t.shape[1] + tok),
            bytes_accessed=2 * full * (n1t.shape[1] + 4 * width),
            transcendentals=0,
        ),
        compiler_params=pltpu.CompilerParams(vmem_limit_bytes=40 * 2**20),
    )(*args)


def ffn_kernel(n2_ref, dy_ref, wg_ref, wu_ref, wd_ref, hid_ref, dgate_ref, dup_ref, dw_hbm, n2t, dyt, held, sems):
    j, steps = pl.program_id(0), pl.num_programs(0)

    @pl.when(j == 0)
    def _():
        n2t[...] = n2_ref[...].T
        dyt[...] = dy_ref[...].T

    size = wg_ref.shape[1]
    slot = lax.rem(j, 2)

    def leave(i, step, slot):
        start = pl.multiple_of((i * steps + step) * size, size)
        return pltpu.make_async_copy(held.at[slot, i], dw_hbm.at[:, pl.ds(start, size)], sems.at[slot, i])

    gate = mm(n2_ref[...], wg_ref[...], NN)
    upper = mm(n2_ref[...], wu_ref[...], NN)
    sigma = lax.logistic(gate)
    act = gate * sigma
    hid_ref[...] = (act * upper).astype(BF16)
    d_hid = mm(dy_ref[...], wd_ref[...], NN)
    dup_ref[...] = (d_hid * act).astype(BF16)
    dgate_ref[...] = (d_hid * upper * sigma * (1.0 + gate * (1.0 - sigma))).astype(BF16)

    @pl.when(j >= 2)
    def _():
        for i in range(3):
            leave(i, j - 2, slot).wait()

    for i, (left, right) in enumerate(((n2t, dgate_ref), (n2t, dup_ref), (dyt, hid_ref))):
        held[slot, i] = mm(left[...], right[...], NN).astype(BF16)
        leave(i, j, slot).start()

    @pl.when(j == steps - 1)
    def _():
        for i in range(3):
            leave(i, j, slot).wait()

        @pl.when(j >= 1)
        def _():
            for i in range(3):
                leave(i, j - 1, 1 - slot).wait()


def ffn(n2, dyr, w, tile):
    tok, full = n2.shape
    hidden = w.shape[1] // 3
    steps = hidden // tile
    act = pl.BlockSpec((tok, full), lambda j: (0, 0))
    part = pl.BlockSpec((tok, tile), lambda j: (0, j))
    return pl.pallas_call(
        ffn_kernel,
        grid=(steps,),
        out_shape=[pltpu.HBM((tok, hidden), BF16)] * 3
        + [pltpu.HBM((full, 3 * hidden), BF16)],
        in_specs=[act, act]
        + [pl.BlockSpec((full, tile), functools.partial(lambda i, j: (0, i * steps + j), i)) for i in range(3)],
        out_specs=[part] * 3 + [pl.BlockSpec(memory_space=pltpu.HBM)],
        scratch_shapes=[
            VMEM((full, tok), BF16),
            VMEM((full, tok), BF16),
            VMEM((2, 3, full, tile), BF16),
            dma(2, 3),
        ],
        cost_estimate=pl.CostEstimate(
            flops=12 * tok * full * hidden,
            bytes_accessed=12 * full * hidden,
            transcendentals=tok * hidden,
        ),
        compiler_params=pltpu.CompilerParams(vmem_limit_bytes=24 * 2**20),
    )(far_away(n2), far_away(dyr), *(far_away(w),) * 3)


def middle_kernel(n, nc, off, g_ref, w_hbm, x_ref, gain_ref, h1_ref, n2_ref, scale_ref, own, sbuf, rbuf, w_ref, hall, ws, s1, r1, s2, r2):
    load = fetch(w_hbm, off, w_ref, ws)
    greet(*group(n))
    me = lax.axis_index("head")
    red = reducer(n, own.shape[0] // nc, me, own, sbuf, rbuf, s1, r1)
    gat = gatherer(n, nc, me, hall, s2, r2)
    load.wait()
    red.send(0, nc, [(g_ref, 0, w_ref, 0)])
    red.relay(0, nc)
    for c in range(nc):
        rows = rows_of(c, red.size)
        h1 = red.take(c) + x_ref[rows, :].astype(F32)
        h1_ref[rows, :] = h1
        gat.send(c, h1.astype(BF16))
    size = min(64, red.size)
    for c in range(nc):
        gat.relay(c)
    for c in range(nc):
        gat.take(c)

        @pl.loop(0, red.size // size)
        def _(i):
            norm_rows(n, hall, pl.ds(pl.multiple_of(c * red.size + i * size, size), size), gain_ref, n2_ref, scale_ref)

    red.finish(0, nc)
    gat.finish()


class Stats:
    def __init__(self, n, nc, me, buf, ssem, rsem):
        self.n, self.nc, self.me = n, nc, me
        self.buf, self.ssem, self.rsem = buf, ssem, rsem

    def copy(self, k, c, source):
        return push(
            self.buf.at[source, c],
            self.buf.at[source, c],
            self.ssem.at[k - 1, c],
            self.rsem.at[k - 1, c],
            head=peer_of(self.me, k, self.n),
        )

    def send(self, c, value):
        size, cols = value.shape
        part = value[:, :128]
        for j in range(1, cols // 128):
            part = part + value[:, j * 128 : (j + 1) * 128]
        line = jnp.sum(part.T, axis=0, keepdims=True)
        self.buf[self.me, c] = jnp.broadcast_to(line, (8, size))
        for k in range(1, self.n):
            self.copy(k, c, self.me).start()

    def take(self, c):
        for k in range(1, self.n):
            self.copy(k, c, peer_of(self.me, self.n - k, self.n)).wait_recv()
        total = self.buf[0, c]
        for s in range(1, self.n):
            total = total + self.buf[s, c]
        size = total.shape[1]
        tall = jnp.broadcast_to(total[:1, :], (128, size))
        return tall.T[:, :1]

    def finish(self):
        for c in range(self.nc):
            for k in range(1, self.n):
                self.copy(k, c, self.me).wait_send()


def norm_back(nc, size, width, grad_of, keep, sta, unit_of, gain_ref, base_of, gain_grad_ref, done):
    for c in range(nc):
        rows = rows_of(c, size)
        grad = grad_of(c)
        keep[rows, :] = grad
        unit = unit_of(rows)
        part = jnp.sum(grad * unit, axis=0, keepdims=True)
        if c == 0:
            gain_grad_ref[...] = part
        else:
            gain_grad_ref[...] += part
        sta.send(c, grad * gain_ref[...] * unit)
    for c in range(nc):
        rows = rows_of(c, size)
        dots = sta.take(c) / width
        scaled = keep[rows, :] * gain_ref[...]
        done(c, rows, base_of(rows, scaled - unit_of(rows) * dots))


def back_kernel(n, nc, off, down, dgate_ref, dup_ref, hid_ref, w_hbm, h1_ref, scale_ref, gain_ref, dy_ref, dh1_ref, dh1r_ref, gain_grad_ref, output_ref, own, sbuf, rbuf, osum, osend, orecv, w_ref, wd_ref, stat, dall, ws, wds, s1, r1, s2, r2, s3, r3, s4, r4):
    load_down = fetch(w_hbm, down, wd_ref, wds)
    load = fetch(w_hbm, off, w_ref, ws)
    greet(*group(n))
    me = lax.axis_index("head")
    pairs = [(dgate_ref, 0, w_ref, 0), (dup_ref, 0, w_ref, dgate_ref.shape[1])]
    size = own.shape[0] // nc
    red = reducer(n, size, me, own, sbuf, rbuf, s1, r1)
    sta = Stats(n, nc, me, stat, s2, r2)
    last = reducer(n, size, me, osum, osend, orecv, s4, r4)
    load.wait()
    gat = gatherer(n, nc, me, dall, s3, r3)
    red.send(0, nc, pairs)
    red.relay(0, nc)

    def unit_of(rows):
        return h1_ref[rows, :].astype(BF16).astype(F32) * scale_ref[rows, :]

    def base_of(rows, back):
        return dy_ref[rows, :] + scale_ref[rows, :] * back

    def done(c, rows, value):
        dh1_ref[rows, :] = value
        gat.send(c, value.astype(BF16))

    norm_back(nc, size, n * red.cols, red.take, own, sta, unit_of, gain_ref, base_of, gain_grad_ref, done)
    for c in range(nc):
        gat.relay(c)
    load_down.wait()
    last.send(0, nc, [(hid_ref, 0, wd_ref, 0)])
    for c in range(nc):
        gat.take(c)
        spread_rows(n, dall, rows_of(c, red.size), dh1r_ref)
    last.relay(0, nc)
    for c in range(nc):
        rows = rows_of(c, size)
        output_ref[rows, :] = (last.take(c) + h1_ref[rows, :]).astype(BF16)
    last.finish(0, nc)
    red.finish(0, nc)
    sta.finish()
    gat.finish()


def leave_kernel(n, n_seq, n_dp, halo, nc, dq_ref, dk_ref, dv_ref, w_hbm, x_ref, scale_ref, gain_ref, dh1_ref, gain_two_ref, group_ref, out_ref, sums_ref, own, sbuf, rbuf, w_ref, stat, gain_s, words, sums, zsend, zrecv, keep, ws, s1, r1, s2, r2, s3, r3, s4, r4, s5, r5):
    load = fetch(w_hbm, 0, w_ref, ws)
    spot, core = lax.axis_index("seq"), lax.axis_index("dp")
    others = [(i, j) for i in range(n_seq) for j in range(n_dp) if i or j]

    def of(i, j):
        return {"seq": lax.rem(spot + i, n_seq), "dp": lax.rem(core + j, n_dp)}

    def sends(j):
        return spot >= halo - j + 1

    def comes(j):
        return (spot + 1 < n_seq) & (spot + 1 >= halo - j + 1)

    for j in range(1, halo + 1):
        @pl.when(jnp.logical_not(comes(j)))
        def _():
            zrecv[j - 1] = jnp.zeros(zrecv.shape[1:], BF16)

    me = lax.axis_index("head")
    words[me] = group_ref[...]
    greet(*group(n), *(of(i, j) for i, j in others))
    tok, width = dq_ref.shape
    size = tok // nc
    red = reducer(n, size, me, own, sbuf, rbuf, s1, r1)
    sta = Stats(n, nc, me, stat, s2, r2)

    def word(k, source):
        return push(
            words.at[source], words.at[source], s3.at[k - 1], r3.at[k - 1], head=peer_of(me, k, n)
        )

    def hop(j, c):
        rows = pl.ds(c * size, size)
        return push(
            zsend.at[j - 1, rows], zrecv.at[j - 1, rows], s5.at[j - 1, c], r5.at[j - 1, c], seq=lax.rem(spot + n_seq - 1, n_seq)
        )

    for k in range(1, n):
        word(k, me).start()
    load.wait()
    pairs = [(dk_ref, 0, w_ref, width), (dv_ref, 0, w_ref, 2 * width)]
    for b in range(halo):
        @pl.when(sends(b + 1))
        def _():
            red.send(b * nc, (b + 1) * nc, pairs)

    red.send(halo * nc, (halo + 1) * nc, [(dq_ref, halo * nc, w_ref, 0)] + pairs)

    for b in range(halo):
        @pl.when(sends(b + 1))
        def _():
            red.relay(b * nc, (b + 1) * nc)

    red.relay(halo * nc, (halo + 1) * nc)

    def total(b, c):
        value = red.take(b * nc + c)
        if b == 0:
            return value

        @pl.when(comes(b))
        def _():
            hop(b, c).wait_recv()

        return value + zrecv[b - 1, pl.ds(c * size, size)].astype(F32)

    for j in range(1, halo + 1):
        for c in range(nc):
            @pl.when(sends(j))
            def _():
                zsend[j - 1, pl.ds(c * size, size)] = total(j - 1, c).astype(BF16)
                hop(j, c).start()

            if j > 1:
                @pl.when(jnp.logical_not(sends(j)) & comes(j - 1))
                def _():
                    hop(j - 1, c).wait_recv()

    def unit_of(rows):
        return x_ref[rows, :].astype(F32) * scale_ref[rows, :]

    def base_of(rows, back):
        return dh1_ref[rows, :] + scale_ref[rows, :] * back

    def done(c, rows, value):
        out_ref[rows, :] = value.astype(BF16)

    norm_back(nc, size, n * red.cols, functools.partial(total, halo), keep, sta, unit_of, gain_ref, base_of, gain_s, done)
    for k in range(1, n):
        word(k, peer_of(me, n - k, n)).wait_recv()
    total = words[0]
    for k in range(1, n):
        total = total + words[k]
    place = spot * n_dp + core
    mine = sums.at[place]
    cols = gain_s.shape[1]
    mine[...] = jnp.zeros((8, cols), F32)
    mine[0:1, :] = gain_s[...]
    mine[1:2, :] = gain_two_ref[...]
    mine[2:4, : total.shape[1]] = total[0:2]

    def share(t):
        i, j = others[t]
        return push(mine, mine, s4.at[t], r4.at[t], **of(i, j))

    def await_from(t):
        i, j = others[t]
        back = lax.rem(spot + n_seq - i, n_seq) * n_dp + lax.rem(core + n_dp - j, n_dp)
        theirs = sums.at[back]
        return push(theirs, theirs, s4.at[t], r4.at[t], **of(i, j))

    for t in range(len(others)):
        share(t).start()
    for t in range(len(others)):
        await_from(t).wait_recv()
    total = sums[0]
    for t in range(1, n_seq * n_dp):
        total = total + sums[t]
    sums_ref[...] = total
    for b in range(halo):
        @pl.when(sends(b + 1))
        def _():
            red.finish(b * nc, (b + 1) * nc)
            for c in range(nc):
                hop(b + 1, c).wait_send()

    red.finish(halo * nc, (halo + 1) * nc)
    sta.finish()
    for k in range(1, n):
        word(k, me).wait_send()
    for t in range(len(others)):
        share(t).wait_send()


def finish_kernel(n, n_seq, n_dp, halo, nc, n1t_hbm, w_hbm, dq_ref, dk_ref, dv_ref, dh1r_ref, g_ref, x_ref, scale_ref, gain_ref, dh1_ref, gain_two_ref, group_ref, out_ref, sums_ref, gq_ref, gk_ref, gv_ref, go_ref, own, sbuf, rbuf, n1t_ref, w_ref, dh1t, mine, given, taken, sent, came, stat, gain_s, words, sums, zsend, zrecv, keep, load_sem, s1, r1, s2, r2, s3, r3, s4, r4, s5, r5, s7, r7, s8, rl, rr):
    loads = [
        fetch(n1t_hbm, 0, n1t_ref, load_sem.at[0]),
        fetch(w_hbm, 0, w_ref, load_sem.at[1]),
    ]
    spot, core = lax.axis_index("seq"), lax.axis_index("dp")
    me = lax.axis_index("head")
    tok, width = dq_ref.shape
    size = tok // nc
    share = mine.shape[1]
    others = [(i, j) for i in range(n_seq) for j in range(n_dp) if i or j]

    def of(i, j):
        return {"seq": lax.rem(spot + i, n_seq), "dp": lax.rem(core + j, n_dp)}

    def sends(j):
        return spot >= halo - j + 1

    def comes(j):
        return (spot + 1 < n_seq) & (spot + 1 >= halo - j + 1)

    for j in range(1, halo + 1):
        @pl.when(jnp.logical_not(comes(j)))
        def _():
            zrecv[j - 1] = jnp.zeros(zrecv.shape[1:], BF16)

    words[me] = group_ref[...]
    dh1t[...] = dh1r_ref[...].T
    greet(*group(n), *(of(i, j) for i, j in others))
    red = reducer(n, size, me, own, sbuf, rbuf, s1, r1)
    sta = Stats(n, nc, me, stat, s2, r2)

    def word(k, source):
        return push(
            words.at[source], words.at[source], s3.at[k - 1], r3.at[k - 1], head=peer_of(me, k, n)
        )

    def hop(j, c):
        rows = pl.ds(c * size, size)
        return push(
            zsend.at[j - 1, rows], zrecv.at[j - 1, rows], s5.at[j - 1, c], r5.at[j - 1, c], seq=lax.rem(spot + n_seq - 1, n_seq)
        )

    for k in range(1, n):
        word(k, me).start()

    def block_grads(i, c, ref):
        rows = rows_of(i * n_dp + c, share)
        ref[:, :width] = mm(n1t_ref[rows, halo * tok :], dq_ref[...], NN).astype(ref.dtype)
        ref[:, width : 2 * width] = mm(n1t_ref[rows, :], dk_ref[...], NN).astype(ref.dtype)
        ref[:, 2 * width : 3 * width] = mm(n1t_ref[rows, :], dv_ref[...], NN).astype(ref.dtype)
        ref[:, 3 * width :] = mm(dh1t[rows, :], g_ref[...], NN).astype(ref.dtype)

    def give(k, i):
        return push(
            given.at[k - 1, i], taken.at[k - 1, i], s7.at[k - 1, i], r7.at[k - 1, i], dp=lax.rem(core + k, n_dp)
        )

    def block_relay(b):
        if b == halo:
            red.relay(b * nc, (b + 1) * nc)
        else:
            @pl.when(sends(b + 1))
            def _():
                red.relay(b * nc, (b + 1) * nc)

    loads[1].wait()
    pairs = [(dk_ref, 0, w_ref, width), (dv_ref, 0, w_ref, 2 * width)]
    for b in range(halo):
        @pl.when(sends(b + 1))
        def _():
            red.send(b * nc, (b + 1) * nc, pairs)

    loads[0].wait()
    for k in range(1, n_dp):

        @pl.loop(0, n_seq)
        def _(i):
            block_grads(i, lax.rem(core + k, n_dp), given.at[k - 1, i])
            give(k, i).start()

    @pl.loop(0, n_seq)
    def _(i):
        block_grads(i, core, mine.at[i])

    half = mine.shape[2] // 2

    def chip(d, p):
        cols = slice(p * half, (p + 1) * half)
        value = mine[d, :, cols]
        for k in range(1, n_dp):
            if p == 0:
                give(k, d).wait_recv()
            value = value + taken[k - 1, d, :, cols].astype(F32)
        return value

    def piece(d, p, slot, sem, to):
        cols = slice(p * half, (p + 1) * half)
        return push(sent.at[d, :, cols], came.at[slot, :, cols], s8.at[d, p], sem.at[d, p], seq=to)

    def right(d, p):
        return piece(d, p, d, rl, lax.rem(spot + 1, n_seq))

    def left(d, p):
        return piece(d, p, jnp.where(spot - 1 == d, n_seq, d), rr, lax.rem(spot + n_seq - 1, n_seq))

    def arrived(d, p, slot, sem):
        return piece(d, p, slot, sem, lax.rem(spot + 1, n_seq))

    def start_line(i, p):
        cols = slice(p * half, (p + 1) * half)
        d = n_seq - 1 - i

        @pl.when(spot == 0)
        def _():
            if i:
                right(d + 1, p).wait_send()
            sent[d, :, cols] = chip(d, p).astype(BF16)
            right(d, p).start()

        @pl.when(spot == n_seq - 1)
        def _():
            if i:
                left(i - 1, p).wait_send()
            sent[i, :, cols] = chip(i, p).astype(BF16)
            left(i, p).start()

    def pass_line(i, p):
        cols = slice(p * half, (p + 1) * half)
        d = n_seq - 1 - i

        @pl.when((spot > 0) & (d > spot))
        def _():
            arrived(d, p, d, rl).wait_recv()
            sent[d, :, cols] = (chip(d, p) + came[d, :, cols].astype(F32)).astype(BF16)
            right(d, p).start()

        @pl.when((spot < n_seq - 1) & (i < spot))
        def _():
            arrived(i, p, i, rr).wait_recv()
            sent[i, :, cols] = (chip(i, p) + came[i, :, cols].astype(F32)).astype(BF16)
            left(i, p).start()

    def total(b, c):
        value = red.take(b * nc + c)
        if b == 0:
            return value

        @pl.when(comes(b))
        def _():
            hop(b, c).wait_recv()

        return value + zrecv[b - 1, pl.ds(c * size, size)].astype(F32)

    def send_hop(j):
        for c in range(nc):
            @pl.when(sends(j))
            def _():
                zsend[j - 1, pl.ds(c * size, size)] = total(j - 1, c).astype(BF16)
                hop(j, c).start()

            if j > 1:
                @pl.when(jnp.logical_not(sends(j)) & comes(j - 1))
                def _():
                    hop(j - 1, c).wait_recv()

    for p in range(2):
        if n_seq > 1:
            start_line(0, p)
    for b in range(halo):
        block_relay(b)
    red.send(halo * nc, (halo + 1) * nc, [(dq_ref, halo * nc, w_ref, 0)] + pairs)
    for t in range(max(n_seq - 1, 1)):
        if t < halo:
            send_hop(t + 1)
        for p in range(2):
            if t < n_seq - 1:
                pass_line(t, p)
            if t + 1 < n_seq - 1:
                start_line(t + 1, p)
        if t == 0:
            block_relay(halo)

    def unit_of(rows):
        return x_ref[rows, :].astype(F32) * scale_ref[rows, :]

    def base_of(rows, back):
        return dh1_ref[rows, :] + scale_ref[rows, :] * back

    def done(c, rows, value):
        out_ref[rows, :] = value.astype(BF16)

    norm_back(nc, size, n * red.cols, functools.partial(total, halo), keep, sta, unit_of, gain_ref, base_of, gain_s, done)
    for k in range(1, n):
        word(k, peer_of(me, n - k, n)).wait_recv()
    group_sum = words[0]
    for k in range(1, n):
        group_sum = group_sum + words[k]
    place = spot * n_dp + core
    slip = sums.at[place]
    cols = gain_s.shape[1]
    slip[...] = jnp.zeros((8, cols), F32)
    slip[0:1, :] = gain_s[...]
    slip[1:2, :] = gain_two_ref[...]
    slip[2:4, : group_sum.shape[1]] = group_sum[0:2]

    def hand(t):
        i, j = others[t]
        return push(slip, slip, s4.at[t], r4.at[t], **of(i, j))

    def handed(t):
        i, j = others[t]
        back = lax.rem(spot + n_seq - i, n_seq) * n_dp + lax.rem(core + n_dp - j, n_dp)
        theirs = sums.at[back]
        return push(theirs, theirs, s4.at[t], r4.at[t], **of(i, j))

    for t in range(len(others)):
        hand(t).start()
    for p in range(2):
        cols = slice(p * half, (p + 1) * half)
        mine[spot, :, cols] = chip(spot, p)

        @pl.when(spot > 0)
        def _():
            arrived(spot, p, spot, rl).wait_recv()
            mine[spot, :, cols] = mine[spot, :, cols] + came[spot, :, cols].astype(F32)

        @pl.when(spot < n_seq - 1)
        def _():
            arrived(spot, p, n_seq, rr).wait_recv()
            mine[spot, :, cols] = mine[spot, :, cols] + came[n_seq, :, cols].astype(F32)

    for i, ref in enumerate((gq_ref, gk_ref, gv_ref, go_ref)):
        ref[...] = mine[spot, :, i * width : (i + 1) * width]
    for t in range(len(others)):
        handed(t).wait_recv()
    full_sum = sums[0]
    for t in range(1, n_seq * n_dp):
        full_sum = full_sum + sums[t]
    sums_ref[...] = full_sum
    for b in range(halo):
        @pl.when(sends(b + 1))
        def _():
            red.finish(b * nc, (b + 1) * nc)
            for c in range(nc):
                hop(b + 1, c).wait_send()

    red.finish(halo * nc, (halo + 1) * nc)
    sta.finish()
    for k in range(1, n):
        word(k, me).wait_send()
    for t in range(len(others)):
        hand(t).wait_send()
    for k in range(1, n_dp):
        for i in range(n_seq):
            give(k, i).wait_send()
    for d in range(n_seq):
        for p in range(2):

            @pl.when((spot < d) & ((spot > 0) | (d == 1)))
            def _():
                right(d, p).wait_send()

            @pl.when((spot > d) & ((spot < n_seq - 1) | (d == n_seq - 2)))
            def _():
                left(d, p).wait_send()


def far_away(x):
    return pltpu.with_memory_space_constraint(x, pltpu.HBM)


def dma(*dims):
    return pltpu.SemaphoreType.DMA(dims)


def talk(kernel, ident, outs, scratch, flops, room, args, far=(), far_outs=(), kept=(), kept_outs=()):
    return pl.pallas_call(
        kernel,
        out_shape=[
            pltpu.HBM(s, d) if i in far_outs or i in kept_outs else jax.ShapeDtypeStruct(s, d)
            for i, (s, d) in enumerate(outs)
        ],
        in_specs=[
            pl.BlockSpec(memory_space=pltpu.HBM) if i in far else whole() for i in range(len(args))
        ],
        out_specs=[
            pl.BlockSpec(memory_space=pltpu.HBM) if i in far_outs else whole()
            for i in range(len(outs))
        ],
        scratch_shapes=scratch,
        cost_estimate=pl.CostEstimate(flops=flops, bytes_accessed=40 * 2**20, transcendentals=0),
        compiler_params=pltpu.CompilerParams(
            collective_id=ident, has_side_effects=True, vmem_limit_bytes=room * 2**20
        ),
    )(*(far_away(a) if i in far or i in kept else a for i, a in enumerate(args)))


def forward_kernel(base, nb_ref, lam_ref, q_ref, k_ref, v_ref, start_ref, gain_ref, o1_ref, o2_ref, lse_ref, g_ref, held, m_s, l_s, acc):
    size = q_ref.shape[0]
    qt = pl.program_id(1)
    q = q_ref[...] * 0.125
    lane = lax.broadcasted_iota(jnp.int32, q.shape, 1)
    zero = jnp.zeros_like(q)
    parts = (jnp.where(lane < HALF, q, zero), jnp.where(lane >= HALF, q, zero))
    key = lax.broadcasted_iota(jnp.int32, (size, size), 0)
    query = lax.broadcasted_iota(jnp.int32, (size, size), 1)
    start = start_ref[...]

    count = nb_ref[qt]

    def scores(d, first):
        where = base + qt - d
        k = k_ref[rows_of(where, size), :]
        allowed = key >= start - where * size
        if first:
            allowed = allowed & (key <= query)
        for m in range(2):
            s = jnp.where(allowed, mm(k, parts[m], NT), NEG_BIG)
            held[d, m] = s
            top = jnp.max(s, axis=0, keepdims=True)
            m_s[m] = top if first else jnp.maximum(m_s[m], top)

    def weights(d, _):
        for m in range(2):
            e = jnp.exp(held[d, m] - m_s[m])
            held[d, m] = e
            l_s[m] += jnp.sum(e, axis=0, keepdims=True)
        return 0

    def mix(d, first):
        v = v_ref[rows_of(base + qt - d, size), :]
        for m in range(2):
            term = mm(v, (held[d, m] * l_s[m]).astype(BF16), TN)
            if first:
                acc[m] = term
            else:
                acc[m] += term

    def each(step):
        def body(d, _):
            step(d, False)
            return 0

        step(0, True)
        lax.fori_loop(1, count, body, 0)

    each(scores)
    l_s[...] = jnp.zeros_like(l_s)
    lax.fori_loop(0, count, weights, 0)
    for m in range(2):
        lse_ref[0, m : m + 1, :] = m_s[m] + jnp.log(l_s[m])
        l_s[m] = 1.0 / l_s[m]
    each(mix)
    o1, o2 = acc[0], acc[1]
    o1_ref[...] = o1
    o2_ref[...] = o2
    diff = o1 - lam_ref[0] * o2
    scale = lax.rsqrt(jnp.mean(diff * diff, axis=0, keepdims=True) + EPS)
    g = diff * scale * gain_ref[...] * KEEP
    g_ref[...] = g.T.astype(BF16)


def backward_kernel(base, nb_ref, lam_ref, q_ref, k_ref, v_ref, start_ref, gain_ref, o1_ref, o2_ref, lse_ref, dg_ref, dq_ref, dk_ref, dv_ref, gain_grad_ref, lam_grad_ref, dq_s, dk_s, dv_s):
    size = q_ref.shape[0]
    h, qt = pl.program_id(0), pl.program_id(1)
    lam = lam_ref[0]

    @pl.when((h == 0) & (qt == 0))
    def _():
        gain_grad_ref[...] = jnp.zeros_like(gain_grad_ref)
        lam_grad_ref[...] = jnp.zeros_like(lam_grad_ref)

    @pl.when(qt == 0)
    def _():
        dk_s[...] = jnp.zeros_like(dk_s)
        dv_s[...] = jnp.zeros_like(dv_s)

    o1, o2 = o1_ref[...], o2_ref[...]
    diff = o1 - lam * o2
    scale = lax.rsqrt(jnp.mean(diff * diff, axis=0, keepdims=True) + EPS)
    unit = diff * scale
    dg = dg_ref[...].T
    gain_grad_ref[...] += jnp.sum(dg * unit, axis=1, keepdims=True) * KEEP
    du = dg * gain_ref[...] * KEEP
    do = scale * (du - unit * jnp.mean(du * unit, axis=0, keepdims=True))
    lam_grad_ref[...] -= jnp.sum(do * o2, axis=1, keepdims=True)
    grads = (do.astype(BF16), (-lam * do).astype(BF16))
    deltas = tuple(
        jnp.sum(g.astype(F32) * o, axis=0, keepdims=True) for g, o in zip(grads, (o1, o2))
    )
    q = q_ref[...] * 0.125
    lane = lax.broadcasted_iota(jnp.int32, q.shape, 1)
    zero = jnp.zeros_like(q)
    parts = (jnp.where(lane < HALF, q, zero), jnp.where(lane >= HALF, q, zero))
    key = lax.broadcasted_iota(jnp.int32, (size, size), 0)
    query = lax.broadcasted_iota(jnp.int32, (size, size), 1)
    start = start_ref[...]
    dq_s[...] = jnp.zeros_like(dq_s)

    def block(where, first):
        rows = rows_of(where, size)
        k, v = k_ref[rows, :], v_ref[rows, :]
        halves = (jnp.where(lane < HALF, k, zero), jnp.where(lane >= HALF, k, zero))
        allowed = key >= start - where * size
        if first:
            allowed = allowed & (key <= query)
        dq = dq_s[...]
        dk = dk_s[rows, :]
        dv = dv_s[rows, :]
        for m in range(2):
            s = mm(k, parts[m], NT)
            p = jnp.where(allowed, jnp.exp(s - lse_ref[0, m : m + 1, :]), 0.0)
            dp = mm(v, grads[m], NN)
            ds = (p * (dp - deltas[m])).astype(BF16)
            dq = dq + mm(halves[m], ds, TN)
            dk = dk + mm(ds, parts[m], NN)
            dv = dv + mm(p.astype(BF16), grads[m], NT)
        dq_s[...] = dq
        dk_s[rows, :] = dk
        dv_s[rows, :] = dv

    block(base + qt, True)

    def earlier(d, _):
        block(base + qt - d, False)
        return 0

    lax.fori_loop(1, nb_ref[qt], earlier, 0)
    dq_ref[...] = (dq_s[...] * 0.125).T.astype(BF16)

    @pl.when(qt == pl.num_programs(1) - 1)
    def _():
        dk_ref[...] = dk_s[...].astype(BF16)
        dv_ref[...] = dv_s[...].astype(BF16)


SMEM = pl.BlockSpec(memory_space=pltpu.SMEM)
TILE = 256


def attend(q, kv, start, nb, lam, gain_col):
    tok, width = q.shape
    heads = width // VDIM
    rows = kv.shape[0]
    size = min(TILE, tok)
    base = (rows - tok) // size
    head_block = pl.BlockSpec((VDIM, size), lambda h, t: (h, t))
    return pl.pallas_call(
        functools.partial(forward_kernel, base),
        grid=(heads, tok // size),
        out_shape=[
            jax.ShapeDtypeStruct((width, tok), F32),
            jax.ShapeDtypeStruct((width, tok), F32),
            jax.ShapeDtypeStruct((heads, 2, tok), F32),
            jax.ShapeDtypeStruct((tok, width), BF16),
        ],
        in_specs=[
            SMEM,
            SMEM,
            pl.BlockSpec((size, VDIM), lambda h, t: (t, h)),
            pl.BlockSpec((rows, VDIM), lambda h, t: (0, h)),
            pl.BlockSpec((rows, VDIM), lambda h, t: (0, heads + h)),
            pl.BlockSpec((1, size), lambda h, t: (0, t)),
            pl.BlockSpec((VDIM, 1), lambda h, t: (0, 0)),
        ],
        out_specs=[
            head_block,
            head_block,
            pl.BlockSpec((1, 2, size), lambda h, t: (h, 0, t)),
            pl.BlockSpec((size, VDIM), lambda h, t: (t, h)),
        ],
        scratch_shapes=[
            VMEM((rows // size, 2, size, size), F32),
            VMEM((2, 1, size), F32),
            VMEM((2, 1, size), F32),
            VMEM((2, VDIM, size), F32),
        ],
        cost_estimate=pl.CostEstimate(
            flops=4 * tok * rows * heads * VDIM,
            bytes_accessed=8 * tok * width + 4 * rows * width,
            transcendentals=2 * tok * rows * heads,
        ),
        compiler_params=pltpu.CompilerParams(vmem_limit_bytes=32 * 2**20),
    )(nb, lam, q, kv, kv, start, gain_col)


def halo_room(rows, tok):
    return 2 * (rows // tok)


def attend_back(q, kv, start, nb, lam, gain_col, o1, o2, lse, dg):
    tok, width = q.shape
    heads = width // VDIM
    rows = kv.shape[0]
    size = min(TILE, tok)
    base = (rows - tok) // size
    head_block = pl.BlockSpec((VDIM, size), lambda h, t: (h, t))
    return pl.pallas_call(
        functools.partial(backward_kernel, base),
        grid=(heads, tok // size),
        out_shape=[
            pltpu.HBM((tok, width), BF16),
            pltpu.HBM((rows, width), BF16),
            pltpu.HBM((rows, width), BF16),
            jax.ShapeDtypeStruct((VDIM, 1), F32),
            jax.ShapeDtypeStruct((VDIM, 1), F32),
        ],
        in_specs=[
            SMEM,
            SMEM,
            pl.BlockSpec((size, VDIM), lambda h, t: (t, h)),
            pl.BlockSpec((rows, VDIM), lambda h, t: (0, h)),
            pl.BlockSpec((rows, VDIM), lambda h, t: (0, heads + h)),
            pl.BlockSpec((1, size), lambda h, t: (0, t)),
            pl.BlockSpec((VDIM, 1), lambda h, t: (0, 0)),
            head_block,
            head_block,
            pl.BlockSpec((1, 2, size), lambda h, t: (h, 0, t)),
            pl.BlockSpec((size, VDIM), lambda h, t: (t, h)),
        ],
        out_specs=[
            pl.BlockSpec((size, VDIM), lambda h, t: (t, h)),
            pl.BlockSpec((rows, VDIM), lambda h, t: (0, h)),
            pl.BlockSpec((rows, VDIM), lambda h, t: (0, h)),
            pl.BlockSpec((VDIM, 1), lambda h, t: (0, 0)),
            pl.BlockSpec((VDIM, 1), lambda h, t: (0, 0)),
        ],
        scratch_shapes=[
            VMEM((VDIM, size), F32),
            VMEM((rows, VDIM), F32),
            VMEM((rows, VDIM), F32),
        ],
        cost_estimate=pl.CostEstimate(
            flops=10 * tok * rows * heads * VDIM,
            bytes_accessed=16 * tok * width + 8 * rows * width,
            transcendentals=2 * tok * rows * heads,
        ),
        compiler_params=pltpu.CompilerParams(vmem_limit_bytes=(12 + halo_room(rows, tok)) * 2**20),
    )(nb, lam, q, kv, kv, start, gain_col, o1, o2, lse, dg)


CHUNKS = 2


def on_device(
    n_head,
    n_seq,
    n_dp,
    inputs,
    w_query,
    w_key,
    w_value,
    w_output,
    w_gate,
    w_up,
    w_down,
    gain_attn,
    gain_ffn,
    group_gain,
    lambda_q1,
    lambda_k1,
    lambda_q2,
    lambda_k2,
    doc_ids,
    needles,
    out_grad,
):
    x = inputs[0]
    tok, cols = x.shape
    n, nc = n_head, CHUNKS
    full = n * cols
    width = w_query.shape[1]
    hidden = w_gate.shape[1]
    me = lax.axis_index("head")
    halo = n_seq // 2

    w_attn = lax.all_gather(
        jnp.concatenate([w_query, w_key, w_value, w_output], axis=1),
        ("seq", "dp"),
        axis=0,
        tiled=True,
    )
    w_ffn = lax.all_gather(
        jnp.concatenate([w_gate, w_up, w_down], axis=1), ("seq", "dp"), axis=0, tiled=True
    )

    weight = jnp.where(needles[0] == 1, 1.0, 0.1).astype(F32)
    dy = out_grad[0].astype(F32) * weight[:, None]
    gain_one = gain_attn[None, :]
    gain_two = gain_ffn[None, :]
    gain_one_cols = lax.dynamic_slice_in_dim(gain_one, me * cols, cols, 1)
    gain_two_cols = lax.dynamic_slice_in_dim(gain_two, me * cols, cols, 1)
    lam = jnp.exp(jnp.sum(lambda_q1 * lambda_k1)) - jnp.exp(jnp.sum(lambda_q2 * lambda_k2))
    lam = (lam + LAMBDA_INIT)[None]
    gain_col = group_gain[:, None]

    docs = jnp.broadcast_to(doc_ids + 1, (8, tok))
    n1, scale_one, dyr, window, n1t = talk(
        functools.partial(enter_kernel, n, n_seq, halo),
        0,
        [
            (((halo + 1) * tok, full), BF16),
            ((tok, 1), F32),
            ((tok, full), BF16),
            ((8, (halo + 1) * tok), jnp.int32),
            ((full, (halo + 1) * tok), BF16),
        ],
        [
            VMEM((n, (halo + 1) * tok, cols), BF16),
            VMEM((n, tok, cols), BF16),
            VMEM((halo + 1, 8, tok), jnp.int32),
            VMEM((full, (halo + 1) * tok), BF16),
            pltpu.SemaphoreType.DMA,
        ]
        + [dma(n - 1, 2 * (halo + 1))] * 2
        + [dma(n - 1, 2)] * 2
        + [dma(max(halo, 1))] * 4,
        tok * full * 8,
        14 + 4 * (halo + 1),
        (x, dy.astype(BF16), gain_one, docs),
        far_outs=(4,),
        kept_outs=(2,),
    )
    start = jnp.sum((window[0][None, :] < docs[0][:, None]).astype(jnp.int32), axis=1)
    size = min(TILE, tok)
    base = halo * tok // size
    first = start[::size]
    nb = base + jnp.arange(tok // size, dtype=jnp.int32) - first // size + 1
    start = start[None, :]

    q = jnp.dot(n1[halo * tok :], w_attn[:, :width], preferred_element_type=F32).astype(BF16)
    kv = jnp.dot(n1, w_attn[:, width : 3 * width], preferred_element_type=F32).astype(BF16)
    o1, o2, lse, grouped = attend(q, kv, start, nb, lam, gain_col)

    exchange = [VMEM((tok, cols), F32), VMEM((n - 1, tok, cols), BF16), VMEM((n - 1, tok, cols), BF16)]
    h1, n2, scale_two = talk(
        functools.partial(middle_kernel, n, nc, 3 * width),
        1,
        [((tok, cols), F32), ((tok, full), BF16), ((tok, 1), F32)],
        exchange
        + [VMEM((full, width), BF16), VMEM((n, tok, cols), BF16), pltpu.SemaphoreType.DMA]
        + [dma(n - 1, nc)] * 4,
        2 * tok * full * width,
        14,
        (grouped, w_attn, x, gain_two),
        far=(1,),
        kept_outs=(1,),
    )
    tile = min(TILE, hidden)
    inner, d_gate, d_up, d_wffn = ffn(n2, dyr, w_ffn, tile)
    g_ffn = lax.psum_scatter(d_wffn, ("seq", "dp"), scatter_dimension=0, tiled=True)

    stat = VMEM((n, nc, 8, tok // nc), F32)
    dh1, dh1r, gain_two_part, output = talk(
        functools.partial(back_kernel, n, nc, 0, 2 * hidden),
        2,
        [((tok, cols), F32), ((tok, full), BF16), ((1, cols), F32), ((tok, cols), BF16)],
        exchange
        + exchange
        + [
            VMEM((full, 2 * hidden), BF16),
            VMEM((full, hidden), BF16),
            stat,
            VMEM((n, tok, cols), BF16),
            pltpu.SemaphoreType.DMA,
            pltpu.SemaphoreType.DMA,
        ]
        + [dma(n - 1, nc)] * 8,
        4 * tok * full * hidden,
        26,
        (d_gate, d_up, inner, w_ffn, h1, scale_two, gain_two_cols, dy),
        far=(3,),
        kept=(0, 1, 2),
    )
    dg = jnp.dot(dh1r, w_attn[:, 3 * width :], preferred_element_type=F32)
    dq, dk, dv, group_part, lam_part = attend_back(
        q, kv, start, nb, lam, gain_col, o1, o2, lse, dg
    )
    group_words = jnp.concatenate(
        [
            group_part.T,
            jnp.broadcast_to(jnp.sum(lam_part), (1, VDIM)),
            jnp.zeros((6, VDIM), F32),
        ]
    )
    others = n_seq * n_dp - 1
    span = (halo + 1) * tok
    if halo <= 2:
        rows = w_query.shape[0]
        line = (n_seq, rows, 4 * width)
        input_grad, sums, g_query, g_key, g_value, g_output = talk(
            functools.partial(finish_kernel, n, n_seq, n_dp, halo, nc),
            3,
            [((tok, cols), BF16), ((8, cols), F32)] + [((rows, width), F32)] * 4,
            [
                VMEM((span, cols), F32),
                VMEM((n - 1, span, cols), BF16),
                VMEM((n - 1, span, cols), BF16),
            ]
            + [
                VMEM((full, span), BF16),
                VMEM((full, 3 * width), BF16),
                VMEM((full, tok), BF16),
                VMEM(line, F32),
                VMEM((max(n_dp - 1, 1),) + line, BF16),
                VMEM((max(n_dp - 1, 1),) + line, BF16),
                VMEM(line, BF16),
                VMEM((n_seq + 1, rows, 4 * width), BF16),
                stat,
                VMEM((1, cols), F32),
                VMEM((n, 8, VDIM), F32),
                VMEM((others + 1, 8, cols), F32),
                VMEM((max(halo, 1), tok, cols), BF16),
                VMEM((max(halo, 1), tok, cols), BF16),
                VMEM((tok, cols), F32),
                dma(2),
            ]
            + [dma(n - 1, (halo + 1) * nc)] * 2
            + [dma(n - 1, nc)] * 2
            + [dma(n - 1)] * 2
            + [dma(max(others, 1))] * 2
            + [dma(max(halo, 1), nc)] * 2
            + [dma(max(n_dp - 1, 1), n_seq)] * 2
            + [dma(n_seq, 2)] * 3,
            6 * tok * full * width * (halo + 1),
            50,
            (n1t, w_attn, dq, dk, dv, dh1r, grouped, x, scale_one, gain_one_cols, dh1, gain_two_part, group_words),
            far=(0, 1),
            kept=(2, 3, 4),
        )
    else:
        d_wattn = projection_grads(halo, n1t, dq, dk, dv, dh1r, grouped)
        d_wattn, g_ffn = lax.optimization_barrier((d_wattn, g_ffn))
        g_attn = lax.psum_scatter(d_wattn, ("seq", "dp"), scatter_dimension=0, tiled=True).astype(F32)
        input_grad, sums = talk(
            functools.partial(leave_kernel, n, n_seq, n_dp, halo, nc),
            3,
            [((tok, cols), BF16), ((8, cols), F32)],
            [
                VMEM((span, cols), F32),
                VMEM((n - 1, span, cols), BF16),
                VMEM((n - 1, span, cols), BF16),
                VMEM((full, 3 * width), BF16),
                stat,
                VMEM((1, cols), F32),
                VMEM((n, 8, VDIM), F32),
                VMEM((others + 1, 8, cols), F32),
                VMEM((max(halo, 1), tok, cols), BF16),
                VMEM((max(halo, 1), tok, cols), BF16),
                VMEM((tok, cols), F32),
                pltpu.SemaphoreType.DMA,
            ]
            + [dma(n - 1, (halo + 1) * nc)] * 2
            + [dma(n - 1, nc)] * 2
            + [dma(n - 1)] * 2
            + [dma(max(others, 1))] * 2
            + [dma(max(halo, 1), nc)] * 2,
            6 * tok * full * width * (halo + 1),
            26 + 5 * halo,
            (dq, dk, dv, w_attn, x, scale_one, gain_one_cols, dh1, gain_two_part, group_words),
            far=(3,),
        )
        g_query, g_key, g_value, g_output = (
            g_attn[:, i * width : (i + 1) * width] for i in range(4)
        )
    g_ffn = g_ffn.astype(F32)
    share = cols // (n_seq * n_dp)
    place = lax.axis_index("seq") * n_dp + lax.axis_index("dp")
    gains = lax.dynamic_slice_in_dim(sums[:2], place * share, share, 1)
    return (
        output[None],
        input_grad[None],
        gains[0],
        gains[1],
        sums[2, :VDIM],
        sums[3, :1],
        g_query,
        g_key,
        g_value,
        g_output,
        g_ffn[:, :hidden],
        g_ffn[:, hidden : 2 * hidden],
        g_ffn[:, 2 * hidden :],
    )


def solution(mesh):
    act = P("dp", "seq", "head")
    mat = P(("seq", "dp"), "head")
    vec = P(("head", "seq", "dp"))
    return jax.shard_map(
        functools.partial(on_device, mesh.shape["head"], mesh.shape["seq"], mesh.shape["dp"]),
        mesh=mesh,
        in_specs=(act,) + (mat,) * 7 + (P(),) * 7 + (P("dp", "seq"),) * 2 + (act,),
        out_specs=(act, act, vec, vec, P(), P()) + (mat,) * 7,
        check_vma=False,
    )
```

```python
import functools
import math

import jax
import jax.numpy as jnp
from jax import lax
from jax.experimental import pallas as pl
from jax.experimental.pallas import tpu as pltpu
from jax.sharding import PartitionSpec as P

HALF = 64
VDIM = 128
EPS = 1e-05
LAMBDA_INIT = 0.8 - 0.6 * math.exp(-0.3)
KEEP = 1.0 - LAMBDA_INIT
NEG_BIG = -1e30
MESH = pl.DeviceIdType.MESH
VMEM = pltpu.VMEM
F32 = jnp.float32
BF16 = jnp.bfloat16
NN = (((1,), (0,)), ((), ()))
NT = (((1,), (1,)), ((), ()))
TN = (((0,), (0,)), ((), ()))


def mm(a, b, dims):
    return lax.dot_general(a, b, dims, preferred_element_type=F32)


def whole():
    return pl.BlockSpec(memory_space=VMEM)


def peer_of(me, k, n):
    return lax.rem(me + k, n)


def greet(*peers):
    barrier = pltpu.get_barrier_semaphore()
    for peer in peers:
        pl.semaphore_signal(barrier, 1, device_id=peer, device_id_type=MESH)
    pl.semaphore_wait(barrier, len(peers))


def along(axis, size, steps):
    spot = lax.axis_index(axis)
    return [{axis: lax.rem(spot + k, size)} for k in steps]


def group(n):
    return along("head", n, range(1, n))


def push(src, dst, send, recv, **peer):
    return pltpu.make_async_remote_copy(
        src_ref=src,
        dst_ref=dst,
        send_sem=send,
        recv_sem=recv,
        device_id=peer,
        device_id_type=MESH,
    )


def rows_of(c, size):
    return pl.ds(pl.multiple_of(c * size, size), size)


def fetch(w_hbm, off, w_ref, sem):
    copy = pltpu.make_async_copy(w_hbm.at[:, off : off + w_ref.shape[1]], w_ref, sem)
    copy.start()
    return copy


class Reduce:
    def __init__(self, n, size, me, own_ref, sbuf, rbuf, ssem, rsem):
        self.n, self.size, self.me = n, size, me
        self.own_ref, self.sbuf, self.rbuf, self.ssem, self.rsem = own_ref, sbuf, rbuf, ssem, rsem
        self.cols = own_ref.shape[1]

    def copy(self, k, c):
        rows = rows_of(c, self.size)
        return push(
            self.sbuf.at[k - 1, rows],
            self.rbuf.at[k - 1, rows],
            self.ssem.at[k - 1, c],
            self.rsem.at[k - 1, c],
            head=peer_of(self.me, k, self.n),
        )

    def send(self, first, last, pairs):
        n = self.n

        def step(t, _):
            turn = t // n
            c = first + turn
            k = t - turn * n + 1
            rows = rows_of(c, self.size)
            peer = peer_of(self.me, k, n)
            part = None
            for a_ref, behind, w_ref, off in pairs:
                span = slice(off, off + a_ref.shape[1])
                term = mm(
                    a_ref[rows_of(c - behind, self.size), :],
                    w_ref[rows_of(peer, self.cols), span],
                    NT,
                )
                part = term if part is None else part + term

            @pl.when(k < n)
            def _():
                self.sbuf[k - 1, rows] = part.astype(BF16)
                self.copy(k, c).start()

            @pl.when(k == n)
            def _():
                self.own_ref[rows, :] = part

            return 0

        lax.fori_loop(0, (last - first) * n, step, 0)

    def relay(self, first, last):
        pass

    def take(self, c):
        rows = rows_of(c, self.size)
        total = self.own_ref[rows, :]
        for k in range(1, self.n):
            self.copy(k, c).wait_recv()
        for k in range(1, self.n):
            total = total + self.rbuf[k - 1, rows].astype(F32)
        return total

    def finish(self, first, last):
        for c in range(first, last):
            for k in range(1, self.n):
                self.copy(k, c).wait_send()


class Gather:
    def __init__(self, n, nc, me, buf, ssem, rsem):
        self.n, self.nc, self.me = n, nc, me
        self.buf, self.ssem, self.rsem = buf, ssem, rsem
        self.size = buf.shape[1] // nc

    def copy(self, k, c, source):
        rows = rows_of(c, self.size)
        return push(
            self.buf.at[source, rows],
            self.buf.at[source, rows],
            self.ssem.at[k - 1, c],
            self.rsem.at[k - 1, c],
            head=peer_of(self.me, k, self.n),
        )

    def send(self, c, value=None):
        if value is not None:
            self.buf[self.me, rows_of(c, self.size)] = value
        for k in range(1, self.n):
            self.copy(k, c, self.me).start()

    def relay(self, c):
        pass

    def take(self, c):
        for k in range(1, self.n):
            self.copy(k, c, peer_of(self.me, self.n - k, self.n)).wait_recv()

    def finish(self, only=None):
        for c in range(self.nc) if only is None else (only,):
            for k in range(1, self.n):
                self.copy(k, c, self.me).wait_send()


def square(me):
    return me + 1 - 2 * lax.rem(me, 2), lax.rem(me + 2, 4), 3 - me


class SquareReduce(Reduce):
    def copy(self, k, c, odd):
        rows = rows_of(c, self.size)
        near, far, _ = square(self.me)
        return push(
            self.sbuf.at[k - 1, rows],
            self.rbuf.at[k - 1, rows],
            self.ssem.at[k - 1, c],
            self.rsem.at[k - 1, c],
            head=far if (k == 2) != odd else near,
        )

    def send(self, first, last, pairs):
        size = self.size
        near, far, across = square(self.me)

        def step(turn, _):
            t = turn // 4
            k = turn - 4 * t
            two = rows_of(t, 2 * size)
            even, odd = rows_of(2 * t, size), rows_of(2 * t + 1, size)
            owner = jnp.where(k == 0, across, jnp.where(k == 1, near, jnp.where(k == 2, far, self.me)))
            part = None
            for a_ref, behind, w_ref, off in pairs:
                span = slice(off, off + a_ref.shape[1])
                term = mm(
                    a_ref[rows_of(t - behind // 2, 2 * size), :],
                    w_ref[rows_of(owner, self.cols), span],
                    NT,
                )
                part = term if part is None else part + term
            self.own_ref[two, :] = part

            @pl.when(k == 0)
            def _():
                self.sbuf[2, two] = part.astype(BF16)
                self.copy(3, 2 * t, False).start()
                self.copy(3, 2 * t + 1, True).start()

            @pl.when(k == 1)
            def _():
                self.sbuf[0, even] = part[:size].astype(BF16)
                self.sbuf[1, odd] = part[size:].astype(BF16)
                self.copy(1, 2 * t, False).start()

            @pl.when(k == 2)
            def _():
                self.sbuf[1, even] = part[:size].astype(BF16)
                self.sbuf[0, odd] = part[size:].astype(BF16)
                self.copy(1, 2 * t + 1, True).start()

            return 0

        lax.fori_loop(2 * first, 2 * last, step, 0)

    def relay(self, first, last):
        for c in range(first, last):
            rows = rows_of(c, self.size)
            odd = c % 2 == 1
            self.copy(3, c, odd).wait_recv()
            both = self.sbuf[1, rows].astype(F32) + self.rbuf[2, rows].astype(F32)
            self.sbuf[1, rows] = both.astype(BF16)
            self.copy(2, c, odd).start()

    def take(self, c):
        rows = rows_of(c, self.size)
        for k in (1, 2):
            self.copy(k, c, c % 2 == 1).wait_recv()
        return self.own_ref[rows, :] + self.rbuf[0, rows].astype(F32) + self.rbuf[1, rows].astype(F32)

    def finish(self, first, last):
        for c in range(first, last):
            for k in range(1, self.n):
                self.copy(k, c, c % 2 == 1).wait_send()


class SquareGather(Gather):
    def own(self, k, c):
        near, far, _ = square(self.me)
        rows = rows_of(c, self.size)
        return push(
            self.buf.at[self.me, rows],
            self.buf.at[self.me, rows],
            self.ssem.at[k - 1, c],
            self.rsem.at[k - 1, c],
            head=(near, far)[k - 1],
        )

    def came(self, k, c):
        source = square(self.me)[k - 1]
        rows = rows_of(c, self.size)
        return push(
            self.buf.at[source, rows],
            self.buf.at[source, rows],
            self.ssem.at[k - 1, c],
            self.rsem.at[k - 1, c],
            head=square(self.me)[0],
        )

    def passed(self, c):
        near, far, _ = square(self.me)
        source, to = (near, far) if c % 2 else (far, near)
        rows = rows_of(c, self.size)
        return push(
            self.buf.at[source, rows],
            self.buf.at[source, rows],
            self.ssem.at[2, c],
            self.rsem.at[2, c],
            head=to,
        )

    def send(self, c, value=None):
        if value is not None:
            self.buf[self.me, rows_of(c, self.size)] = value
        for k in (1, 2):
            self.own(k, c).start()

    def relay(self, c):
        self.came(1 if c % 2 else 2, c).wait_recv()
        self.passed(c).start()

    def take(self, c):
        self.came(2 if c % 2 else 1, c).wait_recv()
        self.came(3, c).wait_recv()

    def finish(self, only=None):
        for c in range(self.nc) if only is None else (only,):
            for k in (1, 2):
                self.own(k, c).wait_send()
            self.passed(c).wait_send()


def reducer(n, *args):
    return (SquareReduce if n == 4 else Reduce)(n, *args)


def gatherer(n, *args):
    return (SquareGather if n == 4 else Gather)(n, *args)


def norm_rows(n, buf, rows, gain_ref, out_ref, scale_ref=None, scale_rows=None):
    cols = buf.shape[2]
    total = None
    for s in range(n):
        piece = buf[s, rows].astype(F32)
        part = jnp.sum(piece * piece, axis=1, keepdims=True)
        total = part if total is None else total + part
    scale = lax.rsqrt(total / (n * cols) + EPS)
    if scale_ref is not None:
        scale_ref[rows if scale_rows is None else scale_rows, :] = scale
    for s in range(n):
        span = slice(s * cols, (s + 1) * cols)
        piece = buf[s, rows].astype(F32)
        out_ref[rows, span] = (piece * scale * gain_ref[:, span]).astype(BF16)


def spread_rows(n, buf, rows, out_ref):
    cols = buf.shape[2]
    for s in range(n):
        out_ref[rows, s * cols : (s + 1) * cols] = buf[s, rows]


def enter_kernel(n, n_seq, halo, x_ref, dy_ref, gain_ref, docs_ref, n1_ref, scale_ref, dyr_ref, window_ref, n1t_hbm, xall, dall, docs, n1t_ref, ts, xs, xr, ds, dr, hs, hr, ks, kr):
    tok = x_ref.shape[0]
    spot = lax.axis_index("seq")
    me = lax.axis_index("head")
    more = spot + 1 < n_seq
    for k in range(1, halo + 1):
        @pl.when(spot < k)
        def _():
            docs[halo - k] = jnp.zeros_like(docs_ref)

    docs[halo] = docs_ref[...]
    xall[me, halo * tok :] = x_ref[...]
    greet(*group(n), *along("seq", n_seq, range(1, n_seq)))
    xg = gatherer(n, 2 * (halo + 1), me, xall, xs, xr)
    dg = gatherer(n, 2, me, dall, ds, dr)

    def word(k):
        return push(
            docs.at[halo], docs.at[halo - k], ks.at[k - 1], kr.at[k - 1], seq=lax.rem(spot + k, n_seq)
        )

    def hop(j):
        here = pl.ds((halo - j + 1) * tok, tok)
        there = pl.ds((halo - j) * tok, tok)
        return push(
            xall.at[me, here], xall.at[me, there], hs.at[j - 1], hr.at[j - 1], seq=lax.rem(spot + 1, n_seq)
        )

    size = min(64, tok)
    per = tok // size

    def block_send(b):
        for c in (2 * b, 2 * b + 1):
            xg.send(c)

    def block_take(b):
        for c in (2 * b, 2 * b + 1):
            xg.relay(c)
        for c in (2 * b, 2 * b + 1):
            xg.take(c)
        own = b == halo

        @pl.loop(0, per)
        def _(i):
            rows = rows_of(b * per + i, size)
            if own:
                norm_rows(n, xall, rows, gain_ref, n1_ref, scale_ref, rows_of(i, size))
            else:
                norm_rows(n, xall, rows, gain_ref, n1_ref)

        rows = slice(b * tok, (b + 1) * tok)
        n1t_ref[:, rows] = n1_ref[rows, :].T

    if halo:
        @pl.when(more)
        def _():
            hop(1).start()

    block_send(halo)
    for k in range(1, halo + 1):
        @pl.when(spot + k < n_seq)
        def _():
            word(k).start()

    for j in range(1, halo + 1):
        @pl.when(spot >= j)
        def _():
            hop(j).wait_recv()

        if j < halo:
            @pl.when((spot >= j) & more)
            def _():
                hop(j + 1).start()

        @pl.when(spot >= j)
        def _():
            block_send(halo - j)

        if j == 1:
            block_take(halo)
        else:
            @pl.when(spot >= j - 1)
            def _():
                block_take(halo - j + 1)

    if not halo:
        block_take(halo)
    dg.send(0, dy_ref[: tok // 2, :])
    dg.send(1, dy_ref[tok // 2 :, :])
    if halo:
        @pl.when(spot >= halo)
        def _():
            block_take(0)

    for j in range(1, halo + 1):
        @pl.when(spot < j)
        def _():
            rows = slice((halo - j) * tok, (halo - j + 1) * tok)
            n1_ref[rows, :] = jnp.zeros((tok, n1_ref.shape[1]), BF16)
            n1t_ref[:, rows] = jnp.zeros((n1_ref.shape[1], tok), BF16)

    leave = pltpu.make_async_copy(n1t_ref, n1t_hbm, ts)
    leave.start()
    for k in range(1, halo + 1):
        @pl.when(spot >= k)
        def _():
            word(k).wait_recv()

    for k in range(halo + 1):
        window_ref[:, k * tok : (k + 1) * tok] = docs[k]
    for c in range(2):
        dg.relay(c)
    for c in range(2):
        dg.take(c)

    @pl.loop(0, per)
    def _(i):
        spread_rows(n, dall, rows_of(i, size), dyr_ref)

    for b in range(halo + 1):
        @pl.when(spot >= halo - b)
        def _():
            xg.finish(2 * b)
            xg.finish(2 * b + 1)

    for j in range(1, halo + 1):
        @pl.when((spot >= j - 1) & more)
        def _():
            hop(j).wait_send()

        @pl.when(spot + j < n_seq)
        def _():
            word(j).wait_send()

    dg.finish()
    leave.wait()


def projection_kernel(halo, n1t_ref, dq_ref, dk_ref, dv_ref, dh1r_ref, g_ref, dw_hbm, dh1t, held, sems):
    full, width = n1t_ref.shape[0], dq_ref.shape[1]
    tok = dq_ref.shape[0]
    size = min(256, full)

    def leave(i):
        return pltpu.make_async_copy(held.at[i], dw_hbm.at[:, i * width : (i + 1) * width], sems.at[i])

    def fill(i, left, right):
        @pl.loop(0, full // size)
        def _(t):
            rows = rows_of(t, size)
            held[i, rows] = mm(left[rows, :], right[...], NN).astype(BF16)

        leave(i).start()

    fill(0, n1t_ref.at[:, halo * tok :], dq_ref)
    fill(1, n1t_ref, dk_ref)
    fill(2, n1t_ref, dv_ref)
    dh1t[...] = dh1r_ref[...].T
    fill(3, dh1t, g_ref)
    for i in range(4):
        leave(i).wait()


def projection_grads(halo, n1t, dq, dk, dv, dh1r, g):
    full, (tok, width) = n1t.shape[0], dq.shape
    args = (n1t, dq, dk, dv, dh1r, g)
    return pl.pallas_call(
        functools.partial(projection_kernel, halo),
        out_shape=pltpu.HBM((full, 4 * width), BF16),
        in_specs=[whole()] * len(args),
        out_specs=pl.BlockSpec(memory_space=pltpu.HBM),
        scratch_shapes=[VMEM((full, tok), BF16), VMEM((4, full, width), BF16), dma(4)],
        cost_estimate=pl.CostEstimate(
            flops=4 * full * width * (n1t.shape[1] + tok),
            bytes_accessed=2 * full * (n1t.shape[1] + 4 * width),
            transcendentals=0,
        ),
        compiler_params=pltpu.CompilerParams(vmem_limit_bytes=40 * 2**20),
    )(*args)


def ffn_kernel(n2_ref, dy_ref, wg_ref, wu_ref, wd_ref, hid_ref, dgate_ref, dup_ref, dw_hbm, n2t, dyt, held, sems):
    j, steps = pl.program_id(0), pl.num_programs(0)

    @pl.when(j == 0)
    def _():
        n2t[...] = n2_ref[...].T
        dyt[...] = dy_ref[...].T

    size = wg_ref.shape[1]
    slot = lax.rem(j, 2)

    def leave(i, step, slot):
        start = pl.multiple_of((i * steps + step) * size, size)
        return pltpu.make_async_copy(held.at[slot, i], dw_hbm.at[:, pl.ds(start, size)], sems.at[slot, i])

    gate = mm(n2_ref[...], wg_ref[...], NN)
    upper = mm(n2_ref[...], wu_ref[...], NN)
    sigma = lax.logistic(gate)
    act = gate * sigma
    hid_ref[...] = (act * upper).astype(BF16)
    d_hid = mm(dy_ref[...], wd_ref[...], NN)
    dup_ref[...] = (d_hid * act).astype(BF16)
    dgate_ref[...] = (d_hid * upper * sigma * (1.0 + gate * (1.0 - sigma))).astype(BF16)

    @pl.when(j >= 2)
    def _():
        for i in range(3):
            leave(i, j - 2, slot).wait()

    for i, (left, right) in enumerate(((n2t, dgate_ref), (n2t, dup_ref), (dyt, hid_ref))):
        held[slot, i] = mm(left[...], right[...], NN).astype(BF16)
        leave(i, j, slot).start()

    @pl.when(j == steps - 1)
    def _():
        for i in range(3):
            leave(i, j, slot).wait()

        @pl.when(j >= 1)
        def _():
            for i in range(3):
                leave(i, j - 1, 1 - slot).wait()


def ffn(n2, dyr, w, tile):
    tok, full = n2.shape
    hidden = w.shape[1] // 3
    steps = hidden // tile
    act = pl.BlockSpec((tok, full), lambda j: (0, 0))
    part = pl.BlockSpec((tok, tile), lambda j: (0, j))
    return pl.pallas_call(
        ffn_kernel,
        grid=(steps,),
        out_shape=[pltpu.HBM((tok, hidden), BF16)] * 3
        + [pltpu.HBM((full, 3 * hidden), BF16)],
        in_specs=[act, act]
        + [pl.BlockSpec((full, tile), functools.partial(lambda i, j: (0, i * steps + j), i)) for i in range(3)],
        out_specs=[part] * 3 + [pl.BlockSpec(memory_space=pltpu.HBM)],
        scratch_shapes=[
            VMEM((full, tok), BF16),
            VMEM((full, tok), BF16),
            VMEM((2, 3, full, tile), BF16),
            dma(2, 3),
        ],
        cost_estimate=pl.CostEstimate(
            flops=12 * tok * full * hidden,
            bytes_accessed=12 * full * hidden,
            transcendentals=tok * hidden,
        ),
        compiler_params=pltpu.CompilerParams(vmem_limit_bytes=40 * 2**20),
    )(far_away(n2), far_away(dyr), *(far_away(w),) * 3)


def middle_kernel(n, nc, off, g_ref, w_hbm, x_ref, gain_ref, h1_ref, n2_ref, scale_ref, own, sbuf, rbuf, w_ref, hall, ws, s1, r1, s2, r2):
    load = fetch(w_hbm, off, w_ref, ws)
    greet(*group(n))
    me = lax.axis_index("head")
    red = reducer(n, own.shape[0] // nc, me, own, sbuf, rbuf, s1, r1)
    gat = gatherer(n, nc, me, hall, s2, r2)
    load.wait()
    red.send(0, nc, [(g_ref, 0, w_ref, 0)])
    red.relay(0, nc)
    for c in range(nc):
        rows = rows_of(c, red.size)
        h1 = red.take(c) + x_ref[rows, :].astype(F32)
        h1_ref[rows, :] = h1
        gat.send(c, h1.astype(BF16))
    size = min(64, red.size)
    for c in range(nc):
        gat.relay(c)
    for c in range(nc):
        gat.take(c)

        @pl.loop(0, red.size // size)
        def _(i):
            norm_rows(n, hall, pl.ds(pl.multiple_of(c * red.size + i * size, size), size), gain_ref, n2_ref, scale_ref)

    red.finish(0, nc)
    gat.finish()


class Stats:
    def __init__(self, n, nc, me, buf, ssem, rsem):
        self.n, self.nc, self.me = n, nc, me
        self.buf, self.ssem, self.rsem = buf, ssem, rsem

    def copy(self, k, c, source):
        return push(
            self.buf.at[source, c],
            self.buf.at[source, c],
            self.ssem.at[k - 1, c],
            self.rsem.at[k - 1, c],
            head=peer_of(self.me, k, self.n),
        )

    def send(self, c, value):
        size, cols = value.shape
        part = value[:, :128]
        for j in range(1, cols // 128):
            part = part + value[:, j * 128 : (j + 1) * 128]
        line = jnp.sum(part.T, axis=0, keepdims=True)
        self.buf[self.me, c] = jnp.broadcast_to(line, (8, size))
        for k in range(1, self.n):
            self.copy(k, c, self.me).start()

    def take(self, c):
        for k in range(1, self.n):
            self.copy(k, c, peer_of(self.me, self.n - k, self.n)).wait_recv()
        total = self.buf[0, c]
        for s in range(1, self.n):
            total = total + self.buf[s, c]
        size = total.shape[1]
        tall = jnp.broadcast_to(total[:1, :], (128, size))
        return tall.T[:, :1]

    def finish(self):
        for c in range(self.nc):
            for k in range(1, self.n):
                self.copy(k, c, self.me).wait_send()


def norm_back(nc, size, width, grad_of, keep, sta, unit_of, gain_ref, base_of, gain_grad_ref, done):
    for c in range(nc):
        rows = rows_of(c, size)
        grad = grad_of(c)
        keep[rows, :] = grad
        unit = unit_of(rows)
        part = jnp.sum(grad * unit, axis=0, keepdims=True)
        if c == 0:
            gain_grad_ref[...] = part
        else:
            gain_grad_ref[...] += part
        sta.send(c, grad * gain_ref[...] * unit)
    for c in range(nc):
        rows = rows_of(c, size)
        dots = sta.take(c) / width
        scaled = keep[rows, :] * gain_ref[...]
        done(c, rows, base_of(rows, scaled - unit_of(rows) * dots))


def back_kernel(n, nc, off, down, dgate_ref, dup_ref, hid_ref, w_hbm, h1_ref, scale_ref, gain_ref, dy_ref, dh1_ref, dh1r_ref, gain_grad_ref, *refs):
    output_ref = None
    if down is not None:
        output_ref, osum, osend, orecv, wd_ref, wds, s4, r4, *refs = refs
        load_down = fetch(w_hbm, down, wd_ref, wds)
    own, sbuf, rbuf, w_ref, stat, dall, ws, s1, r1, s2, r2, s3, r3 = refs
    load = fetch(w_hbm, off, w_ref, ws)
    greet(*group(n))
    me = lax.axis_index("head")
    pairs = [(dgate_ref, 0, w_ref, 0), (dup_ref, 0, w_ref, dgate_ref.shape[1])]
    size = own.shape[0] // nc
    red = reducer(n, size, me, own, sbuf, rbuf, s1, r1)
    sta = Stats(n, nc, me, stat, s2, r2)
    if down is not None:
        last = reducer(n, size, me, osum, osend, orecv, s4, r4)
    load.wait()
    gat = gatherer(n, nc, me, dall, s3, r3)
    red.send(0, nc, pairs)
    red.relay(0, nc)

    def unit_of(rows):
        return h1_ref[rows, :].astype(BF16).astype(F32) * scale_ref[rows, :]

    def base_of(rows, back):
        return dy_ref[rows, :] + scale_ref[rows, :] * back

    def done(c, rows, value):
        dh1_ref[rows, :] = value
        gat.send(c, value.astype(BF16))

    norm_back(nc, size, n * red.cols, red.take, own, sta, unit_of, gain_ref, base_of, gain_grad_ref, done)
    for c in range(nc):
        gat.relay(c)
    if down is not None:
        load_down.wait()
        last.send(0, nc, [(hid_ref, 0, wd_ref, 0)])
    for c in range(nc):
        gat.take(c)
        spread_rows(n, dall, rows_of(c, red.size), dh1r_ref)
    if down is not None:
        last.relay(0, nc)
        for c in range(nc):
            rows = rows_of(c, size)
            output_ref[rows, :] = (last.take(c) + h1_ref[rows, :]).astype(BF16)
        last.finish(0, nc)
    red.finish(0, nc)
    sta.finish()
    gat.finish()


def leave_kernel(n, n_seq, n_dp, halo, nc, dq_ref, dk_ref, dv_ref, w_hbm, x_ref, scale_ref, gain_ref, dh1_ref, gain_two_ref, group_ref, out_ref, sums_ref, own, sbuf, rbuf, w_ref, stat, gain_s, words, sums, zsend, zrecv, keep, ws, s1, r1, s2, r2, s3, r3, s4, r4, s5, r5):
    load = fetch(w_hbm, 0, w_ref, ws)
    spot, core = lax.axis_index("seq"), lax.axis_index("dp")
    others = [(i, j) for i in range(n_seq) for j in range(n_dp) if i or j]

    def of(i, j):
        return {"seq": lax.rem(spot + i, n_seq), "dp": lax.rem(core + j, n_dp)}

    def sends(j):
        return spot >= halo - j + 1

    def comes(j):
        return (spot + 1 < n_seq) & (spot + 1 >= halo - j + 1)

    for j in range(1, halo + 1):
        @pl.when(jnp.logical_not(comes(j)))
        def _():
            zrecv[j - 1] = jnp.zeros(zrecv.shape[1:], BF16)

    me = lax.axis_index("head")
    words[me] = group_ref[...]
    greet(*group(n), *(of(i, j) for i, j in others))
    tok, width = dq_ref.shape
    size = tok // nc
    red = reducer(n, size, me, own, sbuf, rbuf, s1, r1)
    sta = Stats(n, nc, me, stat, s2, r2)

    def word(k, source):
        return push(
            words.at[source], words.at[source], s3.at[k - 1], r3.at[k - 1], head=peer_of(me, k, n)
        )

    def hop(j, c):
        rows = pl.ds(c * size, size)
        return push(
            zsend.at[j - 1, rows], zrecv.at[j - 1, rows], s5.at[j - 1, c], r5.at[j - 1, c], seq=lax.rem(spot + n_seq - 1, n_seq)
        )

    for k in range(1, n):
        word(k, me).start()
    load.wait()
    pairs = [(dk_ref, 0, w_ref, width), (dv_ref, 0, w_ref, 2 * width)]
    for b in range(halo):
        @pl.when(sends(b + 1))
        def _():
            red.send(b * nc, (b + 1) * nc, pairs)

    red.send(halo * nc, (halo + 1) * nc, [(dq_ref, halo * nc, w_ref, 0)] + pairs)

    for b in range(halo):
        @pl.when(sends(b + 1))
        def _():
            red.relay(b * nc, (b + 1) * nc)

    red.relay(halo * nc, (halo + 1) * nc)

    def total(b, c):
        value = red.take(b * nc + c)
        if b == 0:
            return value

        @pl.when(comes(b))
        def _():
            hop(b, c).wait_recv()

        return value + zrecv[b - 1, pl.ds(c * size, size)].astype(F32)

    for j in range(1, halo + 1):
        for c in range(nc):
            @pl.when(sends(j))
            def _():
                zsend[j - 1, pl.ds(c * size, size)] = total(j - 1, c).astype(BF16)
                hop(j, c).start()

            if j > 1:
                @pl.when(jnp.logical_not(sends(j)) & comes(j - 1))
                def _():
                    hop(j - 1, c).wait_recv()

    def unit_of(rows):
        return x_ref[rows, :].astype(F32) * scale_ref[rows, :]

    def base_of(rows, back):
        return dh1_ref[rows, :] + scale_ref[rows, :] * back

    def done(c, rows, value):
        out_ref[rows, :] = value.astype(BF16)

    norm_back(nc, size, n * red.cols, functools.partial(total, halo), keep, sta, unit_of, gain_ref, base_of, gain_s, done)
    for k in range(1, n):
        word(k, peer_of(me, n - k, n)).wait_recv()
    total = words[0]
    for k in range(1, n):
        total = total + words[k]
    place = spot * n_dp + core
    mine = sums.at[place]
    cols = gain_s.shape[1]
    mine[...] = jnp.zeros((8, cols), F32)
    mine[0:1, :] = gain_s[...]
    mine[1:2, :] = gain_two_ref[...]
    mine[2:4, : total.shape[1]] = total[0:2]

    def share(t):
        i, j = others[t]
        return push(mine, mine, s4.at[t], r4.at[t], **of(i, j))

    def await_from(t):
        i, j = others[t]
        back = lax.rem(spot + n_seq - i, n_seq) * n_dp + lax.rem(core + n_dp - j, n_dp)
        theirs = sums.at[back]
        return push(theirs, theirs, s4.at[t], r4.at[t], **of(i, j))

    for t in range(len(others)):
        share(t).start()
    for t in range(len(others)):
        await_from(t).wait_recv()
    total = sums[0]
    for t in range(1, n_seq * n_dp):
        total = total + sums[t]
    sums_ref[...] = total
    for b in range(halo):
        @pl.when(sends(b + 1))
        def _():
            red.finish(b * nc, (b + 1) * nc)
            for c in range(nc):
                hop(b + 1, c).wait_send()

    red.finish(halo * nc, (halo + 1) * nc)
    sta.finish()
    for k in range(1, n):
        word(k, me).wait_send()
    for t in range(len(others)):
        share(t).wait_send()


def finish_kernel(n, n_seq, n_dp, halo, nc, off, n1t_hbm, w_hbm, wd_hbm, dq_ref, dk_ref, dv_ref, dh1r_ref, g_ref, hid_ref, h1_ref, x_ref, scale_ref, gain_ref, dh1_ref, gain_two_ref, group_ref, acts_ref, sums_ref, grads_ref, own, sbuf, rbuf, osum, osend, orecv, n1t_ref, w_ref, wd_ref, dh1t, mine, given, taken, sent, came, stat, gain_s, words, sums, zsend, zrecv, keep, load_sem, s1, r1, s2, r2, s3, r3, s4, r4, s5, r5, s6, r6, s7, r7, s8, rl, rr):
    loads = [
        fetch(n1t_hbm, 0, n1t_ref, load_sem.at[0]),
        fetch(w_hbm, 0, w_ref, load_sem.at[1]),
        fetch(wd_hbm, off, wd_ref, load_sem.at[2]),
    ]
    spot, core = lax.axis_index("seq"), lax.axis_index("dp")
    me = lax.axis_index("head")
    tok, width = dq_ref.shape
    size = tok // nc
    share = mine.shape[1]
    others = [(i, j) for i in range(n_seq) for j in range(n_dp) if i or j]

    def of(i, j):
        return {"seq": lax.rem(spot + i, n_seq), "dp": lax.rem(core + j, n_dp)}

    def sends(j):
        return spot >= halo - j + 1

    def comes(j):
        return (spot + 1 < n_seq) & (spot + 1 >= halo - j + 1)

    for j in range(1, halo + 1):
        @pl.when(jnp.logical_not(comes(j)))
        def _():
            zrecv[j - 1] = jnp.zeros(zrecv.shape[1:], BF16)

    words[me] = group_ref[...]
    dh1t[...] = dh1r_ref[...].T
    greet(*group(n), *(of(i, j) for i, j in others))
    red = reducer(n, size, me, own, sbuf, rbuf, s1, r1)
    sta = Stats(n, nc, me, stat, s2, r2)
    last = reducer(n, size, me, osum, osend, orecv, s6, r6)

    def word(k, source):
        return push(
            words.at[source], words.at[source], s3.at[k - 1], r3.at[k - 1], head=peer_of(me, k, n)
        )

    def hop(j, c):
        rows = pl.ds(c * size, size)
        return push(
            zsend.at[j - 1, rows], zrecv.at[j - 1, rows], s5.at[j - 1, c], r5.at[j - 1, c], seq=lax.rem(spot + n_seq - 1, n_seq)
        )

    for k in range(1, n):
        word(k, me).start()

    def block_grads(i, c, ref):
        rows = rows_of(i * n_dp + c, share)
        ref[:, :width] = mm(n1t_ref[rows, halo * tok :], dq_ref[...], NN).astype(ref.dtype)
        ref[:, width : 2 * width] = mm(n1t_ref[rows, :], dk_ref[...], NN).astype(ref.dtype)
        ref[:, 2 * width : 3 * width] = mm(n1t_ref[rows, :], dv_ref[...], NN).astype(ref.dtype)
        ref[:, 3 * width :] = mm(dh1t[rows, :], g_ref[...], NN).astype(ref.dtype)

    def give(k, i):
        return push(
            given.at[k - 1, i], taken.at[k - 1, i], s7.at[k - 1, i], r7.at[k - 1, i], dp=lax.rem(core + k, n_dp)
        )

    def block_relay(b):
        if b == halo:
            red.relay(b * nc, (b + 1) * nc)
        else:
            @pl.when(sends(b + 1))
            def _():
                red.relay(b * nc, (b + 1) * nc)

    loads[1].wait()
    pairs = [(dk_ref, 0, w_ref, width), (dv_ref, 0, w_ref, 2 * width)]
    for b in range(halo):
        @pl.when(sends(b + 1))
        def _():
            red.send(b * nc, (b + 1) * nc, pairs)

    loads[0].wait()
    for k in range(1, n_dp):

        @pl.loop(0, n_seq)
        def _(i):
            block_grads(i, lax.rem(core + k, n_dp), given.at[k - 1, i])
            give(k, i).start()

    @pl.loop(0, n_seq)
    def _(i):
        block_grads(i, core, mine.at[i])

    half = mine.shape[2] // 2

    def chip(d, p):
        cols = slice(p * half, (p + 1) * half)
        value = mine[d, :, cols]
        for k in range(1, n_dp):
            if p == 0:
                give(k, d).wait_recv()
            value = value + taken[k - 1, d, :, cols].astype(F32)
        return value

    def piece(d, p, slot, sem, to):
        cols = slice(p * half, (p + 1) * half)
        return push(sent.at[d, :, cols], came.at[slot, :, cols], s8.at[d, p], sem.at[d, p], seq=to)

    def right(d, p):
        return piece(d, p, d, rl, lax.rem(spot + 1, n_seq))

    def left(d, p):
        return piece(d, p, jnp.where(spot - 1 == d, n_seq, d), rr, lax.rem(spot + n_seq - 1, n_seq))

    def arrived(d, p, slot, sem):
        return piece(d, p, slot, sem, lax.rem(spot + 1, n_seq))

    def start_line(i, p):
        cols = slice(p * half, (p + 1) * half)
        d = n_seq - 1 - i

        @pl.when(spot == 0)
        def _():
            if i:
                right(d + 1, p).wait_send()
            sent[d, :, cols] = chip(d, p).astype(BF16)
            right(d, p).start()

        @pl.when(spot == n_seq - 1)
        def _():
            if i:
                left(i - 1, p).wait_send()
            sent[i, :, cols] = chip(i, p).astype(BF16)
            left(i, p).start()

    def pass_line(i, p):
        cols = slice(p * half, (p + 1) * half)
        d = n_seq - 1 - i

        @pl.when((spot > 0) & (d > spot))
        def _():
            arrived(d, p, d, rl).wait_recv()
            sent[d, :, cols] = (chip(d, p) + came[d, :, cols].astype(F32)).astype(BF16)
            right(d, p).start()

        @pl.when((spot < n_seq - 1) & (i < spot))
        def _():
            arrived(i, p, i, rr).wait_recv()
            sent[i, :, cols] = (chip(i, p) + came[i, :, cols].astype(F32)).astype(BF16)
            left(i, p).start()

    def total(b, c):
        value = red.take(b * nc + c)
        if b == 0:
            return value

        @pl.when(comes(b))
        def _():
            hop(b, c).wait_recv()

        return value + zrecv[b - 1, pl.ds(c * size, size)].astype(F32)

    def send_hop(j):
        for c in range(nc):
            @pl.when(sends(j))
            def _():
                zsend[j - 1, pl.ds(c * size, size)] = total(j - 1, c).astype(BF16)
                hop(j, c).start()

            if j > 1:
                @pl.when(jnp.logical_not(sends(j)) & comes(j - 1))
                def _():
                    hop(j - 1, c).wait_recv()

    for p in range(2):
        if n_seq > 1:
            start_line(0, p)
    for b in range(halo):
        block_relay(b)
    red.send(halo * nc, (halo + 1) * nc, [(dq_ref, halo * nc, w_ref, 0)] + pairs)
    for t in range(max(n_seq - 1, 1)):
        if t < halo:
            send_hop(t + 1)
        for p in range(2):
            if t < n_seq - 1:
                pass_line(t, p)
            if t + 1 < n_seq - 1:
                start_line(t + 1, p)
        if t == 0:
            block_relay(halo)
            loads[2].wait()
            last.send(0, nc, [(hid_ref, 0, wd_ref, 0)])

    def unit_of(rows):
        return x_ref[rows, :].astype(F32) * scale_ref[rows, :]

    def base_of(rows, back):
        return dh1_ref[rows, :] + scale_ref[rows, :] * back

    def done(c, rows, value):
        acts_ref[0, rows, :] = value.astype(BF16)

    norm_back(nc, size, n * red.cols, functools.partial(total, halo), keep, sta, unit_of, gain_ref, base_of, gain_s, done)
    for k in range(1, n):
        word(k, peer_of(me, n - k, n)).wait_recv()
    group_sum = words[0]
    for k in range(1, n):
        group_sum = group_sum + words[k]
    place = spot * n_dp + core
    slip = sums.at[place]
    cols = gain_s.shape[1]
    slip[...] = jnp.zeros((8, cols), F32)
    slip[0:1, :] = gain_s[...]
    slip[1:2, :] = gain_two_ref[...]
    slip[2:4, : group_sum.shape[1]] = group_sum[0:2]

    def hand(t):
        i, j = others[t]
        return push(slip, slip, s4.at[t], r4.at[t], **of(i, j))

    def handed(t):
        i, j = others[t]
        back = lax.rem(spot + n_seq - i, n_seq) * n_dp + lax.rem(core + n_dp - j, n_dp)
        theirs = sums.at[back]
        return push(theirs, theirs, s4.at[t], r4.at[t], **of(i, j))

    for t in range(len(others)):
        hand(t).start()
    last.relay(0, nc)
    for c in range(nc):
        rows = rows_of(c, size)
        acts_ref[1, rows, :] = (last.take(c) + h1_ref[rows, :]).astype(BF16)
    for p in range(2):
        cols = slice(p * half, (p + 1) * half)
        mine[spot, :, cols] = chip(spot, p)

        @pl.when(spot > 0)
        def _():
            arrived(spot, p, spot, rl).wait_recv()
            mine[spot, :, cols] = mine[spot, :, cols] + came[spot, :, cols].astype(F32)

        @pl.when(spot < n_seq - 1)
        def _():
            arrived(spot, p, n_seq, rr).wait_recv()
            mine[spot, :, cols] = mine[spot, :, cols] + came[n_seq, :, cols].astype(F32)

    grads_ref[...] = mine[spot]
    for t in range(len(others)):
        handed(t).wait_recv()
    full_sum = sums[0]
    for t in range(1, n_seq * n_dp):
        full_sum = full_sum + sums[t]
    sums_ref[...] = full_sum
    for b in range(halo):
        @pl.when(sends(b + 1))
        def _():
            red.finish(b * nc, (b + 1) * nc)
            for c in range(nc):
                hop(b + 1, c).wait_send()

    red.finish(halo * nc, (halo + 1) * nc)
    last.finish(0, nc)
    sta.finish()
    for k in range(1, n):
        word(k, me).wait_send()
    for t in range(len(others)):
        hand(t).wait_send()
    for k in range(1, n_dp):
        for i in range(n_seq):
            give(k, i).wait_send()
    for d in range(n_seq):
        for p in range(2):

            @pl.when((spot < d) & ((spot > 0) | (d == 1)))
            def _():
                right(d, p).wait_send()

            @pl.when((spot > d) & ((spot < n_seq - 1) | (d == n_seq - 2)))
            def _():
                left(d, p).wait_send()


def far_away(x):
    return pltpu.with_memory_space_constraint(x, pltpu.HBM)


def dma(*dims):
    return pltpu.SemaphoreType.DMA(dims)


def talk(kernel, ident, outs, scratch, flops, room, args, far=(), far_outs=(), kept=(), kept_outs=()):
    return pl.pallas_call(
        kernel,
        out_shape=[
            pltpu.HBM(s, d) if i in far_outs or i in kept_outs else jax.ShapeDtypeStruct(s, d)
            for i, (s, d) in enumerate(outs)
        ],
        in_specs=[
            pl.BlockSpec(memory_space=pltpu.HBM) if i in far else whole() for i in range(len(args))
        ],
        out_specs=[
            pl.BlockSpec(memory_space=pltpu.HBM) if i in far_outs else whole()
            for i in range(len(outs))
        ],
        scratch_shapes=scratch,
        cost_estimate=pl.CostEstimate(flops=flops, bytes_accessed=40 * 2**20, transcendentals=0),
        compiler_params=pltpu.CompilerParams(
            collective_id=ident, has_side_effects=True, vmem_limit_bytes=room * 2**20
        ),
    )(*(far_away(a) if i in far or i in kept else a for i, a in enumerate(args)))


def forward_kernel(base, nb_ref, lam_ref, q_ref, k_ref, v_ref, start_ref, gain_ref, o1_ref, o2_ref, lse_ref, g_ref, held, m_s, l_s, acc):
    size = q_ref.shape[0]
    qt = pl.program_id(1)
    q = q_ref[...] * 0.125
    lane = lax.broadcasted_iota(jnp.int32, q.shape, 1)
    zero = jnp.zeros_like(q)
    parts = (jnp.where(lane < HALF, q, zero), jnp.where(lane >= HALF, q, zero))
    key = lax.broadcasted_iota(jnp.int32, (size, size), 0)
    query = lax.broadcasted_iota(jnp.int32, (size, size), 1)
    start = start_ref[...]

    count = nb_ref[qt]

    def scores(d, first):
        where = base + qt - d
        k = k_ref[rows_of(where, size), :]
        allowed = key >= start - where * size
        if first:
            allowed = allowed & (key <= query)
        for m in range(2):
            s = jnp.where(allowed, mm(k, parts[m], NT), NEG_BIG)
            held[d, m] = s
            top = jnp.max(s, axis=0, keepdims=True)
            m_s[m] = top if first else jnp.maximum(m_s[m], top)

    def weights(d, _):
        for m in range(2):
            e = jnp.exp(held[d, m] - m_s[m])
            held[d, m] = e
            l_s[m] += jnp.sum(e, axis=0, keepdims=True)
        return 0

    def mix(d, first):
        v = v_ref[rows_of(base + qt - d, size), :]
        for m in range(2):
            term = mm(v, (held[d, m] * l_s[m]).astype(BF16), TN)
            if first:
                acc[m] = term
            else:
                acc[m] += term

    def each(step):
        def body(d, _):
            step(d, False)
            return 0

        step(0, True)
        lax.fori_loop(1, count, body, 0)

    each(scores)
    l_s[...] = jnp.zeros_like(l_s)
    lax.fori_loop(0, count, weights, 0)
    for m in range(2):
        lse_ref[0, m : m + 1, :] = m_s[m] + jnp.log(l_s[m])
        l_s[m] = 1.0 / l_s[m]
    each(mix)
    o1, o2 = acc[0], acc[1]
    o1_ref[...] = o1
    o2_ref[...] = o2
    diff = o1 - lam_ref[0] * o2
    scale = lax.rsqrt(jnp.mean(diff * diff, axis=0, keepdims=True) + EPS)
    g = diff * scale * gain_ref[...] * KEEP
    g_ref[...] = g.T.astype(BF16)


def backward_kernel(base, nb_ref, lam_ref, q_ref, k_ref, v_ref, start_ref, gain_ref, o1_ref, o2_ref, lse_ref, dg_ref, dq_ref, dk_ref, dv_ref, gain_grad_ref, lam_grad_ref, dq_s, dk_s, dv_s):
    size = q_ref.shape[0]
    h, qt = pl.program_id(0), pl.program_id(1)
    lam = lam_ref[0]

    @pl.when((h == 0) & (qt == 0))
    def _():
        gain_grad_ref[...] = jnp.zeros_like(gain_grad_ref)
        lam_grad_ref[...] = jnp.zeros_like(lam_grad_ref)

    @pl.when(qt == 0)
    def _():
        dk_s[...] = jnp.zeros_like(dk_s)
        dv_s[...] = jnp.zeros_like(dv_s)

    o1, o2 = o1_ref[...], o2_ref[...]
    diff = o1 - lam * o2
    scale = lax.rsqrt(jnp.mean(diff * diff, axis=0, keepdims=True) + EPS)
    unit = diff * scale
    dg = dg_ref[...].T
    gain_grad_ref[...] += jnp.sum(dg * unit, axis=1, keepdims=True) * KEEP
    du = dg * gain_ref[...] * KEEP
    do = scale * (du - unit * jnp.mean(du * unit, axis=0, keepdims=True))
    lam_grad_ref[...] -= jnp.sum(do * o2, axis=1, keepdims=True)
    grads = (do.astype(BF16), (-lam * do).astype(BF16))
    deltas = tuple(
        jnp.sum(g.astype(F32) * o, axis=0, keepdims=True) for g, o in zip(grads, (o1, o2))
    )
    q = q_ref[...] * 0.125
    lane = lax.broadcasted_iota(jnp.int32, q.shape, 1)
    zero = jnp.zeros_like(q)
    parts = (jnp.where(lane < HALF, q, zero), jnp.where(lane >= HALF, q, zero))
    key = lax.broadcasted_iota(jnp.int32, (size, size), 0)
    query = lax.broadcasted_iota(jnp.int32, (size, size), 1)
    start = start_ref[...]
    dq_s[...] = jnp.zeros_like(dq_s)

    def block(where, first):
        rows = rows_of(where, size)
        k, v = k_ref[rows, :], v_ref[rows, :]
        halves = (jnp.where(lane < HALF, k, zero), jnp.where(lane >= HALF, k, zero))
        allowed = key >= start - where * size
        if first:
            allowed = allowed & (key <= query)
        dq = dq_s[...]
        dk = dk_s[rows, :]
        dv = dv_s[rows, :]
        for m in range(2):
            s = mm(k, parts[m], NT)
            p = jnp.where(allowed, jnp.exp(s - lse_ref[0, m : m + 1, :]), 0.0)
            dp = mm(v, grads[m], NN)
            ds = (p * (dp - deltas[m])).astype(BF16)
            dq = dq + mm(halves[m], ds, TN)
            dk = dk + mm(ds, parts[m], NN)
            dv = dv + mm(p.astype(BF16), grads[m], NT)
        dq_s[...] = dq
        dk_s[rows, :] = dk
        dv_s[rows, :] = dv

    block(base + qt, True)

    def earlier(d, _):
        block(base + qt - d, False)
        return 0

    lax.fori_loop(1, nb_ref[qt], earlier, 0)
    dq_ref[...] = (dq_s[...] * 0.125).T.astype(BF16)

    @pl.when(qt == pl.num_programs(1) - 1)
    def _():
        dk_ref[...] = dk_s[...].astype(BF16)
        dv_ref[...] = dv_s[...].astype(BF16)


SMEM = pl.BlockSpec(memory_space=pltpu.SMEM)
TILE = 256


def attend(q, kv, start, nb, lam, gain_col):
    tok, width = q.shape
    heads = width // VDIM
    rows = kv.shape[0]
    size = min(TILE, tok)
    base = (rows - tok) // size
    head_block = pl.BlockSpec((VDIM, size), lambda h, t: (h, t))
    return pl.pallas_call(
        functools.partial(forward_kernel, base),
        grid=(heads, tok // size),
        out_shape=[
            jax.ShapeDtypeStruct((width, tok), F32),
            jax.ShapeDtypeStruct((width, tok), F32),
            jax.ShapeDtypeStruct((heads, 2, tok), F32),
            jax.ShapeDtypeStruct((tok, width), BF16),
        ],
        in_specs=[
            SMEM,
            SMEM,
            pl.BlockSpec((size, VDIM), lambda h, t: (t, h)),
            pl.BlockSpec((rows, VDIM), lambda h, t: (0, h)),
            pl.BlockSpec((rows, VDIM), lambda h, t: (0, heads + h)),
            pl.BlockSpec((1, size), lambda h, t: (0, t)),
            pl.BlockSpec((VDIM, 1), lambda h, t: (0, 0)),
        ],
        out_specs=[
            head_block,
            head_block,
            pl.BlockSpec((1, 2, size), lambda h, t: (h, 0, t)),
            pl.BlockSpec((size, VDIM), lambda h, t: (t, h)),
        ],
        scratch_shapes=[
            VMEM((rows // size, 2, size, size), F32),
            VMEM((2, 1, size), F32),
            VMEM((2, 1, size), F32),
            VMEM((2, VDIM, size), F32),
        ],
        cost_estimate=pl.CostEstimate(
            flops=4 * tok * rows * heads * VDIM,
            bytes_accessed=8 * tok * width + 4 * rows * width,
            transcendentals=2 * tok * rows * heads,
        ),
        compiler_params=pltpu.CompilerParams(vmem_limit_bytes=32 * 2**20),
    )(nb, lam, q, kv, kv, start, gain_col)


def halo_room(rows, tok):
    return 2 * (rows // tok)


def attend_back(q, kv, start, nb, lam, gain_col, o1, o2, lse, dg):
    tok, width = q.shape
    heads = width // VDIM
    rows = kv.shape[0]
    size = min(TILE, tok)
    base = (rows - tok) // size
    head_block = pl.BlockSpec((VDIM, size), lambda h, t: (h, t))
    return pl.pallas_call(
        functools.partial(backward_kernel, base),
        grid=(heads, tok // size),
        out_shape=[
            pltpu.HBM((tok, width), BF16),
            pltpu.HBM((rows, width), BF16),
            pltpu.HBM((rows, width), BF16),
            jax.ShapeDtypeStruct((VDIM, 1), F32),
            jax.ShapeDtypeStruct((VDIM, 1), F32),
        ],
        in_specs=[
            SMEM,
            SMEM,
            pl.BlockSpec((size, VDIM), lambda h, t: (t, h)),
            pl.BlockSpec((rows, VDIM), lambda h, t: (0, h)),
            pl.BlockSpec((rows, VDIM), lambda h, t: (0, heads + h)),
            pl.BlockSpec((1, size), lambda h, t: (0, t)),
            pl.BlockSpec((VDIM, 1), lambda h, t: (0, 0)),
            head_block,
            head_block,
            pl.BlockSpec((1, 2, size), lambda h, t: (h, 0, t)),
            pl.BlockSpec((size, VDIM), lambda h, t: (t, h)),
        ],
        out_specs=[
            pl.BlockSpec((size, VDIM), lambda h, t: (t, h)),
            pl.BlockSpec((rows, VDIM), lambda h, t: (0, h)),
            pl.BlockSpec((rows, VDIM), lambda h, t: (0, h)),
            pl.BlockSpec((VDIM, 1), lambda h, t: (0, 0)),
            pl.BlockSpec((VDIM, 1), lambda h, t: (0, 0)),
        ],
        scratch_shapes=[
            VMEM((VDIM, size), F32),
            VMEM((rows, VDIM), F32),
            VMEM((rows, VDIM), F32),
        ],
        cost_estimate=pl.CostEstimate(
            flops=10 * tok * rows * heads * VDIM,
            bytes_accessed=16 * tok * width + 8 * rows * width,
            transcendentals=2 * tok * rows * heads,
        ),
        compiler_params=pltpu.CompilerParams(vmem_limit_bytes=(12 + halo_room(rows, tok)) * 2**20),
    )(nb, lam, q, kv, kv, start, gain_col, o1, o2, lse, dg)


CHUNKS = 2


def on_device(
    n_head,
    n_seq,
    n_dp,
    inputs,
    w_query,
    w_key,
    w_value,
    w_output,
    w_gate,
    w_up,
    w_down,
    gain_attn,
    gain_ffn,
    group_gain,
    lambda_q1,
    lambda_k1,
    lambda_q2,
    lambda_k2,
    doc_ids,
    needles,
    out_grad,
):
    x = inputs[0]
    tok, cols = x.shape
    n, nc = n_head, CHUNKS
    full = n * cols
    width = w_query.shape[1]
    hidden = w_gate.shape[1]
    me = lax.axis_index("head")
    halo = n_seq // 2

    w_attn = lax.all_gather(
        jnp.concatenate([w_query, w_key, w_value, w_output], axis=1),
        ("seq", "dp"),
        axis=0,
        tiled=True,
    )
    w_ffn = lax.all_gather(
        jnp.concatenate([w_gate, w_up, w_down], axis=1), ("seq", "dp"), axis=0, tiled=True
    )

    weight = jnp.where(needles[0] == 1, 1.0, 0.1).astype(F32)
    dy = out_grad[0].astype(F32) * weight[:, None]
    gain_one = gain_attn[None, :]
    gain_two = gain_ffn[None, :]
    gain_one_cols = lax.dynamic_slice_in_dim(gain_one, me * cols, cols, 1)
    gain_two_cols = lax.dynamic_slice_in_dim(gain_two, me * cols, cols, 1)
    lam = jnp.exp(jnp.sum(lambda_q1 * lambda_k1)) - jnp.exp(jnp.sum(lambda_q2 * lambda_k2))
    lam = (lam + LAMBDA_INIT)[None]
    gain_col = group_gain[:, None]

    docs = jnp.broadcast_to(doc_ids + 1, (8, tok))
    n1, scale_one, dyr, window, n1t = talk(
        functools.partial(enter_kernel, n, n_seq, halo),
        0,
        [
            (((halo + 1) * tok, full), BF16),
            ((tok, 1), F32),
            ((tok, full), BF16),
            ((8, (halo + 1) * tok), jnp.int32),
            ((full, (halo + 1) * tok), BF16),
        ],
        [
            VMEM((n, (halo + 1) * tok, cols), BF16),
            VMEM((n, tok, cols), BF16),
            VMEM((halo + 1, 8, tok), jnp.int32),
            VMEM((full, (halo + 1) * tok), BF16),
            pltpu.SemaphoreType.DMA,
        ]
        + [dma(n - 1, 2 * (halo + 1))] * 2
        + [dma(n - 1, 2)] * 2
        + [dma(max(halo, 1))] * 4,
        tok * full * 8,
        14 + 4 * (halo + 1),
        (x, dy.astype(BF16), gain_one, docs),
        far_outs=(4,),
        kept_outs=(2,),
    )
    start = jnp.sum((window[0][None, :] < docs[0][:, None]).astype(jnp.int32), axis=1)
    size = min(TILE, tok)
    base = halo * tok // size
    first = start[::size]
    nb = base + jnp.arange(tok // size, dtype=jnp.int32) - first // size + 1
    start = start[None, :]

    q = jnp.dot(n1[halo * tok :], w_attn[:, :width], preferred_element_type=F32).astype(BF16)
    kv = jnp.dot(n1, w_attn[:, width : 3 * width], preferred_element_type=F32).astype(BF16)
    o1, o2, lse, grouped = attend(q, kv, start, nb, lam, gain_col)

    exchange = [VMEM((tok, cols), F32), VMEM((n - 1, tok, cols), BF16), VMEM((n - 1, tok, cols), BF16)]
    h1, n2, scale_two = talk(
        functools.partial(middle_kernel, n, nc, 3 * width),
        1,
        [((tok, cols), F32), ((tok, full), BF16), ((tok, 1), F32)],
        exchange
        + [VMEM((full, width), BF16), VMEM((n, tok, cols), BF16), pltpu.SemaphoreType.DMA]
        + [dma(n - 1, nc)] * 4,
        2 * tok * full * width,
        14,
        (grouped, w_attn, x, gain_two),
        far=(1,),
        kept_outs=(1,),
    )
    tile = min(2 * TILE, hidden)
    inner, d_gate, d_up, d_wffn = ffn(n2, dyr, w_ffn, tile)
    g_ffn = lax.psum_scatter(d_wffn, ("seq", "dp"), scatter_dimension=0, tiled=True)

    stat = VMEM((n, nc, 8, tok // nc), F32)
    early = halo > 2
    dh1, dh1r, gain_two_part, *output = talk(
        functools.partial(back_kernel, n, nc, 0, 2 * hidden if early else None),
        2,
        [((tok, cols), F32), ((tok, full), BF16), ((1, cols), F32)]
        + [((tok, cols), BF16)] * early,
        (exchange + [VMEM((full, hidden), BF16), pltpu.SemaphoreType.DMA] + [dma(n - 1, nc)] * 2)
        * early
        + exchange
        + [
            VMEM((full, 2 * hidden), BF16),
            stat,
            VMEM((n, tok, cols), BF16),
            pltpu.SemaphoreType.DMA,
        ]
        + [dma(n - 1, nc)] * 6,
        4 * tok * full * hidden,
        26,
        (d_gate, d_up, inner, w_ffn, h1, scale_two, gain_two_cols, dy),
        far=(3,),
        kept=(0, 1, 2),
    )
    dg = jnp.dot(dh1r, w_attn[:, 3 * width :], preferred_element_type=F32)
    dq, dk, dv, group_part, lam_part = attend_back(
        q, kv, start, nb, lam, gain_col, o1, o2, lse, dg
    )
    group_words = jnp.concatenate(
        [
            group_part.T,
            jnp.broadcast_to(jnp.sum(lam_part), (1, VDIM)),
            jnp.zeros((6, VDIM), F32),
        ]
    )
    others = n_seq * n_dp - 1
    span = (halo + 1) * tok
    if halo <= 2:
        rows = w_query.shape[0]
        line = (n_seq, rows, 4 * width)
        acts, sums, g_attn = talk(
            functools.partial(finish_kernel, n, n_seq, n_dp, halo, nc, 2 * hidden),
            3,
            [((2, tok, cols), BF16), ((8, cols), F32), ((rows, 4 * width), F32)],
            [
                VMEM((span, cols), F32),
                VMEM((n - 1, span, cols), BF16),
                VMEM((n - 1, span, cols), BF16),
            ]
            + exchange
            + [
                VMEM((full, span), BF16),
                VMEM((full, 3 * width), BF16),
                VMEM((full, hidden), BF16),
                VMEM((full, tok), BF16),
                VMEM(line, F32),
                VMEM((max(n_dp - 1, 1),) + line, BF16),
                VMEM((max(n_dp - 1, 1),) + line, BF16),
                VMEM(line, BF16),
                VMEM((n_seq + 1, rows, 4 * width), BF16),
                stat,
                VMEM((1, cols), F32),
                VMEM((n, 8, VDIM), F32),
                VMEM((others + 1, 8, cols), F32),
                VMEM((max(halo, 1), tok, cols), BF16),
                VMEM((max(halo, 1), tok, cols), BF16),
                VMEM((tok, cols), F32),
                dma(3),
            ]
            + [dma(n - 1, (halo + 1) * nc)] * 2
            + [dma(n - 1, nc)] * 2
            + [dma(n - 1)] * 2
            + [dma(max(others, 1))] * 2
            + [dma(max(halo, 1), nc)] * 2
            + [dma(n - 1, nc)] * 2
            + [dma(max(n_dp - 1, 1), n_seq)] * 2
            + [dma(n_seq, 2)] * 3,
            6 * tok * full * width * (halo + 1),
            58,
            (n1t, w_attn, w_ffn, dq, dk, dv, dh1r, grouped, inner, h1, x, scale_one, gain_one_cols, dh1, gain_two_part, group_words),
            far=(0, 1, 2),
            kept=(3, 4, 5, 8),
        )
        input_grad, output = acts[0], acts[1]
    else:
        d_wattn = projection_grads(halo, n1t, dq, dk, dv, dh1r, grouped)
        d_wattn, g_ffn = lax.optimization_barrier((d_wattn, g_ffn))
        g_attn = lax.psum_scatter(d_wattn, ("seq", "dp"), scatter_dimension=0, tiled=True).astype(F32)
        input_grad, sums = talk(
            functools.partial(leave_kernel, n, n_seq, n_dp, halo, nc),
            3,
            [((tok, cols), BF16), ((8, cols), F32)],
            [
                VMEM((span, cols), F32),
                VMEM((n - 1, span, cols), BF16),
                VMEM((n - 1, span, cols), BF16),
                VMEM((full, 3 * width), BF16),
                stat,
                VMEM((1, cols), F32),
                VMEM((n, 8, VDIM), F32),
                VMEM((others + 1, 8, cols), F32),
                VMEM((max(halo, 1), tok, cols), BF16),
                VMEM((max(halo, 1), tok, cols), BF16),
                VMEM((tok, cols), F32),
                pltpu.SemaphoreType.DMA,
            ]
            + [dma(n - 1, (halo + 1) * nc)] * 2
            + [dma(n - 1, nc)] * 2
            + [dma(n - 1)] * 2
            + [dma(max(others, 1))] * 2
            + [dma(max(halo, 1), nc)] * 2,
            6 * tok * full * width * (halo + 1),
            26 + 5 * halo,
            (dq, dk, dv, w_attn, x, scale_one, gain_one_cols, dh1, gain_two_part, group_words),
            far=(3,),
        )
        (output,) = output
    g_query, g_key, g_value, g_output = (
        g_attn[:, i * width : (i + 1) * width] for i in range(4)
    )
    g_ffn = g_ffn.astype(F32)
    share = cols // (n_seq * n_dp)
    place = lax.axis_index("seq") * n_dp + lax.axis_index("dp")
    gains = lax.dynamic_slice_in_dim(sums[:2], place * share, share, 1)
    return (
        output[None],
        input_grad[None],
        gains[0],
        gains[1],
        sums[2, :VDIM],
        sums[3, :1],
        g_query,
        g_key,
        g_value,
        g_output,
        g_ffn[:, :hidden],
        g_ffn[:, hidden : 2 * hidden],
        g_ffn[:, 2 * hidden :],
    )


def solution(mesh):
    act = P("dp", "seq", "head")
    mat = P(("seq", "dp"), "head")
    vec = P(("head", "seq", "dp"))
    return jax.shard_map(
        functools.partial(on_device, mesh.shape["head"], mesh.shape["seq"], mesh.shape["dp"]),
        mesh=mesh,
        in_specs=(act,) + (mat,) * 7 + (P(),) * 7 + (P("dp", "seq"),) * 2 + (act,),
        out_specs=(act, act, vec, vec, P(), P()) + (mat,) * 7,
        check_vma=False,
    )
```

```python
import functools
import math

import jax
import jax.numpy as jnp
from jax import lax
from jax.experimental import pallas as pl
from jax.experimental.pallas import tpu as pltpu
from jax.sharding import PartitionSpec as P

HALF = 64
VDIM = 128
EPS = 1e-05
LAMBDA_INIT = 0.8 - 0.6 * math.exp(-0.3)
KEEP = 1.0 - LAMBDA_INIT
NEG_BIG = -1e30
MESH = pl.DeviceIdType.MESH
VMEM = pltpu.VMEM
F32 = jnp.float32
BF16 = jnp.bfloat16
NN = (((1,), (0,)), ((), ()))
NT = (((1,), (1,)), ((), ()))
TN = (((0,), (0,)), ((), ()))


def mm(a, b, dims):
    return lax.dot_general(a, b, dims, preferred_element_type=F32)


def whole():
    return pl.BlockSpec(memory_space=VMEM)


def peer_of(me, k, n):
    return lax.rem(me + k, n)


def greet(*peers):
    barrier = pltpu.get_barrier_semaphore()
    for peer in peers:
        pl.semaphore_signal(barrier, 1, device_id=peer, device_id_type=MESH)
    pl.semaphore_wait(barrier, len(peers))


def along(axis, size, steps):
    spot = lax.axis_index(axis)
    return [{axis: lax.rem(spot + k, size)} for k in steps]


def group(n):
    return along("head", n, range(1, n))


def push(src, dst, send, recv, **peer):
    return pltpu.make_async_remote_copy(
        src_ref=src,
        dst_ref=dst,
        send_sem=send,
        recv_sem=recv,
        device_id=peer,
        device_id_type=MESH,
    )


def rows_of(c, size):
    return pl.ds(pl.multiple_of(c * size, size), size)


def fetch(w_hbm, off, w_ref, sem):
    copy = pltpu.make_async_copy(w_hbm.at[:, off : off + w_ref.shape[1]], w_ref, sem)
    copy.start()
    return copy


class Reduce:
    def __init__(self, n, size, me, own_ref, sbuf, rbuf, ssem, rsem):
        self.n, self.size, self.me = n, size, me
        self.own_ref, self.sbuf, self.rbuf, self.ssem, self.rsem = own_ref, sbuf, rbuf, ssem, rsem
        self.cols = own_ref.shape[1]

    def copy(self, k, c):
        rows = rows_of(c, self.size)
        return push(
            self.sbuf.at[k - 1, rows],
            self.rbuf.at[k - 1, rows],
            self.ssem.at[k - 1, c],
            self.rsem.at[k - 1, c],
            head=peer_of(self.me, k, self.n),
        )

    def send(self, first, last, pairs):
        n = self.n

        def step(t, _):
            turn = t // n
            c = first + turn
            k = t - turn * n + 1
            rows = rows_of(c, self.size)
            peer = peer_of(self.me, k, n)
            part = None
            for a_ref, behind, w_ref, off in pairs:
                span = slice(off, off + a_ref.shape[1])
                term = mm(
                    a_ref[rows_of(c - behind, self.size), :],
                    w_ref[rows_of(peer, self.cols), span],
                    NT,
                )
                part = term if part is None else part + term

            @pl.when(k < n)
            def _():
                self.sbuf[k - 1, rows] = part.astype(BF16)
                self.copy(k, c).start()

            @pl.when(k == n)
            def _():
                self.own_ref[rows, :] = part

            return 0

        lax.fori_loop(0, (last - first) * n, step, 0)

    def relay(self, first, last):
        pass

    def take(self, c):
        rows = rows_of(c, self.size)
        total = self.own_ref[rows, :]
        for k in range(1, self.n):
            self.copy(k, c).wait_recv()
        for k in range(1, self.n):
            total = total + self.rbuf[k - 1, rows].astype(F32)
        return total

    def finish(self, first, last):
        for c in range(first, last):
            for k in range(1, self.n):
                self.copy(k, c).wait_send()


class Gather:
    def __init__(self, n, nc, me, buf, ssem, rsem):
        self.n, self.nc, self.me = n, nc, me
        self.buf, self.ssem, self.rsem = buf, ssem, rsem
        self.size = buf.shape[1] // nc

    def copy(self, k, c, source):
        rows = rows_of(c, self.size)
        return push(
            self.buf.at[source, rows],
            self.buf.at[source, rows],
            self.ssem.at[k - 1, c],
            self.rsem.at[k - 1, c],
            head=peer_of(self.me, k, self.n),
        )

    def send(self, c, value=None):
        if value is not None:
            self.buf[self.me, rows_of(c, self.size)] = value
        for k in range(1, self.n):
            self.copy(k, c, self.me).start()

    def relay(self, c):
        pass

    def take(self, c):
        for k in range(1, self.n):
            self.copy(k, c, peer_of(self.me, self.n - k, self.n)).wait_recv()

    def finish(self, only=None):
        for c in range(self.nc) if only is None else (only,):
            for k in range(1, self.n):
                self.copy(k, c, self.me).wait_send()


def square(me):
    return me + 1 - 2 * lax.rem(me, 2), lax.rem(me + 2, 4), 3 - me


class SquareReduce(Reduce):
    def copy(self, k, c, odd):
        rows = rows_of(c, self.size)
        near, far, _ = square(self.me)
        return push(
            self.sbuf.at[k - 1, rows],
            self.rbuf.at[k - 1, rows],
            self.ssem.at[k - 1, c],
            self.rsem.at[k - 1, c],
            head=far if (k == 2) != odd else near,
        )

    def send(self, first, last, pairs):
        size = self.size
        near, far, across = square(self.me)

        def step(turn, _):
            t = turn // 4
            k = turn - 4 * t
            two = rows_of(t, 2 * size)
            even, odd = rows_of(2 * t, size), rows_of(2 * t + 1, size)
            owner = jnp.where(k == 0, across, jnp.where(k == 1, near, jnp.where(k == 2, far, self.me)))
            part = None
            for a_ref, behind, w_ref, off in pairs:
                span = slice(off, off + a_ref.shape[1])
                term = mm(
                    a_ref[rows_of(t - behind // 2, 2 * size), :],
                    w_ref[rows_of(owner, self.cols), span],
                    NT,
                )
                part = term if part is None else part + term
            self.own_ref[two, :] = part

            @pl.when(k == 0)
            def _():
                self.sbuf[2, two] = part.astype(BF16)
                self.copy(3, 2 * t, False).start()
                self.copy(3, 2 * t + 1, True).start()

            @pl.when(k == 1)
            def _():
                self.sbuf[0, even] = part[:size].astype(BF16)
                self.sbuf[1, odd] = part[size:].astype(BF16)
                self.copy(1, 2 * t, False).start()

            @pl.when(k == 2)
            def _():
                self.sbuf[1, even] = part[:size].astype(BF16)
                self.sbuf[0, odd] = part[size:].astype(BF16)
                self.copy(1, 2 * t + 1, True).start()

            return 0

        lax.fori_loop(2 * first, 2 * last, step, 0)

    def relay(self, first, last):
        for c in range(first, last):
            rows = rows_of(c, self.size)
            odd = c % 2 == 1
            self.copy(3, c, odd).wait_recv()
            both = self.sbuf[1, rows].astype(F32) + self.rbuf[2, rows].astype(F32)
            self.sbuf[1, rows] = both.astype(BF16)
            self.copy(2, c, odd).start()

    def take(self, c):
        rows = rows_of(c, self.size)
        for k in (1, 2):
            self.copy(k, c, c % 2 == 1).wait_recv()
        return self.own_ref[rows, :] + self.rbuf[0, rows].astype(F32) + self.rbuf[1, rows].astype(F32)

    def finish(self, first, last):
        for c in range(first, last):
            for k in range(1, self.n):
                self.copy(k, c, c % 2 == 1).wait_send()


class SquareGather(Gather):
    def own(self, k, c):
        near, far, _ = square(self.me)
        rows = rows_of(c, self.size)
        return push(
            self.buf.at[self.me, rows],
            self.buf.at[self.me, rows],
            self.ssem.at[k - 1, c],
            self.rsem.at[k - 1, c],
            head=(near, far)[k - 1],
        )

    def came(self, k, c):
        source = square(self.me)[k - 1]
        rows = rows_of(c, self.size)
        return push(
            self.buf.at[source, rows],
            self.buf.at[source, rows],
            self.ssem.at[k - 1, c],
            self.rsem.at[k - 1, c],
            head=square(self.me)[0],
        )

    def passed(self, c):
        near, far, _ = square(self.me)
        source, to = (near, far) if c % 2 else (far, near)
        rows = rows_of(c, self.size)
        return push(
            self.buf.at[source, rows],
            self.buf.at[source, rows],
            self.ssem.at[2, c],
            self.rsem.at[2, c],
            head=to,
        )

    def send(self, c, value=None):
        if value is not None:
            self.buf[self.me, rows_of(c, self.size)] = value
        for k in (1, 2):
            self.own(k, c).start()

    def relay(self, c):
        self.came(1 if c % 2 else 2, c).wait_recv()
        self.passed(c).start()

    def take(self, c):
        self.came(2 if c % 2 else 1, c).wait_recv()
        self.came(3, c).wait_recv()

    def finish(self, only=None):
        for c in range(self.nc) if only is None else (only,):
            for k in (1, 2):
                self.own(k, c).wait_send()
            self.passed(c).wait_send()


def reducer(n, *args):
    return (SquareReduce if n == 4 else Reduce)(n, *args)


def gatherer(n, *args):
    return (SquareGather if n == 4 else Gather)(n, *args)


def norm_rows(n, buf, rows, gain_ref, out_ref, scale_ref=None, scale_rows=None):
    cols = buf.shape[2]
    total = None
    for s in range(n):
        piece = buf[s, rows].astype(F32)
        part = jnp.sum(piece * piece, axis=1, keepdims=True)
        total = part if total is None else total + part
    scale = lax.rsqrt(total / (n * cols) + EPS)
    if scale_ref is not None:
        scale_ref[rows if scale_rows is None else scale_rows, :] = scale
    for s in range(n):
        span = slice(s * cols, (s + 1) * cols)
        piece = buf[s, rows].astype(F32)
        out_ref[rows, span] = (piece * scale * gain_ref[:, span]).astype(BF16)


def spread_rows(n, buf, rows, out_ref):
    cols = buf.shape[2]
    for s in range(n):
        out_ref[rows, s * cols : (s + 1) * cols] = buf[s, rows]


def enter_kernel(n, n_seq, halo, x_ref, dy_ref, gain_ref, docs_ref, n1_ref, scale_ref, dyr_ref, window_ref, n1t_hbm, xall, dall, docs, n1t_ref, ts, xs, xr, ds, dr, hs, hr, ks, kr):
    tok = x_ref.shape[0]
    spot = lax.axis_index("seq")
    me = lax.axis_index("head")
    more = spot + 1 < n_seq
    for k in range(1, halo + 1):
        @pl.when(spot < k)
        def _():
            docs[halo - k] = jnp.zeros_like(docs_ref)

    docs[halo] = docs_ref[...]
    xall[me, halo * tok :] = x_ref[...]
    greet(*group(n), *along("seq", n_seq, range(1, n_seq)))
    xg = gatherer(n, 2 * (halo + 1), me, xall, xs, xr)
    dg = gatherer(n, 2, me, dall, ds, dr)

    def word(k):
        return push(
            docs.at[halo], docs.at[halo - k], ks.at[k - 1], kr.at[k - 1], seq=lax.rem(spot + k, n_seq)
        )

    def hop(j):
        here = pl.ds((halo - j + 1) * tok, tok)
        there = pl.ds((halo - j) * tok, tok)
        return push(
            xall.at[me, here], xall.at[me, there], hs.at[j - 1], hr.at[j - 1], seq=lax.rem(spot + 1, n_seq)
        )

    size = min(64, tok)
    per = tok // size

    def block_send(b):
        for c in (2 * b, 2 * b + 1):
            xg.send(c)

    def block_take(b):
        for c in (2 * b, 2 * b + 1):
            xg.relay(c)
        for c in (2 * b, 2 * b + 1):
            xg.take(c)
        own = b == halo

        @pl.loop(0, per)
        def _(i):
            rows = rows_of(b * per + i, size)
            if own:
                norm_rows(n, xall, rows, gain_ref, n1_ref, scale_ref, rows_of(i, size))
            else:
                norm_rows(n, xall, rows, gain_ref, n1_ref)

        rows = slice(b * tok, (b + 1) * tok)
        n1t_ref[:, rows] = n1_ref[rows, :].T

    if halo:
        @pl.when(more)
        def _():
            hop(1).start()

    block_send(halo)
    for k in range(1, halo + 1):
        @pl.when(spot + k < n_seq)
        def _():
            word(k).start()

    for j in range(1, halo + 1):
        @pl.when(spot >= j)
        def _():
            hop(j).wait_recv()

        if j < halo:
            @pl.when((spot >= j) & more)
            def _():
                hop(j + 1).start()

        @pl.when(spot >= j)
        def _():
            block_send(halo - j)

        if j == 1:
            block_take(halo)
        else:
            @pl.when(spot >= j - 1)
            def _():
                block_take(halo - j + 1)

    if not halo:
        block_take(halo)
    dg.send(0, dy_ref[: tok // 2, :])
    dg.send(1, dy_ref[tok // 2 :, :])
    if halo:
        @pl.when(spot >= halo)
        def _():
            block_take(0)

    for j in range(1, halo + 1):
        @pl.when(spot < j)
        def _():
            rows = slice((halo - j) * tok, (halo - j + 1) * tok)
            n1_ref[rows, :] = jnp.zeros((tok, n1_ref.shape[1]), BF16)
            n1t_ref[:, rows] = jnp.zeros((n1_ref.shape[1], tok), BF16)

    leave = pltpu.make_async_copy(n1t_ref, n1t_hbm, ts)
    leave.start()
    for k in range(1, halo + 1):
        @pl.when(spot >= k)
        def _():
            word(k).wait_recv()

    for k in range(halo + 1):
        window_ref[:, k * tok : (k + 1) * tok] = docs[k]
    for c in range(2):
        dg.relay(c)
    for c in range(2):
        dg.take(c)

    @pl.loop(0, per)
    def _(i):
        spread_rows(n, dall, rows_of(i, size), dyr_ref)

    for b in range(halo + 1):
        @pl.when(spot >= halo - b)
        def _():
            xg.finish(2 * b)
            xg.finish(2 * b + 1)

    for j in range(1, halo + 1):
        @pl.when((spot >= j - 1) & more)
        def _():
            hop(j).wait_send()

        @pl.when(spot + j < n_seq)
        def _():
            word(j).wait_send()

    dg.finish()
    leave.wait()


def projection_kernel(halo, n1t_ref, dq_ref, dk_ref, dv_ref, dh1r_ref, g_ref, dw_hbm, dh1t, held, sems):
    full, width = n1t_ref.shape[0], dq_ref.shape[1]
    tok = dq_ref.shape[0]
    size = min(256, full)

    def leave(i):
        return pltpu.make_async_copy(held.at[i], dw_hbm.at[:, i * width : (i + 1) * width], sems.at[i])

    def fill(i, left, right):
        @pl.loop(0, full // size)
        def _(t):
            rows = rows_of(t, size)
            held[i, rows] = mm(left[rows, :], right[...], NN).astype(BF16)

        leave(i).start()

    fill(0, n1t_ref.at[:, halo * tok :], dq_ref)
    fill(1, n1t_ref, dk_ref)
    fill(2, n1t_ref, dv_ref)
    dh1t[...] = dh1r_ref[...].T
    fill(3, dh1t, g_ref)
    for i in range(4):
        leave(i).wait()


def projection_grads(halo, n1t, dq, dk, dv, dh1r, g):
    full, (tok, width) = n1t.shape[0], dq.shape
    args = (n1t, dq, dk, dv, dh1r, g)
    return pl.pallas_call(
        functools.partial(projection_kernel, halo),
        out_shape=pltpu.HBM((full, 4 * width), BF16),
        in_specs=[whole()] * len(args),
        out_specs=pl.BlockSpec(memory_space=pltpu.HBM),
        scratch_shapes=[VMEM((full, tok), BF16), VMEM((4, full, width), BF16), dma(4)],
        cost_estimate=pl.CostEstimate(
            flops=4 * full * width * (n1t.shape[1] + tok),
            bytes_accessed=2 * full * (n1t.shape[1] + 4 * width),
            transcendentals=0,
        ),
        compiler_params=pltpu.CompilerParams(vmem_limit_bytes=40 * 2**20),
    )(*args)


def ffn_kernel(n2_ref, dy_ref, wg_ref, wu_ref, wd_ref, hid_ref, dgate_ref, dup_ref, dw_hbm, n2t, dyt, held, sems):
    j, steps = pl.program_id(0), pl.num_programs(0)

    @pl.when(j == 0)
    def _():
        n2t[...] = n2_ref[...].T
        dyt[...] = dy_ref[...].T

    size = wg_ref.shape[1]
    slot = lax.rem(j, 2)

    def leave(i, step, slot):
        start = pl.multiple_of((i * steps + step) * size, size)
        return pltpu.make_async_copy(held.at[slot, i], dw_hbm.at[:, pl.ds(start, size)], sems.at[slot, i])

    gate = mm(n2_ref[...], wg_ref[...], NN)
    upper = mm(n2_ref[...], wu_ref[...], NN)
    sigma = lax.logistic(gate)
    act = gate * sigma
    hid_ref[...] = (act * upper).astype(BF16)
    d_hid = mm(dy_ref[...], wd_ref[...], NN)
    dup_ref[...] = (d_hid * act).astype(BF16)
    dgate_ref[...] = (d_hid * upper * sigma * (1.0 + gate * (1.0 - sigma))).astype(BF16)

    @pl.when(j >= 2)
    def _():
        for i in range(3):
            leave(i, j - 2, slot).wait()

    for i, (left, right) in enumerate(((n2t, dgate_ref), (n2t, dup_ref), (dyt, hid_ref))):
        held[slot, i] = mm(left[...], right[...], NN).astype(BF16)
        leave(i, j, slot).start()

    @pl.when(j == steps - 1)
    def _():
        for i in range(3):
            leave(i, j, slot).wait()

        @pl.when(j >= 1)
        def _():
            for i in range(3):
                leave(i, j - 1, 1 - slot).wait()


def ffn(n2, dyr, w, tile):
    tok, full = n2.shape
    hidden = w.shape[1] // 3
    steps = hidden // tile
    act = pl.BlockSpec((tok, full), lambda j: (0, 0))
    part = pl.BlockSpec((tok, tile), lambda j: (0, j))
    return pl.pallas_call(
        ffn_kernel,
        grid=(steps,),
        out_shape=[pltpu.HBM((tok, hidden), BF16)] * 3
        + [pltpu.HBM((full, 3 * hidden), BF16)],
        in_specs=[act, act]
        + [pl.BlockSpec((full, tile), functools.partial(lambda i, j: (0, i * steps + j), i)) for i in range(3)],
        out_specs=[part] * 3 + [pl.BlockSpec(memory_space=pltpu.HBM)],
        scratch_shapes=[
            VMEM((full, tok), BF16),
            VMEM((full, tok), BF16),
            VMEM((2, 3, full, tile), BF16),
            dma(2, 3),
        ],
        cost_estimate=pl.CostEstimate(
            flops=12 * tok * full * hidden,
            bytes_accessed=12 * full * hidden,
            transcendentals=tok * hidden,
        ),
        compiler_params=pltpu.CompilerParams(vmem_limit_bytes=40 * 2**20),
    )(far_away(n2), far_away(dyr), *(far_away(w),) * 3)


def middle_kernel(n, nc, off, g_ref, w_hbm, x_ref, gain_ref, h1_ref, n2_ref, scale_ref, own, sbuf, rbuf, w_ref, hall, ws, s1, r1, s2, r2):
    load = fetch(w_hbm, off, w_ref, ws)
    greet(*group(n))
    me = lax.axis_index("head")
    red = reducer(n, own.shape[0] // nc, me, own, sbuf, rbuf, s1, r1)
    gat = gatherer(n, nc, me, hall, s2, r2)
    load.wait()
    red.send(0, nc, [(g_ref, 0, w_ref, 0)])
    red.relay(0, nc)
    for c in range(nc):
        rows = rows_of(c, red.size)
        h1 = red.take(c) + x_ref[rows, :].astype(F32)
        h1_ref[rows, :] = h1
        gat.send(c, h1.astype(BF16))
    size = min(64, red.size)
    for c in range(nc):
        gat.relay(c)
    for c in range(nc):
        gat.take(c)

        @pl.loop(0, red.size // size)
        def _(i):
            norm_rows(n, hall, pl.ds(pl.multiple_of(c * red.size + i * size, size), size), gain_ref, n2_ref, scale_ref)

    red.finish(0, nc)
    gat.finish()


class Stats:
    def __init__(self, n, nc, me, buf, ssem, rsem):
        self.n, self.nc, self.me = n, nc, me
        self.buf, self.ssem, self.rsem = buf, ssem, rsem

    def copy(self, k, c, source):
        return push(
            self.buf.at[source, c],
            self.buf.at[source, c],
            self.ssem.at[k - 1, c],
            self.rsem.at[k - 1, c],
            head=peer_of(self.me, k, self.n),
        )

    def send(self, c, value):
        size, cols = value.shape
        part = value[:, :128]
        for j in range(1, cols // 128):
            part = part + value[:, j * 128 : (j + 1) * 128]
        line = jnp.sum(part.T, axis=0, keepdims=True)
        self.buf[self.me, c] = jnp.broadcast_to(line, (8, size))
        for k in range(1, self.n):
            self.copy(k, c, self.me).start()

    def take(self, c):
        for k in range(1, self.n):
            self.copy(k, c, peer_of(self.me, self.n - k, self.n)).wait_recv()
        total = self.buf[0, c]
        for s in range(1, self.n):
            total = total + self.buf[s, c]
        size = total.shape[1]
        tall = jnp.broadcast_to(total[:1, :], (128, size))
        return tall.T[:, :1]

    def finish(self):
        for c in range(self.nc):
            for k in range(1, self.n):
                self.copy(k, c, self.me).wait_send()


def norm_back(nc, size, width, grad_of, keep, sta, unit_of, gain_ref, base_of, gain_grad_ref, done):
    for c in range(nc):
        rows = rows_of(c, size)
        grad = grad_of(c)
        keep[rows, :] = grad
        unit = unit_of(rows)
        part = jnp.sum(grad * unit, axis=0, keepdims=True)
        if c == 0:
            gain_grad_ref[...] = part
        else:
            gain_grad_ref[...] += part
        sta.send(c, grad * gain_ref[...] * unit)
    for c in range(nc):
        rows = rows_of(c, size)
        dots = sta.take(c) / width
        scaled = keep[rows, :] * gain_ref[...]
        done(c, rows, base_of(rows, scaled - unit_of(rows) * dots))


def back_kernel(n, nc, off, down, dgate_ref, dup_ref, hid_ref, w_hbm, h1_ref, scale_ref, gain_ref, dy_ref, dh1_ref, dh1r_ref, gain_grad_ref, *refs):
    output_ref = None
    if down is not None:
        output_ref, osum, osend, orecv, wd_ref, wds, s4, r4, *refs = refs
        load_down = fetch(w_hbm, down, wd_ref, wds)
    own, sbuf, rbuf, w_ref, stat, dall, ws, s1, r1, s2, r2, s3, r3 = refs
    load = fetch(w_hbm, off, w_ref, ws)
    greet(*group(n))
    me = lax.axis_index("head")
    pairs = [(dgate_ref, 0, w_ref, 0), (dup_ref, 0, w_ref, dgate_ref.shape[1])]
    size = own.shape[0] // nc
    red = reducer(n, size, me, own, sbuf, rbuf, s1, r1)
    sta = Stats(n, nc, me, stat, s2, r2)
    if down is not None:
        last = reducer(n, size, me, osum, osend, orecv, s4, r4)
    load.wait()
    gat = gatherer(n, nc, me, dall, s3, r3)
    red.send(0, nc, pairs)
    red.relay(0, nc)

    def unit_of(rows):
        return h1_ref[rows, :].astype(BF16).astype(F32) * scale_ref[rows, :]

    def base_of(rows, back):
        return dy_ref[rows, :] + scale_ref[rows, :] * back

    def done(c, rows, value):
        dh1_ref[rows, :] = value
        gat.send(c, value.astype(BF16))

    norm_back(nc, size, n * red.cols, red.take, own, sta, unit_of, gain_ref, base_of, gain_grad_ref, done)
    for c in range(nc):
        gat.relay(c)
    if down is not None:
        load_down.wait()
        last.send(0, nc, [(hid_ref, 0, wd_ref, 0)])
    for c in range(nc):
        gat.take(c)
        spread_rows(n, dall, rows_of(c, red.size), dh1r_ref)
    if down is not None:
        last.relay(0, nc)
        for c in range(nc):
            rows = rows_of(c, size)
            output_ref[rows, :] = (last.take(c) + h1_ref[rows, :]).astype(BF16)
        last.finish(0, nc)
    red.finish(0, nc)
    sta.finish()
    gat.finish()


def leave_kernel(n, n_seq, n_dp, halo, nc, dq_ref, dk_ref, dv_ref, w_hbm, x_ref, scale_ref, gain_ref, dh1_ref, gain_two_ref, group_ref, out_ref, sums_ref, own, sbuf, rbuf, w_ref, stat, gain_s, words, sums, zsend, zrecv, keep, ws, s1, r1, s2, r2, s3, r3, s4, r4, s5, r5):
    load = fetch(w_hbm, 0, w_ref, ws)
    spot, core = lax.axis_index("seq"), lax.axis_index("dp")
    others = [(i, j) for i in range(n_seq) for j in range(n_dp) if i or j]

    def of(i, j):
        return {"seq": lax.rem(spot + i, n_seq), "dp": lax.rem(core + j, n_dp)}

    def sends(j):
        return spot >= halo - j + 1

    def comes(j):
        return (spot + 1 < n_seq) & (spot + 1 >= halo - j + 1)

    for j in range(1, halo + 1):
        @pl.when(jnp.logical_not(comes(j)))
        def _():
            zrecv[j - 1] = jnp.zeros(zrecv.shape[1:], BF16)

    me = lax.axis_index("head")
    words[me] = group_ref[...]
    greet(*group(n), *(of(i, j) for i, j in others))
    tok, width = dq_ref.shape
    size = tok // nc
    red = reducer(n, size, me, own, sbuf, rbuf, s1, r1)
    sta = Stats(n, nc, me, stat, s2, r2)

    def word(k, source):
        return push(
            words.at[source], words.at[source], s3.at[k - 1], r3.at[k - 1], head=peer_of(me, k, n)
        )

    def hop(j, c):
        rows = pl.ds(c * size, size)
        return push(
            zsend.at[j - 1, rows], zrecv.at[j - 1, rows], s5.at[j - 1, c], r5.at[j - 1, c], seq=lax.rem(spot + n_seq - 1, n_seq)
        )

    for k in range(1, n):
        word(k, me).start()
    load.wait()
    pairs = [(dk_ref, 0, w_ref, width), (dv_ref, 0, w_ref, 2 * width)]
    for b in range(halo):
        @pl.when(sends(b + 1))
        def _():
            red.send(b * nc, (b + 1) * nc, pairs)

    red.send(halo * nc, (halo + 1) * nc, [(dq_ref, halo * nc, w_ref, 0)] + pairs)

    for b in range(halo):
        @pl.when(sends(b + 1))
        def _():
            red.relay(b * nc, (b + 1) * nc)

    red.relay(halo * nc, (halo + 1) * nc)

    def total(b, c):
        value = red.take(b * nc + c)
        if b == 0:
            return value

        @pl.when(comes(b))
        def _():
            hop(b, c).wait_recv()

        return value + zrecv[b - 1, pl.ds(c * size, size)].astype(F32)

    for j in range(1, halo + 1):
        for c in range(nc):
            @pl.when(sends(j))
            def _():
                zsend[j - 1, pl.ds(c * size, size)] = total(j - 1, c).astype(BF16)
                hop(j, c).start()

            if j > 1:
                @pl.when(jnp.logical_not(sends(j)) & comes(j - 1))
                def _():
                    hop(j - 1, c).wait_recv()

    def unit_of(rows):
        return x_ref[rows, :].astype(F32) * scale_ref[rows, :]

    def base_of(rows, back):
        return dh1_ref[rows, :] + scale_ref[rows, :] * back

    def done(c, rows, value):
        out_ref[rows, :] = value.astype(BF16)

    norm_back(nc, size, n * red.cols, functools.partial(total, halo), keep, sta, unit_of, gain_ref, base_of, gain_s, done)
    for k in range(1, n):
        word(k, peer_of(me, n - k, n)).wait_recv()
    total = words[0]
    for k in range(1, n):
        total = total + words[k]
    place = spot * n_dp + core
    mine = sums.at[place]
    cols = gain_s.shape[1]
    mine[...] = jnp.zeros((8, cols), F32)
    mine[0:1, :] = gain_s[...]
    mine[1:2, :] = gain_two_ref[...]
    mine[2:4, : total.shape[1]] = total[0:2]

    def share(t):
        i, j = others[t]
        return push(mine, mine, s4.at[t], r4.at[t], **of(i, j))

    def await_from(t):
        i, j = others[t]
        back = lax.rem(spot + n_seq - i, n_seq) * n_dp + lax.rem(core + n_dp - j, n_dp)
        theirs = sums.at[back]
        return push(theirs, theirs, s4.at[t], r4.at[t], **of(i, j))

    for t in range(len(others)):
        share(t).start()
    for t in range(len(others)):
        await_from(t).wait_recv()
    total = sums[0]
    for t in range(1, n_seq * n_dp):
        total = total + sums[t]
    sums_ref[...] = total
    for b in range(halo):
        @pl.when(sends(b + 1))
        def _():
            red.finish(b * nc, (b + 1) * nc)
            for c in range(nc):
                hop(b + 1, c).wait_send()

    red.finish(halo * nc, (halo + 1) * nc)
    sta.finish()
    for k in range(1, n):
        word(k, me).wait_send()
    for t in range(len(others)):
        share(t).wait_send()


def finish_kernel(n, n_seq, n_dp, halo, nc, off, n1t_hbm, w_hbm, wd_hbm, dq_ref, dk_ref, dv_ref, dh1r_ref, g_ref, hid_ref, h1_ref, x_ref, scale_ref, gain_ref, dh1_ref, gain_two_ref, group_ref, acts_ref, sums_ref, grads_ref, own, sbuf, rbuf, osum, osend, orecv, n1t_ref, w_ref, wd_ref, dh1t, mine, given, taken, sent, came, stat, gain_s, words, sums, zsend, zrecv, keep, load_sem, s1, r1, s2, r2, s3, r3, s4, r4, s5, r5, s6, r6, s7, r7, s8, rl, rr):
    loads = [
        fetch(n1t_hbm, 0, n1t_ref, load_sem.at[0]),
        fetch(w_hbm, 0, w_ref, load_sem.at[1]),
        fetch(wd_hbm, off, wd_ref, load_sem.at[2]),
    ]
    spot, core = lax.axis_index("seq"), lax.axis_index("dp")
    me = lax.axis_index("head")
    tok, width = dq_ref.shape
    size = tok // nc
    share = mine.shape[1]
    others = [(i, j) for i in range(n_seq) for j in range(n_dp) if i or j]

    def of(i, j):
        return {"seq": lax.rem(spot + i, n_seq), "dp": lax.rem(core + j, n_dp)}

    def sends(j):
        return spot >= halo - j + 1

    def comes(j):
        return (spot + 1 < n_seq) & (spot + 1 >= halo - j + 1)

    for j in range(1, halo + 1):
        @pl.when(jnp.logical_not(comes(j)))
        def _():
            zrecv[j - 1] = jnp.zeros(zrecv.shape[1:], BF16)

    words[me] = group_ref[...]
    dh1t[...] = dh1r_ref[...].T
    greet(*group(n), *(of(i, j) for i, j in others))
    red = reducer(n, size, me, own, sbuf, rbuf, s1, r1)
    sta = Stats(n, nc, me, stat, s2, r2)
    last = reducer(n, size, me, osum, osend, orecv, s6, r6)

    def word(k, source):
        return push(
            words.at[source], words.at[source], s3.at[k - 1], r3.at[k - 1], head=peer_of(me, k, n)
        )

    def hop(j, c):
        rows = pl.ds(c * size, size)
        return push(
            zsend.at[j - 1, rows], zrecv.at[j - 1, rows], s5.at[j - 1, c], r5.at[j - 1, c], seq=lax.rem(spot + n_seq - 1, n_seq)
        )

    for k in range(1, n):
        word(k, me).start()

    def block_grads(i, c, ref):
        rows = rows_of(i * n_dp + c, share)
        ref[:, :width] = mm(n1t_ref[rows, halo * tok :], dq_ref[...], NN).astype(ref.dtype)
        ref[:, width : 2 * width] = mm(n1t_ref[rows, :], dk_ref[...], NN).astype(ref.dtype)
        ref[:, 2 * width : 3 * width] = mm(n1t_ref[rows, :], dv_ref[...], NN).astype(ref.dtype)
        ref[:, 3 * width :] = mm(dh1t[rows, :], g_ref[...], NN).astype(ref.dtype)

    def give(k, i):
        return push(
            given.at[k - 1, i], taken.at[k - 1, i], s7.at[k - 1, i], r7.at[k - 1, i], dp=lax.rem(core + k, n_dp)
        )

    def block_relay(b):
        if b == halo:
            red.relay(b * nc, (b + 1) * nc)
        else:
            @pl.when(sends(b + 1))
            def _():
                red.relay(b * nc, (b + 1) * nc)

    loads[1].wait()
    pairs = [(dk_ref, 0, w_ref, width), (dv_ref, 0, w_ref, 2 * width)]
    for b in range(halo):
        @pl.when(sends(b + 1))
        def _():
            red.send(b * nc, (b + 1) * nc, pairs)

    loads[0].wait()
    for k in range(1, n_dp):

        @pl.loop(0, n_seq)
        def _(i):
            block_grads(i, lax.rem(core + k, n_dp), given.at[k - 1, i])
            give(k, i).start()

    @pl.loop(0, n_seq)
    def _(i):
        block_grads(i, core, mine.at[i])

    half = mine.shape[2] // 2

    def chip(d, p):
        cols = slice(p * half, (p + 1) * half)
        value = mine[d, :, cols]
        for k in range(1, n_dp):
            if p == 0:
                give(k, d).wait_recv()
            value = value + taken[k - 1, d, :, cols].astype(F32)
        return value

    def piece(d, p, slot, sem, to):
        cols = slice(p * half, (p + 1) * half)
        return push(sent.at[d, :, cols], came.at[slot, :, cols], s8.at[d, p], sem.at[d, p], seq=to)

    def right(d, p):
        return piece(d, p, d, rl, lax.rem(spot + 1, n_seq))

    def left(d, p):
        return piece(d, p, jnp.where(spot - 1 == d, n_seq, d), rr, lax.rem(spot + n_seq - 1, n_seq))

    def arrived(d, p, slot, sem):
        return piece(d, p, slot, sem, lax.rem(spot + 1, n_seq))

    def start_line(i, p):
        cols = slice(p * half, (p + 1) * half)
        d = n_seq - 1 - i

        @pl.when(spot == 0)
        def _():
            if i:
                right(d + 1, p).wait_send()
            sent[d, :, cols] = chip(d, p).astype(BF16)
            right(d, p).start()

        @pl.when(spot == n_seq - 1)
        def _():
            if i:
                left(i - 1, p).wait_send()
            sent[i, :, cols] = chip(i, p).astype(BF16)
            left(i, p).start()

    def pass_line(i, p):
        cols = slice(p * half, (p + 1) * half)
        d = n_seq - 1 - i

        @pl.when((spot > 0) & (d > spot))
        def _():
            arrived(d, p, d, rl).wait_recv()
            sent[d, :, cols] = (chip(d, p) + came[d, :, cols].astype(F32)).astype(BF16)
            right(d, p).start()

        @pl.when((spot < n_seq - 1) & (i < spot))
        def _():
            arrived(i, p, i, rr).wait_recv()
            sent[i, :, cols] = (chip(i, p) + came[i, :, cols].astype(F32)).astype(BF16)
            left(i, p).start()

    def total(b, c):
        value = red.take(b * nc + c)
        if b == 0:
            return value

        @pl.when(comes(b))
        def _():
            hop(b, c).wait_recv()

        return value + zrecv[b - 1, pl.ds(c * size, size)].astype(F32)

    def send_hop(j):
        for c in range(nc):
            @pl.when(sends(j))
            def _():
                zsend[j - 1, pl.ds(c * size, size)] = total(j - 1, c).astype(BF16)
                hop(j, c).start()

            if j > 1:
                @pl.when(jnp.logical_not(sends(j)) & comes(j - 1))
                def _():
                    hop(j - 1, c).wait_recv()

    for p in range(2):
        if n_seq > 1:
            start_line(0, p)
    for b in range(halo):
        block_relay(b)
    red.send(halo * nc, (halo + 1) * nc, [(dq_ref, halo * nc, w_ref, 0)] + pairs)
    for t in range(max(n_seq - 1, 1)):
        if t < halo:
            send_hop(t + 1)
        for p in range(2):
            if t < n_seq - 1:
                pass_line(t, p)
            if t + 1 < n_seq - 1:
                start_line(t + 1, p)
        if t == 0:
            block_relay(halo)
            loads[2].wait()
            last.send(0, nc, [(hid_ref, 0, wd_ref, 0)])

    def unit_of(rows):
        return x_ref[rows, :].astype(F32) * scale_ref[rows, :]

    def base_of(rows, back):
        return dh1_ref[rows, :] + scale_ref[rows, :] * back

    def done(c, rows, value):
        acts_ref[0, rows, :] = value.astype(BF16)

    norm_back(nc, size, n * red.cols, functools.partial(total, halo), keep, sta, unit_of, gain_ref, base_of, gain_s, done)
    for k in range(1, n):
        word(k, peer_of(me, n - k, n)).wait_recv()
    group_sum = words[0]
    for k in range(1, n):
        group_sum = group_sum + words[k]
    place = spot * n_dp + core
    slip = sums.at[place]
    cols = gain_s.shape[1]
    slip[...] = jnp.zeros((8, cols), F32)
    slip[0:1, :] = gain_s[...]
    slip[1:2, :] = gain_two_ref[...]
    slip[2:4, : group_sum.shape[1]] = group_sum[0:2]

    def hand(t):
        i, j = others[t]
        return push(slip, slip, s4.at[t], r4.at[t], **of(i, j))

    def handed(t):
        i, j = others[t]
        back = lax.rem(spot + n_seq - i, n_seq) * n_dp + lax.rem(core + n_dp - j, n_dp)
        theirs = sums.at[back]
        return push(theirs, theirs, s4.at[t], r4.at[t], **of(i, j))

    for t in range(len(others)):
        hand(t).start()
    last.relay(0, nc)
    for c in range(nc):
        rows = rows_of(c, size)
        acts_ref[1, rows, :] = (last.take(c) + h1_ref[rows, :]).astype(BF16)
    for p in range(2):
        cols = slice(p * half, (p + 1) * half)
        mine[spot, :, cols] = chip(spot, p)

        @pl.when(spot > 0)
        def _():
            arrived(spot, p, spot, rl).wait_recv()
            mine[spot, :, cols] = mine[spot, :, cols] + came[spot, :, cols].astype(F32)

        @pl.when(spot < n_seq - 1)
        def _():
            arrived(spot, p, n_seq, rr).wait_recv()
            mine[spot, :, cols] = mine[spot, :, cols] + came[n_seq, :, cols].astype(F32)

    grads_ref[...] = mine[spot]
    for t in range(len(others)):
        handed(t).wait_recv()
    full_sum = sums[0]
    for t in range(1, n_seq * n_dp):
        full_sum = full_sum + sums[t]
    sums_ref[...] = full_sum
    for b in range(halo):
        @pl.when(sends(b + 1))
        def _():
            red.finish(b * nc, (b + 1) * nc)
            for c in range(nc):
                hop(b + 1, c).wait_send()

    red.finish(halo * nc, (halo + 1) * nc)
    last.finish(0, nc)
    sta.finish()
    for k in range(1, n):
        word(k, me).wait_send()
    for t in range(len(others)):
        hand(t).wait_send()
    for k in range(1, n_dp):
        for i in range(n_seq):
            give(k, i).wait_send()
    for d in range(n_seq):
        for p in range(2):

            @pl.when((spot < d) & ((spot > 0) | (d == 1)))
            def _():
                right(d, p).wait_send()

            @pl.when((spot > d) & ((spot < n_seq - 1) | (d == n_seq - 2)))
            def _():
                left(d, p).wait_send()


def far_away(x):
    return pltpu.with_memory_space_constraint(x, pltpu.HBM)


def dma(*dims):
    return pltpu.SemaphoreType.DMA(dims)


def talk(kernel, ident, outs, scratch, flops, room, args, far=(), far_outs=(), kept=(), kept_outs=()):
    return pl.pallas_call(
        kernel,
        out_shape=[
            pltpu.HBM(s, d) if i in far_outs or i in kept_outs else jax.ShapeDtypeStruct(s, d)
            for i, (s, d) in enumerate(outs)
        ],
        in_specs=[
            pl.BlockSpec(memory_space=pltpu.HBM) if i in far else whole() for i in range(len(args))
        ],
        out_specs=[
            pl.BlockSpec(memory_space=pltpu.HBM) if i in far_outs else whole()
            for i in range(len(outs))
        ],
        scratch_shapes=scratch,
        cost_estimate=pl.CostEstimate(flops=flops, bytes_accessed=40 * 2**20, transcendentals=0),
        compiler_params=pltpu.CompilerParams(
            collective_id=ident, has_side_effects=True, vmem_limit_bytes=room * 2**20
        ),
    )(*(far_away(a) if i in far or i in kept else a for i, a in enumerate(args)))


def forward_kernel(base, nb_ref, lam_ref, q_ref, k_ref, v_ref, start_ref, gain_ref, o1_ref, o2_ref, lse_ref, g_ref, held, m_s, l_s, acc):
    size = q_ref.shape[0]
    qt = pl.program_id(1)
    q = q_ref[...] * 0.125
    lane = lax.broadcasted_iota(jnp.int32, q.shape, 1)
    zero = jnp.zeros_like(q)
    parts = (jnp.where(lane < HALF, q, zero), jnp.where(lane >= HALF, q, zero))
    key = lax.broadcasted_iota(jnp.int32, (size, size), 0)
    query = lax.broadcasted_iota(jnp.int32, (size, size), 1)
    start = start_ref[...]

    count = nb_ref[qt]

    def scores(d, first):
        where = base + qt - d
        k = k_ref[rows_of(where, size), :]
        allowed = key >= start - where * size
        if first:
            allowed = allowed & (key <= query)
        for m in range(2):
            s = jnp.where(allowed, mm(k, parts[m], NT), NEG_BIG)
            held[d, m] = s
            top = jnp.max(s, axis=0, keepdims=True)
            m_s[m] = top if first else jnp.maximum(m_s[m], top)

    def weights(d, _):
        for m in range(2):
            e = jnp.exp(held[d, m] - m_s[m])
            held[d, m] = e
            l_s[m] += jnp.sum(e, axis=0, keepdims=True)
        return 0

    def mix(d, first):
        v = v_ref[rows_of(base + qt - d, size), :]
        for m in range(2):
            term = mm(v, (held[d, m] * l_s[m]).astype(BF16), TN)
            if first:
                acc[m] = term
            else:
                acc[m] += term

    def each(step):
        def body(d, _):
            step(d, False)
            return 0

        step(0, True)
        lax.fori_loop(1, count, body, 0)

    each(scores)
    l_s[...] = jnp.zeros_like(l_s)
    lax.fori_loop(0, count, weights, 0)
    for m in range(2):
        lse_ref[0, m : m + 1, :] = m_s[m] + jnp.log(l_s[m])
        l_s[m] = 1.0 / l_s[m]
    each(mix)
    o1, o2 = acc[0], acc[1]
    o1_ref[...] = o1
    o2_ref[...] = o2
    diff = o1 - lam_ref[0] * o2
    scale = lax.rsqrt(jnp.mean(diff * diff, axis=0, keepdims=True) + EPS)
    g = diff * scale * gain_ref[...] * KEEP
    g_ref[...] = g.T.astype(BF16)


def backward_kernel(base, nb_ref, lam_ref, q_ref, k_ref, v_ref, start_ref, gain_ref, o1_ref, o2_ref, lse_ref, dg_ref, dq_ref, dk_ref, dv_ref, gain_grad_ref, lam_grad_ref, dq_s, dk_s, dv_s):
    size = q_ref.shape[0]
    h, qt = pl.program_id(0), pl.program_id(1)
    lam = lam_ref[0]

    @pl.when((h == 0) & (qt == 0))
    def _():
        gain_grad_ref[...] = jnp.zeros_like(gain_grad_ref)
        lam_grad_ref[...] = jnp.zeros_like(lam_grad_ref)

    @pl.when(qt == 0)
    def _():
        dk_s[...] = jnp.zeros_like(dk_s)
        dv_s[...] = jnp.zeros_like(dv_s)

    o1, o2 = o1_ref[...], o2_ref[...]
    diff = o1 - lam * o2
    scale = lax.rsqrt(jnp.mean(diff * diff, axis=0, keepdims=True) + EPS)
    unit = diff * scale
    dg = dg_ref[...].T
    gain_grad_ref[...] += jnp.sum(dg * unit, axis=1, keepdims=True) * KEEP
    du = dg * gain_ref[...] * KEEP
    do = scale * (du - unit * jnp.mean(du * unit, axis=0, keepdims=True))
    lam_grad_ref[...] -= jnp.sum(do * o2, axis=1, keepdims=True)
    grads = (do.astype(BF16), (-lam * do).astype(BF16))
    deltas = tuple(
        jnp.sum(g.astype(F32) * o, axis=0, keepdims=True) for g, o in zip(grads, (o1, o2))
    )
    q = q_ref[...] * 0.125
    lane = lax.broadcasted_iota(jnp.int32, q.shape, 1)
    zero = jnp.zeros_like(q)
    parts = (jnp.where(lane < HALF, q, zero), jnp.where(lane >= HALF, q, zero))
    key = lax.broadcasted_iota(jnp.int32, (size, size), 0)
    query = lax.broadcasted_iota(jnp.int32, (size, size), 1)
    start = start_ref[...]
    dq_s[...] = jnp.zeros_like(dq_s)

    def block(where, first):
        rows = rows_of(where, size)
        k, v = k_ref[rows, :], v_ref[rows, :]
        halves = (jnp.where(lane < HALF, k, zero), jnp.where(lane >= HALF, k, zero))
        allowed = key >= start - where * size
        if first:
            allowed = allowed & (key <= query)
        dq = dq_s[...]
        dk = dk_s[rows, :]
        dv = dv_s[rows, :]
        for m in range(2):
            s = mm(k, parts[m], NT)
            p = jnp.where(allowed, jnp.exp(s - lse_ref[0, m : m + 1, :]), 0.0)
            dp = mm(v, grads[m], NN)
            ds = (p * (dp - deltas[m])).astype(BF16)
            dq = dq + mm(halves[m], ds, TN)
            dk = dk + mm(ds, parts[m], NN)
            dv = dv + mm(p.astype(BF16), grads[m], NT)
        dq_s[...] = dq
        dk_s[rows, :] = dk
        dv_s[rows, :] = dv

    block(base + qt, True)

    def earlier(d, _):
        block(base + qt - d, False)
        return 0

    lax.fori_loop(1, nb_ref[qt], earlier, 0)
    dq_ref[...] = (dq_s[...] * 0.125).T.astype(BF16)

    @pl.when(qt == pl.num_programs(1) - 1)
    def _():
        dk_ref[...] = dk_s[...].astype(BF16)
        dv_ref[...] = dv_s[...].astype(BF16)


SMEM = pl.BlockSpec(memory_space=pltpu.SMEM)
TILE = 256


def attend(q, kv, start, nb, lam, gain_col):
    tok, width = q.shape
    heads = width // VDIM
    rows = kv.shape[0]
    size = min(TILE, tok)
    base = (rows - tok) // size
    head_block = pl.BlockSpec((VDIM, size), lambda h, t: (h, t))
    return pl.pallas_call(
        functools.partial(forward_kernel, base),
        grid=(heads, tok // size),
        out_shape=[
            jax.ShapeDtypeStruct((width, tok), F32),
            jax.ShapeDtypeStruct((width, tok), F32),
            jax.ShapeDtypeStruct((heads, 2, tok), F32),
            jax.ShapeDtypeStruct((tok, width), BF16),
        ],
        in_specs=[
            SMEM,
            SMEM,
            pl.BlockSpec((size, VDIM), lambda h, t: (t, h)),
            pl.BlockSpec((rows, VDIM), lambda h, t: (0, h)),
            pl.BlockSpec((rows, VDIM), lambda h, t: (0, heads + h)),
            pl.BlockSpec((1, size), lambda h, t: (0, t)),
            pl.BlockSpec((VDIM, 1), lambda h, t: (0, 0)),
        ],
        out_specs=[
            head_block,
            head_block,
            pl.BlockSpec((1, 2, size), lambda h, t: (h, 0, t)),
            pl.BlockSpec((size, VDIM), lambda h, t: (t, h)),
        ],
        scratch_shapes=[
            VMEM((rows // size, 2, size, size), F32),
            VMEM((2, 1, size), F32),
            VMEM((2, 1, size), F32),
            VMEM((2, VDIM, size), F32),
        ],
        cost_estimate=pl.CostEstimate(
            flops=4 * tok * rows * heads * VDIM,
            bytes_accessed=8 * tok * width + 4 * rows * width,
            transcendentals=2 * tok * rows * heads,
        ),
        compiler_params=pltpu.CompilerParams(vmem_limit_bytes=32 * 2**20),
    )(nb, lam, q, kv, kv, start, gain_col)


def halo_room(rows, tok):
    return 2 * (rows // tok)


def attend_back(q, kv, start, nb, lam, gain_col, o1, o2, lse, dg):
    tok, width = q.shape
    heads = width // VDIM
    rows = kv.shape[0]
    size = min(TILE, tok)
    base = (rows - tok) // size
    head_block = pl.BlockSpec((VDIM, size), lambda h, t: (h, t))
    return pl.pallas_call(
        functools.partial(backward_kernel, base),
        grid=(heads, tok // size),
        out_shape=[
            pltpu.HBM((tok, width), BF16),
            pltpu.HBM((rows, width), BF16),
            pltpu.HBM((rows, width), BF16),
            jax.ShapeDtypeStruct((VDIM, 1), F32),
            jax.ShapeDtypeStruct((VDIM, 1), F32),
        ],
        in_specs=[
            SMEM,
            SMEM,
            pl.BlockSpec((size, VDIM), lambda h, t: (t, h)),
            pl.BlockSpec((rows, VDIM), lambda h, t: (0, h)),
            pl.BlockSpec((rows, VDIM), lambda h, t: (0, heads + h)),
            pl.BlockSpec((1, size), lambda h, t: (0, t)),
            pl.BlockSpec((VDIM, 1), lambda h, t: (0, 0)),
            head_block,
            head_block,
            pl.BlockSpec((1, 2, size), lambda h, t: (h, 0, t)),
            pl.BlockSpec((size, VDIM), lambda h, t: (t, h)),
        ],
        out_specs=[
            pl.BlockSpec((size, VDIM), lambda h, t: (t, h)),
            pl.BlockSpec((rows, VDIM), lambda h, t: (0, h)),
            pl.BlockSpec((rows, VDIM), lambda h, t: (0, h)),
            pl.BlockSpec((VDIM, 1), lambda h, t: (0, 0)),
            pl.BlockSpec((VDIM, 1), lambda h, t: (0, 0)),
        ],
        scratch_shapes=[
            VMEM((VDIM, size), F32),
            VMEM((rows, VDIM), F32),
            VMEM((rows, VDIM), F32),
        ],
        cost_estimate=pl.CostEstimate(
            flops=10 * tok * rows * heads * VDIM,
            bytes_accessed=16 * tok * width + 8 * rows * width,
            transcendentals=2 * tok * rows * heads,
        ),
        compiler_params=pltpu.CompilerParams(vmem_limit_bytes=(12 + halo_room(rows, tok)) * 2**20),
    )(nb, lam, q, kv, kv, start, gain_col, o1, o2, lse, dg)


def pack_kernel(count, *refs):
    pieces, outs, sems = refs[:count], refs[count:-1], refs[-1]
    copies, out, off = [], 0, 0
    for i, piece in enumerate(pieces):
        width = piece.shape[1]
        if off + width > outs[out].shape[1]:
            out, off = out + 1, 0
        copies.append(
            pltpu.make_async_copy(piece, outs[out].at[:, off : off + width], sems.at[i])
        )
        off += width
    for copy in copies:
        copy.start()
    for copy in copies:
        copy.wait()


def pack(*groups):
    pieces = [p for group in groups for p in group]
    hbm = pl.BlockSpec(memory_space=pltpu.HBM)
    return pl.pallas_call(
        functools.partial(pack_kernel, len(pieces)),
        out_shape=[
            pltpu.HBM((g[0].shape[0], sum(p.shape[1] for p in g)), g[0].dtype) for g in groups
        ],
        in_specs=[hbm] * len(pieces),
        out_specs=[hbm] * len(groups),
        scratch_shapes=[dma(len(pieces))],
        cost_estimate=pl.CostEstimate(flops=0, bytes_accessed=4 * 2**20, transcendentals=0),
        compiler_params=pltpu.CompilerParams(vmem_limit_bytes=2**20),
    )(*(far_away(p) for p in pieces))


CHUNKS = 2


def on_device(
    n_head,
    n_seq,
    n_dp,
    inputs,
    w_query,
    w_key,
    w_value,
    w_output,
    w_gate,
    w_up,
    w_down,
    gain_attn,
    gain_ffn,
    group_gain,
    lambda_q1,
    lambda_k1,
    lambda_q2,
    lambda_k2,
    doc_ids,
    needles,
    out_grad,
):
    x = inputs[0]
    tok, cols = x.shape
    n, nc = n_head, CHUNKS
    full = n * cols
    width = w_query.shape[1]
    hidden = w_gate.shape[1]
    me = lax.axis_index("head")
    halo = n_seq // 2

    p_attn, p_ffn = pack((w_query, w_key, w_value, w_output), (w_gate, w_up, w_down))
    w_attn = lax.all_gather(
        p_attn,
        ("seq", "dp"),
        axis=0,
        tiled=True,
    )
    w_ffn = lax.all_gather(
        p_ffn, ("seq", "dp"), axis=0, tiled=True
    )

    weight = jnp.where(needles[0] == 1, 1.0, 0.1).astype(F32)
    dy = out_grad[0].astype(F32) * weight[:, None]
    gain_one = gain_attn[None, :]
    gain_two = gain_ffn[None, :]
    gain_one_cols = lax.dynamic_slice_in_dim(gain_one, me * cols, cols, 1)
    gain_two_cols = lax.dynamic_slice_in_dim(gain_two, me * cols, cols, 1)
    lam = jnp.exp(jnp.sum(lambda_q1 * lambda_k1)) - jnp.exp(jnp.sum(lambda_q2 * lambda_k2))
    lam = (lam + LAMBDA_INIT)[None]
    gain_col = group_gain[:, None]

    docs = jnp.broadcast_to(doc_ids + 1, (8, tok))
    n1, scale_one, dyr, window, n1t = talk(
        functools.partial(enter_kernel, n, n_seq, halo),
        0,
        [
            (((halo + 1) * tok, full), BF16),
            ((tok, 1), F32),
            ((tok, full), BF16),
            ((8, (halo + 1) * tok), jnp.int32),
            ((full, (halo + 1) * tok), BF16),
        ],
        [
            VMEM((n, (halo + 1) * tok, cols), BF16),
            VMEM((n, tok, cols), BF16),
            VMEM((halo + 1, 8, tok), jnp.int32),
            VMEM((full, (halo + 1) * tok), BF16),
            pltpu.SemaphoreType.DMA,
        ]
        + [dma(n - 1, 2 * (halo + 1))] * 2
        + [dma(n - 1, 2)] * 2
        + [dma(max(halo, 1))] * 4,
        tok * full * 8,
        14 + 4 * (halo + 1),
        (x, dy.astype(BF16), gain_one, docs),
        far_outs=(4,),
        kept_outs=(2,),
    )
    start = jnp.sum((window[0][None, :] < docs[0][:, None]).astype(jnp.int32), axis=1)
    size = min(TILE, tok)
    base = halo * tok // size
    first = start[::size]
    nb = base + jnp.arange(tok // size, dtype=jnp.int32) - first // size + 1
    start = start[None, :]

    q = jnp.dot(n1[halo * tok :], w_attn[:, :width], preferred_element_type=F32).astype(BF16)
    kv = jnp.dot(n1, w_attn[:, width : 3 * width], preferred_element_type=F32).astype(BF16)
    o1, o2, lse, grouped = attend(q, kv, start, nb, lam, gain_col)

    exchange = [VMEM((tok, cols), F32), VMEM((n - 1, tok, cols), BF16), VMEM((n - 1, tok, cols), BF16)]
    h1, n2, scale_two = talk(
        functools.partial(middle_kernel, n, nc, 3 * width),
        1,
        [((tok, cols), F32), ((tok, full), BF16), ((tok, 1), F32)],
        exchange
        + [VMEM((full, width), BF16), VMEM((n, tok, cols), BF16), pltpu.SemaphoreType.DMA]
        + [dma(n - 1, nc)] * 4,
        2 * tok * full * width,
        14,
        (grouped, w_attn, x, gain_two),
        far=(1,),
        kept_outs=(1,),
    )
    tile = min(2 * TILE, hidden)
    inner, d_gate, d_up, d_wffn = ffn(n2, dyr, w_ffn, tile)
    g_ffn = lax.psum_scatter(d_wffn, ("seq", "dp"), scatter_dimension=0, tiled=True)

    stat = VMEM((n, nc, 8, tok // nc), F32)
    early = halo > 2
    dh1, dh1r, gain_two_part, *output = talk(
        functools.partial(back_kernel, n, nc, 0, 2 * hidden if early else None),
        2,
        [((tok, cols), F32), ((tok, full), BF16), ((1, cols), F32)]
        + [((tok, cols), BF16)] * early,
        (exchange + [VMEM((full, hidden), BF16), pltpu.SemaphoreType.DMA] + [dma(n - 1, nc)] * 2)
        * early
        + exchange
        + [
            VMEM((full, 2 * hidden), BF16),
            stat,
            VMEM((n, tok, cols), BF16),
            pltpu.SemaphoreType.DMA,
        ]
        + [dma(n - 1, nc)] * 6,
        4 * tok * full * hidden,
        26,
        (d_gate, d_up, inner, w_ffn, h1, scale_two, gain_two_cols, dy),
        far=(3,),
        kept=(0, 1, 2),
    )
    dg = jnp.dot(dh1r, w_attn[:, 3 * width :], preferred_element_type=F32)
    dq, dk, dv, group_part, lam_part = attend_back(
        q, kv, start, nb, lam, gain_col, o1, o2, lse, dg
    )
    group_words = jnp.concatenate(
        [
            group_part.T,
            jnp.broadcast_to(jnp.sum(lam_part), (1, VDIM)),
            jnp.zeros((6, VDIM), F32),
        ]
    )
    others = n_seq * n_dp - 1
    span = (halo + 1) * tok
    if halo <= 2:
        rows = w_query.shape[0]
        line = (n_seq, rows, 4 * width)
        acts, sums, g_attn = talk(
            functools.partial(finish_kernel, n, n_seq, n_dp, halo, nc, 2 * hidden),
            3,
            [((2, tok, cols), BF16), ((8, cols), F32), ((rows, 4 * width), F32)],
            [
                VMEM((span, cols), F32),
                VMEM((n - 1, span, cols), BF16),
                VMEM((n - 1, span, cols), BF16),
            ]
            + exchange
            + [
                VMEM((full, span), BF16),
                VMEM((full, 3 * width), BF16),
                VMEM((full, hidden), BF16),
                VMEM((full, tok), BF16),
                VMEM(line, F32),
                VMEM((max(n_dp - 1, 1),) + line, BF16),
                VMEM((max(n_dp - 1, 1),) + line, BF16),
                VMEM(line, BF16),
                VMEM((n_seq + 1, rows, 4 * width), BF16),
                stat,
                VMEM((1, cols), F32),
                VMEM((n, 8, VDIM), F32),
                VMEM((others + 1, 8, cols), F32),
                VMEM((max(halo, 1), tok, cols), BF16),
                VMEM((max(halo, 1), tok, cols), BF16),
                VMEM((tok, cols), F32),
                dma(3),
            ]
            + [dma(n - 1, (halo + 1) * nc)] * 2
            + [dma(n - 1, nc)] * 2
            + [dma(n - 1)] * 2
            + [dma(max(others, 1))] * 2
            + [dma(max(halo, 1), nc)] * 2
            + [dma(n - 1, nc)] * 2
            + [dma(max(n_dp - 1, 1), n_seq)] * 2
            + [dma(n_seq, 2)] * 3,
            6 * tok * full * width * (halo + 1),
            58,
            (n1t, w_attn, w_ffn, dq, dk, dv, dh1r, grouped, inner, h1, x, scale_one, gain_one_cols, dh1, gain_two_part, group_words),
            far=(0, 1, 2),
            kept=(3, 4, 5, 8),
        )
        input_grad, output = acts[0], acts[1]
    else:
        d_wattn = projection_grads(halo, n1t, dq, dk, dv, dh1r, grouped)
        d_wattn, g_ffn = lax.optimization_barrier((d_wattn, g_ffn))
        g_attn = lax.psum_scatter(d_wattn, ("seq", "dp"), scatter_dimension=0, tiled=True).astype(F32)
        input_grad, sums = talk(
            functools.partial(leave_kernel, n, n_seq, n_dp, halo, nc),
            3,
            [((tok, cols), BF16), ((8, cols), F32)],
            [
                VMEM((span, cols), F32),
                VMEM((n - 1, span, cols), BF16),
                VMEM((n - 1, span, cols), BF16),
                VMEM((full, 3 * width), BF16),
                stat,
                VMEM((1, cols), F32),
                VMEM((n, 8, VDIM), F32),
                VMEM((others + 1, 8, cols), F32),
                VMEM((max(halo, 1), tok, cols), BF16),
                VMEM((max(halo, 1), tok, cols), BF16),
                VMEM((tok, cols), F32),
                pltpu.SemaphoreType.DMA,
            ]
            + [dma(n - 1, (halo + 1) * nc)] * 2
            + [dma(n - 1, nc)] * 2
            + [dma(n - 1)] * 2
            + [dma(max(others, 1))] * 2
            + [dma(max(halo, 1), nc)] * 2,
            6 * tok * full * width * (halo + 1),
            26 + 5 * halo,
            (dq, dk, dv, w_attn, x, scale_one, gain_one_cols, dh1, gain_two_part, group_words),
            far=(3,),
        )
        (output,) = output
    g_query, g_key, g_value, g_output = (
        g_attn[:, i * width : (i + 1) * width] for i in range(4)
    )
    g_ffn = g_ffn.astype(F32)
    share = cols // (n_seq * n_dp)
    place = lax.axis_index("seq") * n_dp + lax.axis_index("dp")
    gains = lax.dynamic_slice_in_dim(sums[:2], place * share, share, 1)
    return (
        output[None],
        input_grad[None],
        gains[0],
        gains[1],
        sums[2, :VDIM],
        sums[3, :1],
        g_query,
        g_key,
        g_value,
        g_output,
        g_ffn[:, :hidden],
        g_ffn[:, hidden : 2 * hidden],
        g_ffn[:, 2 * hidden :],
    )


def solution(mesh):
    act = P("dp", "seq", "head")
    mat = P(("seq", "dp"), "head")
    vec = P(("head", "seq", "dp"))
    return jax.shard_map(
        functools.partial(on_device, mesh.shape["head"], mesh.shape["seq"], mesh.shape["dp"]),
        mesh=mesh,
        in_specs=(act,) + (mat,) * 7 + (P(),) * 7 + (P("dp", "seq"),) * 2 + (act,),
        out_specs=(act, act, vec, vec, P(), P()) + (mat,) * 7,
        check_vma=False,
    )
```

```python
import functools
import math

import jax
import jax.numpy as jnp
from jax import lax
from jax.experimental import pallas as pl
from jax.experimental.pallas import tpu as pltpu
from jax.sharding import PartitionSpec as P

HALF = 64
VDIM = 128
EPS = 1e-05
LAMBDA_INIT = 0.8 - 0.6 * math.exp(-0.3)
KEEP = 1.0 - LAMBDA_INIT
NEG_BIG = -1e30
MESH = pl.DeviceIdType.MESH
VMEM = pltpu.VMEM
F32 = jnp.float32
BF16 = jnp.bfloat16
NN = (((1,), (0,)), ((), ()))
NT = (((1,), (1,)), ((), ()))
TN = (((0,), (0,)), ((), ()))


def mm(a, b, dims):
    return lax.dot_general(a, b, dims, preferred_element_type=F32)


def whole():
    return pl.BlockSpec(memory_space=VMEM)


def peer_of(me, k, n):
    return lax.rem(me + k, n)


def greet(*peers):
    barrier = pltpu.get_barrier_semaphore()
    for peer in peers:
        pl.semaphore_signal(barrier, 1, device_id=peer, device_id_type=MESH)
    pl.semaphore_wait(barrier, len(peers))


def along(axis, size, steps):
    spot = lax.axis_index(axis)
    return [{axis: lax.rem(spot + k, size)} for k in steps]


def group(n):
    return along("head", n, range(1, n))


def push(src, dst, send, recv, **peer):
    return pltpu.make_async_remote_copy(
        src_ref=src,
        dst_ref=dst,
        send_sem=send,
        recv_sem=recv,
        device_id=peer,
        device_id_type=MESH,
    )


def rows_of(c, size):
    return pl.ds(pl.multiple_of(c * size, size), size)


def fetch(w_hbm, off, w_ref, sem):
    copy = pltpu.make_async_copy(w_hbm.at[:, off : off + w_ref.shape[1]], w_ref, sem)
    copy.start()
    return copy


class Reduce:
    def __init__(self, n, size, me, own_ref, sbuf, rbuf, ssem, rsem):
        self.n, self.size, self.me = n, size, me
        self.own_ref, self.sbuf, self.rbuf, self.ssem, self.rsem = own_ref, sbuf, rbuf, ssem, rsem
        self.cols = own_ref.shape[1]

    def copy(self, k, c):
        rows = rows_of(c, self.size)
        return push(
            self.sbuf.at[k - 1, rows],
            self.rbuf.at[k - 1, rows],
            self.ssem.at[k - 1, c],
            self.rsem.at[k - 1, c],
            head=peer_of(self.me, k, self.n),
        )

    def send(self, first, last, pairs):
        n = self.n

        def step(t, _):
            turn = t // n
            c = first + turn
            k = t - turn * n + 1
            rows = rows_of(c, self.size)
            peer = peer_of(self.me, k, n)
            part = None
            for a_ref, behind, w_ref, off in pairs:
                span = slice(off, off + a_ref.shape[1])
                term = mm(
                    a_ref[rows_of(c - behind, self.size), :],
                    w_ref[rows_of(peer, self.cols), span],
                    NT,
                )
                part = term if part is None else part + term

            @pl.when(k < n)
            def _():
                self.sbuf[k - 1, rows] = part.astype(BF16)
                self.copy(k, c).start()

            @pl.when(k == n)
            def _():
                self.own_ref[rows, :] = part

            return 0

        lax.fori_loop(0, (last - first) * n, step, 0)

    def relay(self, first, last):
        pass

    def take(self, c):
        rows = rows_of(c, self.size)
        total = self.own_ref[rows, :]
        for k in range(1, self.n):
            self.copy(k, c).wait_recv()
        for k in range(1, self.n):
            total = total + self.rbuf[k - 1, rows].astype(F32)
        return total

    def finish(self, first, last):
        for c in range(first, last):
            for k in range(1, self.n):
                self.copy(k, c).wait_send()


class Gather:
    def __init__(self, n, nc, me, buf, ssem, rsem):
        self.n, self.nc, self.me = n, nc, me
        self.buf, self.ssem, self.rsem = buf, ssem, rsem
        self.size = buf.shape[1] // nc

    def copy(self, k, c, source):
        rows = rows_of(c, self.size)
        return push(
            self.buf.at[source, rows],
            self.buf.at[source, rows],
            self.ssem.at[k - 1, c],
            self.rsem.at[k - 1, c],
            head=peer_of(self.me, k, self.n),
        )

    def send(self, c, value=None):
        if value is not None:
            self.buf[self.me, rows_of(c, self.size)] = value
        for k in range(1, self.n):
            self.copy(k, c, self.me).start()

    def relay(self, c):
        pass

    def take(self, c):
        for k in range(1, self.n):
            self.copy(k, c, peer_of(self.me, self.n - k, self.n)).wait_recv()

    def finish(self, only=None):
        for c in range(self.nc) if only is None else (only,):
            for k in range(1, self.n):
                self.copy(k, c, self.me).wait_send()


def square(me):
    return me + 1 - 2 * lax.rem(me, 2), lax.rem(me + 2, 4), 3 - me


class SquareReduce(Reduce):
    def copy(self, k, c, odd):
        rows = rows_of(c, self.size)
        near, far, _ = square(self.me)
        return push(
            self.sbuf.at[k - 1, rows],
            self.rbuf.at[k - 1, rows],
            self.ssem.at[k - 1, c],
            self.rsem.at[k - 1, c],
            head=far if (k == 2) != odd else near,
        )

    def send(self, first, last, pairs):
        size = self.size
        near, far, across = square(self.me)

        def step(turn, _):
            t = turn // 4
            k = turn - 4 * t
            two = rows_of(t, 2 * size)
            even, odd = rows_of(2 * t, size), rows_of(2 * t + 1, size)
            owner = jnp.where(k == 0, across, jnp.where(k == 1, near, jnp.where(k == 2, far, self.me)))
            part = None
            for a_ref, behind, w_ref, off in pairs:
                span = slice(off, off + a_ref.shape[1])
                term = mm(
                    a_ref[rows_of(t - behind // 2, 2 * size), :],
                    w_ref[rows_of(owner, self.cols), span],
                    NT,
                )
                part = term if part is None else part + term
            self.own_ref[two, :] = part

            @pl.when(k == 0)
            def _():
                self.sbuf[2, two] = part.astype(BF16)
                self.copy(3, 2 * t, False).start()
                self.copy(3, 2 * t + 1, True).start()

            @pl.when(k == 1)
            def _():
                self.sbuf[0, even] = part[:size].astype(BF16)
                self.sbuf[1, odd] = part[size:].astype(BF16)
                self.copy(1, 2 * t, False).start()

            @pl.when(k == 2)
            def _():
                self.sbuf[1, even] = part[:size].astype(BF16)
                self.sbuf[0, odd] = part[size:].astype(BF16)
                self.copy(1, 2 * t + 1, True).start()

            return 0

        lax.fori_loop(2 * first, 2 * last, step, 0)

    def relay(self, first, last):
        for c in range(first, last):
            rows = rows_of(c, self.size)
            odd = c % 2 == 1
            self.copy(3, c, odd).wait_recv()
            both = self.sbuf[1, rows].astype(F32) + self.rbuf[2, rows].astype(F32)
            self.sbuf[1, rows] = both.astype(BF16)
            self.copy(2, c, odd).start()

    def take(self, c):
        rows = rows_of(c, self.size)
        for k in (1, 2):
            self.copy(k, c, c % 2 == 1).wait_recv()
        return self.own_ref[rows, :] + self.rbuf[0, rows].astype(F32) + self.rbuf[1, rows].astype(F32)

    def finish(self, first, last):
        for c in range(first, last):
            for k in range(1, self.n):
                self.copy(k, c, c % 2 == 1).wait_send()


class SquareGather(Gather):
    def own(self, k, c):
        near, far, _ = square(self.me)
        rows = rows_of(c, self.size)
        return push(
            self.buf.at[self.me, rows],
            self.buf.at[self.me, rows],
            self.ssem.at[k - 1, c],
            self.rsem.at[k - 1, c],
            head=(near, far)[k - 1],
        )

    def came(self, k, c):
        source = square(self.me)[k - 1]
        rows = rows_of(c, self.size)
        return push(
            self.buf.at[source, rows],
            self.buf.at[source, rows],
            self.ssem.at[k - 1, c],
            self.rsem.at[k - 1, c],
            head=square(self.me)[0],
        )

    def passed(self, c):
        near, far, _ = square(self.me)
        source, to = (near, far) if c % 2 else (far, near)
        rows = rows_of(c, self.size)
        return push(
            self.buf.at[source, rows],
            self.buf.at[source, rows],
            self.ssem.at[2, c],
            self.rsem.at[2, c],
            head=to,
        )

    def send(self, c, value=None):
        if value is not None:
            self.buf[self.me, rows_of(c, self.size)] = value
        for k in (1, 2):
            self.own(k, c).start()

    def relay(self, c):
        self.came(1 if c % 2 else 2, c).wait_recv()
        self.passed(c).start()

    def take(self, c):
        self.came(2 if c % 2 else 1, c).wait_recv()
        self.came(3, c).wait_recv()

    def finish(self, only=None):
        for c in range(self.nc) if only is None else (only,):
            for k in (1, 2):
                self.own(k, c).wait_send()
            self.passed(c).wait_send()


def reducer(n, *args):
    return (SquareReduce if n == 4 else Reduce)(n, *args)


def gatherer(n, *args):
    return (SquareGather if n == 4 else Gather)(n, *args)


def norm_rows(n, buf, rows, gain_ref, out_ref, scale_ref=None, scale_rows=None):
    cols = buf.shape[2]
    total = None
    for s in range(n):
        piece = buf[s, rows].astype(F32)
        part = jnp.sum(piece * piece, axis=1, keepdims=True)
        total = part if total is None else total + part
    scale = lax.rsqrt(total / (n * cols) + EPS)
    if scale_ref is not None:
        scale_ref[rows if scale_rows is None else scale_rows, :] = scale
    for s in range(n):
        span = slice(s * cols, (s + 1) * cols)
        piece = buf[s, rows].astype(F32)
        out_ref[rows, span] = (piece * scale * gain_ref[:, span]).astype(BF16)


def spread_rows(n, buf, rows, out_ref):
    cols = buf.shape[2]
    for s in range(n):
        out_ref[rows, s * cols : (s + 1) * cols] = buf[s, rows]


def enter_kernel(n, n_seq, halo, x_ref, dy_ref, gain_ref, docs_ref, n1_ref, scale_ref, dyr_ref, window_ref, n1t_hbm, xall, dall, docs, n1t_ref, ts, xs, xr, ds, dr, hs, hr, ks, kr):
    tok = x_ref.shape[0]
    spot = lax.axis_index("seq")
    me = lax.axis_index("head")
    more = spot + 1 < n_seq
    for k in range(1, halo + 1):
        @pl.when(spot < k)
        def _():
            docs[halo - k] = jnp.zeros_like(docs_ref)

    docs[halo] = docs_ref[...]
    xall[me, halo * tok :] = x_ref[...]
    greet(*group(n), *along("seq", n_seq, range(1, n_seq)))
    xg = gatherer(n, 2 * (halo + 1), me, xall, xs, xr)
    dg = gatherer(n, 2, me, dall, ds, dr)

    def word(k):
        return push(
            docs.at[halo], docs.at[halo - k], ks.at[k - 1], kr.at[k - 1], seq=lax.rem(spot + k, n_seq)
        )

    def hop(j):
        here = pl.ds((halo - j + 1) * tok, tok)
        there = pl.ds((halo - j) * tok, tok)
        return push(
            xall.at[me, here], xall.at[me, there], hs.at[j - 1], hr.at[j - 1], seq=lax.rem(spot + 1, n_seq)
        )

    size = min(64, tok)
    per = tok // size

    def block_send(b):
        for c in (2 * b, 2 * b + 1):
            xg.send(c)

    def block_take(b):
        for c in (2 * b, 2 * b + 1):
            xg.relay(c)
        for c in (2 * b, 2 * b + 1):
            xg.take(c)
        own = b == halo

        @pl.loop(0, per)
        def _(i):
            rows = rows_of(b * per + i, size)
            if own:
                norm_rows(n, xall, rows, gain_ref, n1_ref, scale_ref, rows_of(i, size))
            else:
                norm_rows(n, xall, rows, gain_ref, n1_ref)

        rows = slice(b * tok, (b + 1) * tok)
        n1t_ref[:, rows] = n1_ref[rows, :].T

    if halo:
        @pl.when(more)
        def _():
            hop(1).start()

    block_send(halo)
    for k in range(1, halo + 1):
        @pl.when(spot + k < n_seq)
        def _():
            word(k).start()

    for j in range(1, halo + 1):
        @pl.when(spot >= j)
        def _():
            hop(j).wait_recv()

        if j < halo:
            @pl.when((spot >= j) & more)
            def _():
                hop(j + 1).start()

        @pl.when(spot >= j)
        def _():
            block_send(halo - j)

        if j == 1:
            block_take(halo)
        else:
            @pl.when(spot >= j - 1)
            def _():
                block_take(halo - j + 1)

    if not halo:
        block_take(halo)
    dg.send(0, dy_ref[: tok // 2, :])
    dg.send(1, dy_ref[tok // 2 :, :])
    if halo:
        @pl.when(spot >= halo)
        def _():
            block_take(0)

    for j in range(1, halo + 1):
        @pl.when(spot < j)
        def _():
            rows = slice((halo - j) * tok, (halo - j + 1) * tok)
            n1_ref[rows, :] = jnp.zeros((tok, n1_ref.shape[1]), BF16)
            n1t_ref[:, rows] = jnp.zeros((n1_ref.shape[1], tok), BF16)

    leave = pltpu.make_async_copy(n1t_ref, n1t_hbm, ts)
    leave.start()
    for k in range(1, halo + 1):
        @pl.when(spot >= k)
        def _():
            word(k).wait_recv()

    for k in range(halo + 1):
        window_ref[:, k * tok : (k + 1) * tok] = docs[k]
    for c in range(2):
        dg.relay(c)
    for c in range(2):
        dg.take(c)

    @pl.loop(0, per)
    def _(i):
        spread_rows(n, dall, rows_of(i, size), dyr_ref)

    for b in range(halo + 1):
        @pl.when(spot >= halo - b)
        def _():
            xg.finish(2 * b)
            xg.finish(2 * b + 1)

    for j in range(1, halo + 1):
        @pl.when((spot >= j - 1) & more)
        def _():
            hop(j).wait_send()

        @pl.when(spot + j < n_seq)
        def _():
            word(j).wait_send()

    dg.finish()
    leave.wait()


def projection_kernel(halo, n1t_ref, dq_ref, dk_ref, dv_ref, dh1r_ref, g_ref, dw_hbm, dh1t, held, sems):
    full, width = n1t_ref.shape[0], dq_ref.shape[1]
    tok = dq_ref.shape[0]
    size = min(256, full)

    def leave(i):
        return pltpu.make_async_copy(held.at[i], dw_hbm.at[:, i * width : (i + 1) * width], sems.at[i])

    def fill(i, left, right):
        @pl.loop(0, full // size)
        def _(t):
            rows = rows_of(t, size)
            held[i, rows] = mm(left[rows, :], right[...], NN).astype(BF16)

        leave(i).start()

    fill(0, n1t_ref.at[:, halo * tok :], dq_ref)
    fill(1, n1t_ref, dk_ref)
    fill(2, n1t_ref, dv_ref)
    dh1t[...] = dh1r_ref[...].T
    fill(3, dh1t, g_ref)
    for i in range(4):
        leave(i).wait()


def projection_grads(halo, n1t, dq, dk, dv, dh1r, g):
    full, (tok, width) = n1t.shape[0], dq.shape
    args = (n1t, dq, dk, dv, dh1r, g)
    return pl.pallas_call(
        functools.partial(projection_kernel, halo),
        out_shape=pltpu.HBM((full, 4 * width), BF16),
        in_specs=[whole()] * len(args),
        out_specs=pl.BlockSpec(memory_space=pltpu.HBM),
        scratch_shapes=[VMEM((full, tok), BF16), VMEM((4, full, width), BF16), dma(4)],
        cost_estimate=pl.CostEstimate(
            flops=4 * full * width * (n1t.shape[1] + tok),
            bytes_accessed=2 * full * (n1t.shape[1] + 4 * width),
            transcendentals=0,
        ),
        compiler_params=pltpu.CompilerParams(vmem_limit_bytes=40 * 2**20),
    )(*args)


def ffn_kernel(n2_ref, dy_ref, wg_ref, wu_ref, wd_ref, hid_ref, dgate_ref, dup_ref, dw_hbm, n2t, dyt, held, sems):
    j, steps = pl.program_id(0), pl.num_programs(0)

    @pl.when(j == 0)
    def _():
        n2t[...] = n2_ref[...].T
        dyt[...] = dy_ref[...].T

    size = wg_ref.shape[1]
    slot = lax.rem(j, 2)

    def leave(i, step, slot):
        start = pl.multiple_of((i * steps + step) * size, size)
        return pltpu.make_async_copy(held.at[slot, i], dw_hbm.at[:, pl.ds(start, size)], sems.at[slot, i])

    gate = mm(n2_ref[...], wg_ref[...], NN)
    upper = mm(n2_ref[...], wu_ref[...], NN)
    sigma = lax.logistic(gate)
    act = gate * sigma
    hid_ref[...] = (act * upper).astype(BF16)
    d_hid = mm(dy_ref[...], wd_ref[...], NN)
    dup_ref[...] = (d_hid * act).astype(BF16)
    dgate_ref[...] = (d_hid * upper * sigma * (1.0 + gate * (1.0 - sigma))).astype(BF16)

    @pl.when(j >= 2)
    def _():
        for i in range(3):
            leave(i, j - 2, slot).wait()

    for i, (left, right) in enumerate(((n2t, dgate_ref), (n2t, dup_ref), (dyt, hid_ref))):
        held[slot, i] = mm(left[...], right[...], NN).astype(BF16)
        leave(i, j, slot).start()

    @pl.when(j == steps - 1)
    def _():
        for i in range(3):
            leave(i, j, slot).wait()

        @pl.when(j >= 1)
        def _():
            for i in range(3):
                leave(i, j - 1, 1 - slot).wait()


def ffn(n2, dyr, w, tile):
    tok, full = n2.shape
    hidden = w.shape[1] // 3
    steps = hidden // tile
    act = pl.BlockSpec((tok, full), lambda j: (0, 0))
    part = pl.BlockSpec((tok, tile), lambda j: (0, j))
    return pl.pallas_call(
        ffn_kernel,
        grid=(steps,),
        out_shape=[pltpu.HBM((tok, hidden), BF16)] * 3
        + [pltpu.HBM((full, 3 * hidden), BF16)],
        in_specs=[act, act]
        + [pl.BlockSpec((full, tile), functools.partial(lambda i, j: (0, i * steps + j), i)) for i in range(3)],
        out_specs=[part] * 3 + [pl.BlockSpec(memory_space=pltpu.HBM)],
        scratch_shapes=[
            VMEM((full, tok), BF16),
            VMEM((full, tok), BF16),
            VMEM((2, 3, full, tile), BF16),
            dma(2, 3),
        ],
        cost_estimate=pl.CostEstimate(
            flops=12 * tok * full * hidden,
            bytes_accessed=12 * full * hidden,
            transcendentals=tok * hidden,
        ),
        compiler_params=pltpu.CompilerParams(vmem_limit_bytes=40 * 2**20),
    )(n2, far_away(dyr), *(far_away(w),) * 3)


def middle_kernel(n, nc, off, g_ref, w_hbm, x_ref, gain_ref, h1_ref, n2_ref, scale_ref, own, sbuf, rbuf, w_ref, hall, ws, s1, r1, s2, r2):
    load = fetch(w_hbm, off, w_ref, ws)
    greet(*group(n))
    me = lax.axis_index("head")
    red = reducer(n, own.shape[0] // nc, me, own, sbuf, rbuf, s1, r1)
    gat = gatherer(n, nc, me, hall, s2, r2)
    load.wait()
    red.send(0, nc, [(g_ref, 0, w_ref, 0)])
    red.relay(0, nc)
    for c in range(nc):
        rows = rows_of(c, red.size)
        h1 = red.take(c) + x_ref[rows, :].astype(F32)
        h1_ref[rows, :] = h1
        gat.send(c, h1.astype(BF16))
    size = min(64, red.size)
    for c in range(nc):
        gat.relay(c)
    for c in range(nc):
        gat.take(c)

        @pl.loop(0, red.size // size)
        def _(i):
            norm_rows(n, hall, pl.ds(pl.multiple_of(c * red.size + i * size, size), size), gain_ref, n2_ref, scale_ref)

    red.finish(0, nc)
    gat.finish()


class Stats:
    def __init__(self, n, nc, me, buf, ssem, rsem):
        self.n, self.nc, self.me = n, nc, me
        self.buf, self.ssem, self.rsem = buf, ssem, rsem

    def copy(self, k, c, source):
        return push(
            self.buf.at[source, c],
            self.buf.at[source, c],
            self.ssem.at[k - 1, c],
            self.rsem.at[k - 1, c],
            head=peer_of(self.me, k, self.n),
        )

    def send(self, c, value):
        size, cols = value.shape
        part = value[:, :128]
        for j in range(1, cols // 128):
            part = part + value[:, j * 128 : (j + 1) * 128]
        line = jnp.sum(part.T, axis=0, keepdims=True)
        self.buf[self.me, c] = jnp.broadcast_to(line, (8, size))
        for k in range(1, self.n):
            self.copy(k, c, self.me).start()

    def take(self, c):
        for k in range(1, self.n):
            self.copy(k, c, peer_of(self.me, self.n - k, self.n)).wait_recv()
        total = self.buf[0, c]
        for s in range(1, self.n):
            total = total + self.buf[s, c]
        size = total.shape[1]
        tall = jnp.broadcast_to(total[:1, :], (128, size))
        return tall.T[:, :1]

    def finish(self):
        for c in range(self.nc):
            for k in range(1, self.n):
                self.copy(k, c, self.me).wait_send()


def norm_back(nc, size, width, grad_of, keep, sta, unit_of, gain_ref, base_of, gain_grad_ref, done):
    for c in range(nc):
        rows = rows_of(c, size)
        grad = grad_of(c)
        keep[rows, :] = grad
        unit = unit_of(rows)
        part = jnp.sum(grad * unit, axis=0, keepdims=True)
        if c == 0:
            gain_grad_ref[...] = part
        else:
            gain_grad_ref[...] += part
        sta.send(c, grad * gain_ref[...] * unit)
    for c in range(nc):
        rows = rows_of(c, size)
        dots = sta.take(c) / width
        scaled = keep[rows, :] * gain_ref[...]
        done(c, rows, base_of(rows, scaled - unit_of(rows) * dots))


def back_kernel(n, nc, off, down, dgate_ref, dup_ref, hid_ref, w_hbm, h1_ref, scale_ref, gain_ref, dy_ref, dh1_ref, dh1r_ref, gain_grad_ref, *refs):
    output_ref = None
    if down is not None:
        output_ref, osum, osend, orecv, wd_ref, wds, s4, r4, *refs = refs
        load_down = fetch(w_hbm, down, wd_ref, wds)
    own, sbuf, rbuf, w_ref, stat, dall, ws, s1, r1, s2, r2, s3, r3 = refs
    load = fetch(w_hbm, off, w_ref, ws)
    greet(*group(n))
    me = lax.axis_index("head")
    pairs = [(dgate_ref, 0, w_ref, 0), (dup_ref, 0, w_ref, dgate_ref.shape[1])]
    size = own.shape[0] // nc
    red = reducer(n, size, me, own, sbuf, rbuf, s1, r1)
    sta = Stats(n, nc, me, stat, s2, r2)
    if down is not None:
        last = reducer(n, size, me, osum, osend, orecv, s4, r4)
    load.wait()
    gat = gatherer(n, nc, me, dall, s3, r3)
    red.send(0, nc, pairs)
    red.relay(0, nc)

    def unit_of(rows):
        return h1_ref[rows, :].astype(BF16).astype(F32) * scale_ref[rows, :]

    def base_of(rows, back):
        return dy_ref[rows, :] + scale_ref[rows, :] * back

    def done(c, rows, value):
        dh1_ref[rows, :] = value
        gat.send(c, value.astype(BF16))

    norm_back(nc, size, n * red.cols, red.take, own, sta, unit_of, gain_ref, base_of, gain_grad_ref, done)
    for c in range(nc):
        gat.relay(c)
    if down is not None:
        load_down.wait()
        last.send(0, nc, [(hid_ref, 0, wd_ref, 0)])
    for c in range(nc):
        gat.take(c)
        spread_rows(n, dall, rows_of(c, red.size), dh1r_ref)
    if down is not None:
        last.relay(0, nc)
        for c in range(nc):
            rows = rows_of(c, size)
            output_ref[rows, :] = (last.take(c) + h1_ref[rows, :]).astype(BF16)
        last.finish(0, nc)
    red.finish(0, nc)
    sta.finish()
    gat.finish()


def leave_kernel(n, n_seq, n_dp, halo, nc, dq_ref, dk_ref, dv_ref, w_hbm, x_ref, scale_ref, gain_ref, dh1_ref, gain_two_ref, group_ref, out_ref, sums_ref, own, sbuf, rbuf, w_ref, stat, gain_s, words, sums, zsend, zrecv, keep, ws, s1, r1, s2, r2, s3, r3, s4, r4, s5, r5):
    load = fetch(w_hbm, 0, w_ref, ws)
    spot, core = lax.axis_index("seq"), lax.axis_index("dp")
    others = [(i, j) for i in range(n_seq) for j in range(n_dp) if i or j]

    def of(i, j):
        return {"seq": lax.rem(spot + i, n_seq), "dp": lax.rem(core + j, n_dp)}

    def sends(j):
        return spot >= halo - j + 1

    def comes(j):
        return (spot + 1 < n_seq) & (spot + 1 >= halo - j + 1)

    for j in range(1, halo + 1):
        @pl.when(jnp.logical_not(comes(j)))
        def _():
            zrecv[j - 1] = jnp.zeros(zrecv.shape[1:], BF16)

    me = lax.axis_index("head")
    words[me] = group_ref[...]
    greet(*group(n), *(of(i, j) for i, j in others))
    tok, width = dq_ref.shape
    size = tok // nc
    red = reducer(n, size, me, own, sbuf, rbuf, s1, r1)
    sta = Stats(n, nc, me, stat, s2, r2)

    def word(k, source):
        return push(
            words.at[source], words.at[source], s3.at[k - 1], r3.at[k - 1], head=peer_of(me, k, n)
        )

    def hop(j, c):
        rows = pl.ds(c * size, size)
        return push(
            zsend.at[j - 1, rows], zrecv.at[j - 1, rows], s5.at[j - 1, c], r5.at[j - 1, c], seq=lax.rem(spot + n_seq - 1, n_seq)
        )

    for k in range(1, n):
        word(k, me).start()
    load.wait()
    pairs = [(dk_ref, 0, w_ref, width), (dv_ref, 0, w_ref, 2 * width)]
    for b in range(halo):
        @pl.when(sends(b + 1))
        def _():
            red.send(b * nc, (b + 1) * nc, pairs)

    red.send(halo * nc, (halo + 1) * nc, [(dq_ref, halo * nc, w_ref, 0)] + pairs)

    for b in range(halo):
        @pl.when(sends(b + 1))
        def _():
            red.relay(b * nc, (b + 1) * nc)

    red.relay(halo * nc, (halo + 1) * nc)

    def total(b, c):
        value = red.take(b * nc + c)
        if b == 0:
            return value

        @pl.when(comes(b))
        def _():
            hop(b, c).wait_recv()

        return value + zrecv[b - 1, pl.ds(c * size, size)].astype(F32)

    for j in range(1, halo + 1):
        for c in range(nc):
            @pl.when(sends(j))
            def _():
                zsend[j - 1, pl.ds(c * size, size)] = total(j - 1, c).astype(BF16)
                hop(j, c).start()

            if j > 1:
                @pl.when(jnp.logical_not(sends(j)) & comes(j - 1))
                def _():
                    hop(j - 1, c).wait_recv()

    def unit_of(rows):
        return x_ref[rows, :].astype(F32) * scale_ref[rows, :]

    def base_of(rows, back):
        return dh1_ref[rows, :] + scale_ref[rows, :] * back

    def done(c, rows, value):
        out_ref[rows, :] = value.astype(BF16)

    norm_back(nc, size, n * red.cols, functools.partial(total, halo), keep, sta, unit_of, gain_ref, base_of, gain_s, done)
    for k in range(1, n):
        word(k, peer_of(me, n - k, n)).wait_recv()
    total = words[0]
    for k in range(1, n):
        total = total + words[k]
    place = spot * n_dp + core
    mine = sums.at[place]
    cols = gain_s.shape[1]
    mine[...] = jnp.zeros((8, cols), F32)
    mine[0:1, :] = gain_s[...]
    mine[1:2, :] = gain_two_ref[...]
    mine[2:4, : total.shape[1]] = total[0:2]

    def share(t):
        i, j = others[t]
        return push(mine, mine, s4.at[t], r4.at[t], **of(i, j))

    def await_from(t):
        i, j = others[t]
        back = lax.rem(spot + n_seq - i, n_seq) * n_dp + lax.rem(core + n_dp - j, n_dp)
        theirs = sums.at[back]
        return push(theirs, theirs, s4.at[t], r4.at[t], **of(i, j))

    for t in range(len(others)):
        share(t).start()
    for t in range(len(others)):
        await_from(t).wait_recv()
    total = sums[0]
    for t in range(1, n_seq * n_dp):
        total = total + sums[t]
    sums_ref[...] = total
    for b in range(halo):
        @pl.when(sends(b + 1))
        def _():
            red.finish(b * nc, (b + 1) * nc)
            for c in range(nc):
                hop(b + 1, c).wait_send()

    red.finish(halo * nc, (halo + 1) * nc)
    sta.finish()
    for k in range(1, n):
        word(k, me).wait_send()
    for t in range(len(others)):
        share(t).wait_send()


def finish_kernel(n, n_seq, n_dp, halo, nc, off, n1t_hbm, w_hbm, wd_hbm, dq_ref, dk_ref, dv_ref, dh1r_ref, g_ref, hid_ref, h1_ref, x_ref, scale_ref, gain_ref, dh1_ref, gain_two_ref, group_ref, acts_ref, sums_ref, grads_ref, own, sbuf, rbuf, osum, osend, orecv, n1t_ref, w_ref, wd_ref, dh1t, mine, given, taken, sent, came, stat, gain_s, words, sums, zsend, zrecv, keep, load_sem, s1, r1, s2, r2, s3, r3, s4, r4, s5, r5, s6, r6, s7, r7, s8, rl, rr):
    loads = [
        fetch(n1t_hbm, 0, n1t_ref, load_sem.at[0]),
        fetch(w_hbm, 0, w_ref, load_sem.at[1]),
        fetch(wd_hbm, off, wd_ref, load_sem.at[2]),
    ]
    spot, core = lax.axis_index("seq"), lax.axis_index("dp")
    me = lax.axis_index("head")
    tok, width = dq_ref.shape
    size = tok // nc
    share = mine.shape[1]
    others = [(i, j) for i in range(n_seq) for j in range(n_dp) if i or j]

    def of(i, j):
        return {"seq": lax.rem(spot + i, n_seq), "dp": lax.rem(core + j, n_dp)}

    def sends(j):
        return spot >= halo - j + 1

    def comes(j):
        return (spot + 1 < n_seq) & (spot + 1 >= halo - j + 1)

    for j in range(1, halo + 1):
        @pl.when(jnp.logical_not(comes(j)))
        def _():
            zrecv[j - 1] = jnp.zeros(zrecv.shape[1:], BF16)

    words[me] = group_ref[...]
    dh1t[...] = dh1r_ref[...].T
    greet(*group(n), *(of(i, j) for i, j in others))
    red = reducer(n, size, me, own, sbuf, rbuf, s1, r1)
    sta = Stats(n, nc, me, stat, s2, r2)
    last = reducer(n, size, me, osum, osend, orecv, s6, r6)

    def word(k, source):
        return push(
            words.at[source], words.at[source], s3.at[k - 1], r3.at[k - 1], head=peer_of(me, k, n)
        )

    def hop(j, c):
        rows = pl.ds(c * size, size)
        return push(
            zsend.at[j - 1, rows], zrecv.at[j - 1, rows], s5.at[j - 1, c], r5.at[j - 1, c], seq=lax.rem(spot + n_seq - 1, n_seq)
        )

    for k in range(1, n):
        word(k, me).start()

    def block_grads(i, c, ref):
        rows = rows_of(i * n_dp + c, share)
        ref[:, :width] = mm(n1t_ref[rows, halo * tok :], dq_ref[...], NN).astype(ref.dtype)
        ref[:, width : 2 * width] = mm(n1t_ref[rows, :], dk_ref[...], NN).astype(ref.dtype)
        ref[:, 2 * width : 3 * width] = mm(n1t_ref[rows, :], dv_ref[...], NN).astype(ref.dtype)
        ref[:, 3 * width :] = mm(dh1t[rows, :], g_ref[...], NN).astype(ref.dtype)

    def give(k, i):
        return push(
            given.at[k - 1, i], taken.at[k - 1, i], s7.at[k - 1, i], r7.at[k - 1, i], dp=lax.rem(core + k, n_dp)
        )

    def block_relay(b):
        if b == halo:
            red.relay(b * nc, (b + 1) * nc)
        else:
            @pl.when(sends(b + 1))
            def _():
                red.relay(b * nc, (b + 1) * nc)

    loads[1].wait()
    pairs = [(dk_ref, 0, w_ref, width), (dv_ref, 0, w_ref, 2 * width)]
    for b in range(halo):
        @pl.when(sends(b + 1))
        def _():
            red.send(b * nc, (b + 1) * nc, pairs)

    loads[0].wait()
    for k in range(1, n_dp):

        @pl.loop(0, n_seq)
        def _(i):
            block_grads(i, lax.rem(core + k, n_dp), given.at[k - 1, i])
            give(k, i).start()

    @pl.loop(0, n_seq)
    def _(i):
        block_grads(i, core, mine.at[i])

    half = mine.shape[2] // 2

    def chip(d, p):
        cols = slice(p * half, (p + 1) * half)
        value = mine[d, :, cols]
        for k in range(1, n_dp):
            if p == 0:
                give(k, d).wait_recv()
            value = value + taken[k - 1, d, :, cols].astype(F32)
        return value

    def piece(d, p, slot, sem, to):
        cols = slice(p * half, (p + 1) * half)
        return push(sent.at[d, :, cols], came.at[slot, :, cols], s8.at[d, p], sem.at[d, p], seq=to)

    def right(d, p):
        return piece(d, p, d, rl, lax.rem(spot + 1, n_seq))

    def left(d, p):
        return piece(d, p, jnp.where(spot - 1 == d, n_seq, d), rr, lax.rem(spot + n_seq - 1, n_seq))

    def arrived(d, p, slot, sem):
        return piece(d, p, slot, sem, lax.rem(spot + 1, n_seq))

    def start_line(i, p):
        cols = slice(p * half, (p + 1) * half)
        d = n_seq - 1 - i

        @pl.when(spot == 0)
        def _():
            if i:
                right(d + 1, p).wait_send()
            sent[d, :, cols] = chip(d, p).astype(BF16)
            right(d, p).start()

        @pl.when(spot == n_seq - 1)
        def _():
            if i:
                left(i - 1, p).wait_send()
            sent[i, :, cols] = chip(i, p).astype(BF16)
            left(i, p).start()

    def pass_line(i, p):
        cols = slice(p * half, (p + 1) * half)
        d = n_seq - 1 - i

        @pl.when((spot > 0) & (d > spot))
        def _():
            arrived(d, p, d, rl).wait_recv()
            sent[d, :, cols] = (chip(d, p) + came[d, :, cols].astype(F32)).astype(BF16)
            right(d, p).start()

        @pl.when((spot < n_seq - 1) & (i < spot))
        def _():
            arrived(i, p, i, rr).wait_recv()
            sent[i, :, cols] = (chip(i, p) + came[i, :, cols].astype(F32)).astype(BF16)
            left(i, p).start()

    def total(b, c):
        value = red.take(b * nc + c)
        if b == 0:
            return value

        @pl.when(comes(b))
        def _():
            hop(b, c).wait_recv()

        return value + zrecv[b - 1, pl.ds(c * size, size)].astype(F32)

    def send_hop(j):
        for c in range(nc):
            @pl.when(sends(j))
            def _():
                zsend[j - 1, pl.ds(c * size, size)] = total(j - 1, c).astype(BF16)
                hop(j, c).start()

            if j > 1:
                @pl.when(jnp.logical_not(sends(j)) & comes(j - 1))
                def _():
                    hop(j - 1, c).wait_recv()

    for p in range(2):
        if n_seq > 1:
            start_line(0, p)
    for b in range(halo):
        block_relay(b)
    red.send(halo * nc, (halo + 1) * nc, [(dq_ref, halo * nc, w_ref, 0)] + pairs)
    for t in range(max(n_seq - 1, 1)):
        if t < halo:
            send_hop(t + 1)
        for p in range(2):
            if t < n_seq - 1:
                pass_line(t, p)
            if t + 1 < n_seq - 1:
                start_line(t + 1, p)
        if t == 0:
            block_relay(halo)
            loads[2].wait()
            last.send(0, nc, [(hid_ref, 0, wd_ref, 0)])

    def unit_of(rows):
        return x_ref[rows, :].astype(F32) * scale_ref[rows, :]

    def base_of(rows, back):
        return dh1_ref[rows, :] + scale_ref[rows, :] * back

    def done(c, rows, value):
        acts_ref[0, rows, :] = value.astype(BF16)

    norm_back(nc, size, n * red.cols, functools.partial(total, halo), keep, sta, unit_of, gain_ref, base_of, gain_s, done)
    for k in range(1, n):
        word(k, peer_of(me, n - k, n)).wait_recv()
    group_sum = words[0]
    for k in range(1, n):
        group_sum = group_sum + words[k]
    place = spot * n_dp + core
    slip = sums.at[place]
    cols = gain_s.shape[1]
    slip[...] = jnp.zeros((8, cols), F32)
    slip[0:1, :] = gain_s[...]
    slip[1:2, :] = gain_two_ref[...]
    slip[2:4, : group_sum.shape[1]] = group_sum[0:2]

    def hand(t):
        i, j = others[t]
        return push(slip, slip, s4.at[t], r4.at[t], **of(i, j))

    def handed(t):
        i, j = others[t]
        back = lax.rem(spot + n_seq - i, n_seq) * n_dp + lax.rem(core + n_dp - j, n_dp)
        theirs = sums.at[back]
        return push(theirs, theirs, s4.at[t], r4.at[t], **of(i, j))

    for t in range(len(others)):
        hand(t).start()
    last.relay(0, nc)
    for c in range(nc):
        rows = rows_of(c, size)
        acts_ref[1, rows, :] = (last.take(c) + h1_ref[rows, :]).astype(BF16)
    for p in range(2):
        cols = slice(p * half, (p + 1) * half)
        mine[spot, :, cols] = chip(spot, p)

        @pl.when(spot > 0)
        def _():
            arrived(spot, p, spot, rl).wait_recv()
            mine[spot, :, cols] = mine[spot, :, cols] + came[spot, :, cols].astype(F32)

        @pl.when(spot < n_seq - 1)
        def _():
            arrived(spot, p, n_seq, rr).wait_recv()
            mine[spot, :, cols] = mine[spot, :, cols] + came[n_seq, :, cols].astype(F32)

    grads_ref[...] = mine[spot]
    for t in range(len(others)):
        handed(t).wait_recv()
    full_sum = sums[0]
    for t in range(1, n_seq * n_dp):
        full_sum = full_sum + sums[t]
    sums_ref[...] = full_sum
    for b in range(halo):
        @pl.when(sends(b + 1))
        def _():
            red.finish(b * nc, (b + 1) * nc)
            for c in range(nc):
                hop(b + 1, c).wait_send()

    red.finish(halo * nc, (halo + 1) * nc)
    last.finish(0, nc)
    sta.finish()
    for k in range(1, n):
        word(k, me).wait_send()
    for t in range(len(others)):
        hand(t).wait_send()
    for k in range(1, n_dp):
        for i in range(n_seq):
            give(k, i).wait_send()
    for d in range(n_seq):
        for p in range(2):

            @pl.when((spot < d) & ((spot > 0) | (d == 1)))
            def _():
                right(d, p).wait_send()

            @pl.when((spot > d) & ((spot < n_seq - 1) | (d == n_seq - 2)))
            def _():
                left(d, p).wait_send()


def far_away(x):
    return pltpu.with_memory_space_constraint(x, pltpu.HBM)


def dma(*dims):
    return pltpu.SemaphoreType.DMA(dims)


def talk(kernel, ident, outs, scratch, flops, room, args, far=(), far_outs=(), kept=(), kept_outs=()):
    return pl.pallas_call(
        kernel,
        out_shape=[
            pltpu.HBM(s, d) if i in far_outs or i in kept_outs else jax.ShapeDtypeStruct(s, d)
            for i, (s, d) in enumerate(outs)
        ],
        in_specs=[
            pl.BlockSpec(memory_space=pltpu.HBM) if i in far else whole() for i in range(len(args))
        ],
        out_specs=[
            pl.BlockSpec(memory_space=pltpu.HBM) if i in far_outs else whole()
            for i in range(len(outs))
        ],
        scratch_shapes=scratch,
        cost_estimate=pl.CostEstimate(flops=flops, bytes_accessed=40 * 2**20, transcendentals=0),
        compiler_params=pltpu.CompilerParams(
            collective_id=ident, has_side_effects=True, vmem_limit_bytes=room * 2**20
        ),
    )(*(far_away(a) if i in far or i in kept else a for i, a in enumerate(args)))


def forward_kernel(base, nb_ref, lam_ref, q_ref, k_ref, v_ref, start_ref, gain_ref, o1_ref, o2_ref, lse_ref, g_ref, held, m_s, l_s, acc):
    size = q_ref.shape[0]
    qt = pl.program_id(1)
    q = q_ref[...] * 0.125
    lane = lax.broadcasted_iota(jnp.int32, q.shape, 1)
    zero = jnp.zeros_like(q)
    parts = (jnp.where(lane < HALF, q, zero), jnp.where(lane >= HALF, q, zero))
    key = lax.broadcasted_iota(jnp.int32, (size, size), 0)
    query = lax.broadcasted_iota(jnp.int32, (size, size), 1)
    start = start_ref[...]

    count = nb_ref[qt]

    def scores(d, first):
        where = base + qt - d
        k = k_ref[rows_of(where, size), :]
        allowed = key >= start - where * size
        if first:
            allowed = allowed & (key <= query)
        for m in range(2):
            s = jnp.where(allowed, mm(k, parts[m], NT), NEG_BIG)
            held[d, m] = s
            top = jnp.max(s, axis=0, keepdims=True)
            m_s[m] = top if first else jnp.maximum(m_s[m], top)

    def weights(d, _):
        for m in range(2):
            e = jnp.exp(held[d, m] - m_s[m])
            held[d, m] = e
            l_s[m] += jnp.sum(e, axis=0, keepdims=True)
        return 0

    def mix(d, first):
        v = v_ref[rows_of(base + qt - d, size), :]
        for m in range(2):
            term = mm(v, (held[d, m] * l_s[m]).astype(BF16), TN)
            if first:
                acc[m] = term
            else:
                acc[m] += term

    def each(step):
        def body(d, _):
            step(d, False)
            return 0

        step(0, True)
        lax.fori_loop(1, count, body, 0)

    each(scores)
    l_s[...] = jnp.zeros_like(l_s)
    lax.fori_loop(0, count, weights, 0)
    for m in range(2):
        lse_ref[0, m : m + 1, :] = m_s[m] + jnp.log(l_s[m])
        l_s[m] = 1.0 / l_s[m]
    each(mix)
    o1, o2 = acc[0], acc[1]
    o1_ref[...] = o1
    o2_ref[...] = o2
    diff = o1 - lam_ref[0] * o2
    scale = lax.rsqrt(jnp.mean(diff * diff, axis=0, keepdims=True) + EPS)
    g = diff * scale * gain_ref[...] * KEEP
    g_ref[...] = g.T.astype(BF16)


def backward_kernel(base, nb_ref, lam_ref, q_ref, k_ref, v_ref, start_ref, gain_ref, o1_ref, o2_ref, lse_ref, dg_ref, dq_ref, dk_ref, dv_ref, gain_grad_ref, lam_grad_ref, dq_s, dk_s, dv_s):
    size = q_ref.shape[0]
    h, qt = pl.program_id(0), pl.program_id(1)
    lam = lam_ref[0]

    @pl.when((h == 0) & (qt == 0))
    def _():
        gain_grad_ref[...] = jnp.zeros_like(gain_grad_ref)
        lam_grad_ref[...] = jnp.zeros_like(lam_grad_ref)

    @pl.when(qt == 0)
    def _():
        dk_s[...] = jnp.zeros_like(dk_s)
        dv_s[...] = jnp.zeros_like(dv_s)

    o1, o2 = o1_ref[...], o2_ref[...]
    diff = o1 - lam * o2
    scale = lax.rsqrt(jnp.mean(diff * diff, axis=0, keepdims=True) + EPS)
    unit = diff * scale
    dg = dg_ref[...].T
    gain_grad_ref[...] += jnp.sum(dg * unit, axis=1, keepdims=True) * KEEP
    du = dg * gain_ref[...] * KEEP
    do = scale * (du - unit * jnp.mean(du * unit, axis=0, keepdims=True))
    lam_grad_ref[...] -= jnp.sum(do * o2, axis=1, keepdims=True)
    grads = (do.astype(BF16), (-lam * do).astype(BF16))
    deltas = tuple(
        jnp.sum(g.astype(F32) * o, axis=0, keepdims=True) for g, o in zip(grads, (o1, o2))
    )
    q = q_ref[...] * 0.125
    lane = lax.broadcasted_iota(jnp.int32, q.shape, 1)
    zero = jnp.zeros_like(q)
    parts = (jnp.where(lane < HALF, q, zero), jnp.where(lane >= HALF, q, zero))
    key = lax.broadcasted_iota(jnp.int32, (size, size), 0)
    query = lax.broadcasted_iota(jnp.int32, (size, size), 1)
    start = start_ref[...]
    dq_s[...] = jnp.zeros_like(dq_s)

    def block(where, first):
        rows = rows_of(where, size)
        k, v = k_ref[rows, :], v_ref[rows, :]
        halves = (jnp.where(lane < HALF, k, zero), jnp.where(lane >= HALF, k, zero))
        allowed = key >= start - where * size
        if first:
            allowed = allowed & (key <= query)
        dq = dq_s[...]
        dk = dk_s[rows, :]
        dv = dv_s[rows, :]
        for m in range(2):
            s = mm(k, parts[m], NT)
            p = jnp.where(allowed, jnp.exp(s - lse_ref[0, m : m + 1, :]), 0.0)
            dp = mm(v, grads[m], NN)
            ds = (p * (dp - deltas[m])).astype(BF16)
            dq = dq + mm(halves[m], ds, TN)
            dk = dk + mm(ds, parts[m], NN)
            dv = dv + mm(p.astype(BF16), grads[m], NT)
        dq_s[...] = dq
        dk_s[rows, :] = dk
        dv_s[rows, :] = dv

    block(base + qt, True)

    def earlier(d, _):
        block(base + qt - d, False)
        return 0

    lax.fori_loop(1, nb_ref[qt], earlier, 0)
    dq_ref[...] = (dq_s[...] * 0.125).T.astype(BF16)

    @pl.when(qt == pl.num_programs(1) - 1)
    def _():
        dk_ref[...] = dk_s[...].astype(BF16)
        dv_ref[...] = dv_s[...].astype(BF16)


SMEM = pl.BlockSpec(memory_space=pltpu.SMEM)
TILE = 256


def attend(q, kv, start, nb, lam, gain_col):
    tok, width = q.shape
    heads = width // VDIM
    rows = kv.shape[0]
    size = min(TILE, tok)
    base = (rows - tok) // size
    head_block = pl.BlockSpec((VDIM, size), lambda h, t: (h, t))
    return pl.pallas_call(
        functools.partial(forward_kernel, base),
        grid=(heads, tok // size),
        out_shape=[
            jax.ShapeDtypeStruct((width, tok), F32),
            jax.ShapeDtypeStruct((width, tok), F32),
            jax.ShapeDtypeStruct((heads, 2, tok), F32),
            jax.ShapeDtypeStruct((tok, width), BF16),
        ],
        in_specs=[
            SMEM,
            SMEM,
            pl.BlockSpec((size, VDIM), lambda h, t: (t, h)),
            pl.BlockSpec((rows, VDIM), lambda h, t: (0, h)),
            pl.BlockSpec((rows, VDIM), lambda h, t: (0, heads + h)),
            pl.BlockSpec((1, size), lambda h, t: (0, t)),
            pl.BlockSpec((VDIM, 1), lambda h, t: (0, 0)),
        ],
        out_specs=[
            head_block,
            head_block,
            pl.BlockSpec((1, 2, size), lambda h, t: (h, 0, t)),
            pl.BlockSpec((size, VDIM), lambda h, t: (t, h)),
        ],
        scratch_shapes=[
            VMEM((rows // size, 2, size, size), F32),
            VMEM((2, 1, size), F32),
            VMEM((2, 1, size), F32),
            VMEM((2, VDIM, size), F32),
        ],
        cost_estimate=pl.CostEstimate(
            flops=4 * tok * rows * heads * VDIM,
            bytes_accessed=8 * tok * width + 4 * rows * width,
            transcendentals=2 * tok * rows * heads,
        ),
        compiler_params=pltpu.CompilerParams(vmem_limit_bytes=32 * 2**20),
    )(nb, lam, q, kv, kv, start, gain_col)


def halo_room(rows, tok):
    return 2 * (rows // tok)


def attend_back(q, kv, start, nb, lam, gain_col, o1, o2, lse, dg):
    tok, width = q.shape
    heads = width // VDIM
    rows = kv.shape[0]
    size = min(TILE, tok)
    base = (rows - tok) // size
    head_block = pl.BlockSpec((VDIM, size), lambda h, t: (h, t))
    return pl.pallas_call(
        functools.partial(backward_kernel, base),
        grid=(heads, tok // size),
        out_shape=[
            pltpu.HBM((tok, width), BF16),
            pltpu.HBM((rows, width), BF16),
            pltpu.HBM((rows, width), BF16),
            jax.ShapeDtypeStruct((VDIM, 1), F32),
            jax.ShapeDtypeStruct((VDIM, 1), F32),
        ],
        in_specs=[
            SMEM,
            SMEM,
            pl.BlockSpec((size, VDIM), lambda h, t: (t, h)),
            pl.BlockSpec((rows, VDIM), lambda h, t: (0, h)),
            pl.BlockSpec((rows, VDIM), lambda h, t: (0, heads + h)),
            pl.BlockSpec((1, size), lambda h, t: (0, t)),
            pl.BlockSpec((VDIM, 1), lambda h, t: (0, 0)),
            head_block,
            head_block,
            pl.BlockSpec((1, 2, size), lambda h, t: (h, 0, t)),
            pl.BlockSpec((size, VDIM), lambda h, t: (t, h)),
        ],
        out_specs=[
            pl.BlockSpec((size, VDIM), lambda h, t: (t, h)),
            pl.BlockSpec((rows, VDIM), lambda h, t: (0, h)),
            pl.BlockSpec((rows, VDIM), lambda h, t: (0, h)),
            pl.BlockSpec((VDIM, 1), lambda h, t: (0, 0)),
            pl.BlockSpec((VDIM, 1), lambda h, t: (0, 0)),
        ],
        scratch_shapes=[
            VMEM((VDIM, size), F32),
            VMEM((rows, VDIM), F32),
            VMEM((rows, VDIM), F32),
        ],
        cost_estimate=pl.CostEstimate(
            flops=10 * tok * rows * heads * VDIM,
            bytes_accessed=16 * tok * width + 8 * rows * width,
            transcendentals=2 * tok * rows * heads,
        ),
        compiler_params=pltpu.CompilerParams(vmem_limit_bytes=(12 + halo_room(rows, tok)) * 2**20),
    )(nb, lam, q, kv, kv, start, gain_col, o1, o2, lse, dg)


CHUNKS = 2


def on_device(
    n_head,
    n_seq,
    n_dp,
    inputs,
    w_query,
    w_key,
    w_value,
    w_output,
    w_gate,
    w_up,
    w_down,
    gain_attn,
    gain_ffn,
    group_gain,
    lambda_q1,
    lambda_k1,
    lambda_q2,
    lambda_k2,
    doc_ids,
    needles,
    out_grad,
):
    x = inputs[0]
    tok, cols = x.shape
    n, nc = n_head, CHUNKS
    full = n * cols
    width = w_query.shape[1]
    hidden = w_gate.shape[1]
    me = lax.axis_index("head")
    halo = n_seq // 2

    w_attn = lax.all_gather(
        jnp.concatenate([w_query, w_key, w_value, w_output], axis=1),
        ("seq", "dp"),
        axis=0,
        tiled=True,
    )
    w_ffn = lax.all_gather(
        jnp.concatenate([w_gate, w_up, w_down], axis=1), ("seq", "dp"), axis=0, tiled=True
    )

    weight = jnp.where(needles[0] == 1, 1.0, 0.1).astype(F32)
    dy = out_grad[0].astype(F32) * weight[:, None]
    gain_one = gain_attn[None, :]
    gain_two = gain_ffn[None, :]
    gain_one_cols = lax.dynamic_slice_in_dim(gain_one, me * cols, cols, 1)
    gain_two_cols = lax.dynamic_slice_in_dim(gain_two, me * cols, cols, 1)
    lam = jnp.exp(jnp.sum(lambda_q1 * lambda_k1)) - jnp.exp(jnp.sum(lambda_q2 * lambda_k2))
    lam = (lam + LAMBDA_INIT)[None]
    gain_col = group_gain[:, None]

    docs = jnp.broadcast_to(doc_ids + 1, (8, tok))
    n1, scale_one, dyr, window, n1t = talk(
        functools.partial(enter_kernel, n, n_seq, halo),
        0,
        [
            (((halo + 1) * tok, full), BF16),
            ((tok, 1), F32),
            ((tok, full), BF16),
            ((8, (halo + 1) * tok), jnp.int32),
            ((full, (halo + 1) * tok), BF16),
        ],
        [
            VMEM((n, (halo + 1) * tok, cols), BF16),
            VMEM((n, tok, cols), BF16),
            VMEM((halo + 1, 8, tok), jnp.int32),
            VMEM((full, (halo + 1) * tok), BF16),
            pltpu.SemaphoreType.DMA,
        ]
        + [dma(n - 1, 2 * (halo + 1))] * 2
        + [dma(n - 1, 2)] * 2
        + [dma(max(halo, 1))] * 4,
        tok * full * 8,
        14 + 4 * (halo + 1),
        (x, dy.astype(BF16), gain_one, docs),
        far_outs=(4,),
        kept_outs=(2,),
    )
    start = jnp.sum((window[0][None, :] < docs[0][:, None]).astype(jnp.int32), axis=1)
    size = min(TILE, tok)
    base = halo * tok // size
    first = start[::size]
    nb = base + jnp.arange(tok // size, dtype=jnp.int32) - first // size + 1
    start = start[None, :]

    q = jnp.dot(n1[halo * tok :], w_attn[:, :width], preferred_element_type=F32).astype(BF16)
    kv = jnp.dot(n1, w_attn[:, width : 3 * width], preferred_element_type=F32).astype(BF16)
    o1, o2, lse, grouped = attend(q, kv, start, nb, lam, gain_col)

    exchange = [VMEM((tok, cols), F32), VMEM((n - 1, tok, cols), BF16), VMEM((n - 1, tok, cols), BF16)]
    h1, n2, scale_two = talk(
        functools.partial(middle_kernel, n, nc, 3 * width),
        1,
        [((tok, cols), F32), ((tok, full), BF16), ((tok, 1), F32)],
        exchange
        + [VMEM((full, width), BF16), VMEM((n, tok, cols), BF16), pltpu.SemaphoreType.DMA]
        + [dma(n - 1, nc)] * 4,
        2 * tok * full * width,
        14,
        (grouped, w_attn, x, gain_two),
        far=(1,),
    )
    tile = min(2 * TILE, hidden)
    inner, d_gate, d_up, d_wffn = ffn(n2, dyr, w_ffn, tile)
    g_ffn = lax.psum_scatter(d_wffn, ("seq", "dp"), scatter_dimension=0, tiled=True)

    stat = VMEM((n, nc, 8, tok // nc), F32)
    early = halo > 2
    dh1, dh1r, gain_two_part, *output = talk(
        functools.partial(back_kernel, n, nc, 0, 2 * hidden if early else None),
        2,
        [((tok, cols), F32), ((tok, full), BF16), ((1, cols), F32)]
        + [((tok, cols), BF16)] * early,
        (exchange + [VMEM((full, hidden), BF16), pltpu.SemaphoreType.DMA] + [dma(n - 1, nc)] * 2)
        * early
        + exchange
        + [
            VMEM((full, 2 * hidden), BF16),
            stat,
            VMEM((n, tok, cols), BF16),
            pltpu.SemaphoreType.DMA,
        ]
        + [dma(n - 1, nc)] * 6,
        4 * tok * full * hidden,
        26,
        (d_gate, d_up, inner, w_ffn, h1, scale_two, gain_two_cols, dy),
        far=(3,),
        kept=(0, 1, 2),
    )
    dg = jnp.dot(dh1r, w_attn[:, 3 * width :], preferred_element_type=F32)
    dq, dk, dv, group_part, lam_part = attend_back(
        q, kv, start, nb, lam, gain_col, o1, o2, lse, dg
    )
    group_words = jnp.concatenate(
        [
            group_part.T,
            jnp.broadcast_to(jnp.sum(lam_part), (1, VDIM)),
            jnp.zeros((6, VDIM), F32),
        ]
    )
    others = n_seq * n_dp - 1
    span = (halo + 1) * tok
    if halo <= 2:
        rows = w_query.shape[0]
        line = (n_seq, rows, 4 * width)
        acts, sums, g_attn = talk(
            functools.partial(finish_kernel, n, n_seq, n_dp, halo, nc, 2 * hidden),
            3,
            [((2, tok, cols), BF16), ((8, cols), F32), ((rows, 4 * width), F32)],
            [
                VMEM((span, cols), F32),
                VMEM((n - 1, span, cols), BF16),
                VMEM((n - 1, span, cols), BF16),
            ]
            + exchange
            + [
                VMEM((full, span), BF16),
                VMEM((full, 3 * width), BF16),
                VMEM((full, hidden), BF16),
                VMEM((full, tok), BF16),
                VMEM(line, F32),
                VMEM((max(n_dp - 1, 1),) + line, BF16),
                VMEM((max(n_dp - 1, 1),) + line, BF16),
                VMEM(line, BF16),
                VMEM((n_seq + 1, rows, 4 * width), BF16),
                stat,
                VMEM((1, cols), F32),
                VMEM((n, 8, VDIM), F32),
                VMEM((others + 1, 8, cols), F32),
                VMEM((max(halo, 1), tok, cols), BF16),
                VMEM((max(halo, 1), tok, cols), BF16),
                VMEM((tok, cols), F32),
                dma(3),
            ]
            + [dma(n - 1, (halo + 1) * nc)] * 2
            + [dma(n - 1, nc)] * 2
            + [dma(n - 1)] * 2
            + [dma(max(others, 1))] * 2
            + [dma(max(halo, 1), nc)] * 2
            + [dma(n - 1, nc)] * 2
            + [dma(max(n_dp - 1, 1), n_seq)] * 2
            + [dma(n_seq, 2)] * 3,
            6 * tok * full * width * (halo + 1),
            58,
            (n1t, w_attn, w_ffn, dq, dk, dv, dh1r, grouped, inner, h1, x, scale_one, gain_one_cols, dh1, gain_two_part, group_words),
            far=(0, 1, 2),
            kept=(3, 4, 5, 8),
        )
        input_grad, output = acts[0], acts[1]
    else:
        d_wattn = projection_grads(halo, n1t, dq, dk, dv, dh1r, grouped)
        d_wattn, g_ffn = lax.optimization_barrier((d_wattn, g_ffn))
        g_attn = lax.psum_scatter(d_wattn, ("seq", "dp"), scatter_dimension=0, tiled=True).astype(F32)
        input_grad, sums = talk(
            functools.partial(leave_kernel, n, n_seq, n_dp, halo, nc),
            3,
            [((tok, cols), BF16), ((8, cols), F32)],
            [
                VMEM((span, cols), F32),
                VMEM((n - 1, span, cols), BF16),
                VMEM((n - 1, span, cols), BF16),
                VMEM((full, 3 * width), BF16),
                stat,
                VMEM((1, cols), F32),
                VMEM((n, 8, VDIM), F32),
                VMEM((others + 1, 8, cols), F32),
                VMEM((max(halo, 1), tok, cols), BF16),
                VMEM((max(halo, 1), tok, cols), BF16),
                VMEM((tok, cols), F32),
                pltpu.SemaphoreType.DMA,
            ]
            + [dma(n - 1, (halo + 1) * nc)] * 2
            + [dma(n - 1, nc)] * 2
            + [dma(n - 1)] * 2
            + [dma(max(others, 1))] * 2
            + [dma(max(halo, 1), nc)] * 2,
            6 * tok * full * width * (halo + 1),
            26 + 5 * halo,
            (dq, dk, dv, w_attn, x, scale_one, gain_one_cols, dh1, gain_two_part, group_words),
            far=(3,),
        )
        (output,) = output
    g_query, g_key, g_value, g_output = (
        g_attn[:, i * width : (i + 1) * width] for i in range(4)
    )
    g_ffn = g_ffn.astype(F32)
    share = cols // (n_seq * n_dp)
    place = lax.axis_index("seq") * n_dp + lax.axis_index("dp")
    gains = lax.dynamic_slice_in_dim(sums[:2], place * share, share, 1)
    return (
        output[None],
        input_grad[None],
        gains[0],
        gains[1],
        sums[2, :VDIM],
        sums[3, :1],
        g_query,
        g_key,
        g_value,
        g_output,
        g_ffn[:, :hidden],
        g_ffn[:, hidden : 2 * hidden],
        g_ffn[:, 2 * hidden :],
    )


def solution(mesh):
    act = P("dp", "seq", "head")
    mat = P(("seq", "dp"), "head")
    vec = P(("head", "seq", "dp"))
    return jax.shard_map(
        functools.partial(on_device, mesh.shape["head"], mesh.shape["seq"], mesh.shape["dp"]),
        mesh=mesh,
        in_specs=(act,) + (mat,) * 7 + (P(),) * 7 + (P("dp", "seq"),) * 2 + (act,),
        out_specs=(act, act, vec, vec, P(), P()) + (mat,) * 7,
        check_vma=False,
    )
```
